512 devices in a mesh: grid: 64 (over z, y), scen: 8 (over x, core).
Axes of the slice: x: 4, y: 4, z: 16, core: 2. Of those that a mesh axis runs over, the one named last changes fastest.
Arguments:
- volt_init: float32 [2, 16384, 1024], P(None, 'grid', 'scen'), may hold values from 0.9 to 1.1
- line_dual: float32 [4, 16384, 1024], P(None, 'grid', 'scen'), may hold values from -1 to 1
- conductance: float32 [16384], P('grid'), may hold values from 0.2 to 2
- susceptance: float32 [16384], P('grid'), may hold values from -6 to -1
- endpoint_owner: int32 [32768, 1], P('grid'), may hold values from 0 to 63; in each aligned block of 512 rows (0 to 511, 512 to 1023, ...) at most 16 rows name the same one
- endpoint_bus: int32 [32768], P('grid'), may hold values from 0 to 255
- line_count: int32 [64], P('grid'), may hold values from 0 to 256, as said below
- bus_region: int32 [16384], P('grid'), may hold values from 0 to 15
- vm_set: float32 [16384], P('grid'), may hold values from 0.85 to 1.15
- stiffness: float32 [16384], P('grid'), may hold values from 0.2 to 2
- load: float32 [16384, 1024], P('grid', 'scen'), may hold values from -6 to 6
- price_init: float32 [16384, 1024], P('grid', 'scen'), may hold values from -3 to 3
- na_dual_init: float32 [16384, 1024], P('grid', 'scen'), may hold values from -2 to 2
- commit_init: float32 [16384], P('grid'), may hold values from 0 to 2
- cost_quad: float32 [16384], P('grid'), may hold values from 0.1 to 1
- cost_lin: float32 [16384], P('grid'), may hold values from -1 to 1
- pmax: float32 [16384], P('grid'), may hold values from 0.5 to 4
Outputs:
- volt: float32 [2, 16384, 1024], P(None, 'grid', 'scen')
- dual: float32 [4, 16384, 1024], P(None, 'grid', 'scen')
- dispatch: float32 [16384, 1024], P('grid', 'scen')
- price: float32 [16384, 1024], P('grid', 'scen')
- commit: float32 [16384], P('grid')
The draws below stay inside these ranges and needn't reach their ends.
Inputs may be any that keep to these rules, and one draw needn't show every extreme that they name: `endpoint_owner`: in each aligned block of 512 rows (one device's line ends) no owner is named more than 16 times, a bound that some block reaches. `line_count`: device i and device i + 32 have 256 live lines or fewer together; some device has exactly 256; a device's live lines are its first slots.
All inputs are finite; a program needn't handle non-finite values.
Results may differ from the reference program's by a relative error of at most 0.0003.
Values sent between devices are 32-bit elements; how exact they have to be, the bound alone decides.
No kernel may reach another device: no remote copies, remote signals or barrier semaphores. Data moves between devices by JAX's collectives and lax.ppermute only.
A program may use at most 64 MiB of HBM per device.

```python
import math
from functools import partial
import jax
import jax.numpy as jnp
import numpy as np
from jax import lax

LCAP = 256
BUS_DEV = 256
SCEN_DEV = 128
NEWTON = 3
ITERS = 2
REGIONS = 16
LINES = 16384
BUSES = 16384
SCEN = 1024
CAP = 16
N_GRID = 64


def draw_line_count(key, part):
    half = N_GRID // 2
    keys = jax.random.split(jax.random.fold_in(key, 7), 4)
    heavy = jax.random.randint(keys[0], (half,), LCAP // 2, LCAP + 1)
    chosen = jax.random.randint(keys[1], (), 0, half)
    heavy = jnp.where(jnp.arange(half) == chosen, LCAP, heavy)
    light = jax.random.randint(keys[2], (half,), 0, LCAP - heavy + 1)
    flip = jax.random.randint(keys[3], (half,), 0, 2)
    lower_half = jnp.where(flip == 1, heavy, light)
    upper_half = jnp.where(flip == 1, light, heavy)
    return jnp.concatenate([lower_half, upper_half]).astype(jnp.int32)


def with_ends(drawn, rng, low, largest):
    extent = drawn.shape
    index_at = [jax.random.randint(jax.random.fold_in(rng, axis), (), 0, extent[axis]) for axis in range(len(extent))]
    drawn = drawn.at[tuple(index_at)].set(low)
    longest = extent.index(max(extent))
    index_at[longest] = (index_at[longest] + 1) % extent[longest]
    return drawn.at[tuple(index_at)].set(largest)


def block_levels(own_key, shape, cuts, least, top_value):
    gain = 1.0
    for position, blocks in cuts:
        heights = jax.random.uniform(jax.random.fold_in(jax.random.fold_in(own_key, 6), position), (blocks,), jnp.float32, least / len(cuts), top_value / len(cuts))
        gain = gain * jnp.repeat(jnp.exp(heights), shape[position] // blocks).reshape((-1,) + (1,) * (len(shape) - 1 - position))
    return gain


def assign_block(key, own, number, rows, number_of, top, bound, skew):
    order = jax.random.permutation(key, number_of)
    heavy_load, common = portions_of(number_of, rows * top, bound, skew, True), portions_of(number_of, rows * top, bound, skew, False)
    places = jnp.arange(number_of)

    def named(sizes, turn):
        used = int((sizes > 0).sum())
        fixed = max(1, used // 4)
        moved = fixed + (places - fixed + turn * (used - fixed)) % max(1, number_of - fixed)
        return jnp.zeros((number_of,), jnp.int32).at[order[jnp.where(places < fixed, places, moved)]].set(jnp.asarray(sizes, jnp.int32))

    sizes = jnp.where(number % 4 == 0, named(heavy_load, number // 4), named(common, number - number // 4 - 1))
    mixed = jax.random.permutation(jax.random.fold_in(own, 3), number_of)
    donor, sink = mixed[0:number_of // 2 * 2:2], mixed[1:number_of // 2 * 2:2]
    margin = jnp.minimum(sizes[donor] - 1, bound - sizes[sink]) // 2
    margin = jnp.where((donor == order[0]) | (sink == order[0]) | (sizes[sink] == 0), 0, jnp.maximum(margin, 0))
    moved = jax.random.randint(jax.random.fold_in(own, 4), (number_of // 2,), 0, 1 << 20) % (margin + 1)
    sizes = sizes.at[donor].add(-moved).at[sink].add(moved)
    labels = jnp.searchsorted(jnp.cumsum(sizes), jnp.arange(rows * top), side="right").astype(jnp.int32)
    listing = labels.reshape(top, rows).T
    listing = listing[jax.random.permutation(jax.random.fold_in(own, 1), rows)]
    turn = jax.random.randint(jax.random.fold_in(own, 2), (rows, 1), 0, top)
    return jnp.take_along_axis(listing, (jnp.arange(top)[None, :] + turn) % top, axis=1)


def portions_of(amount, total, reach, slope, full):
    loads = [(1 << 20) // math.isqrt(rank ** slope) + 1 for rank in range(1, amount + 1)]
    largest = reach if full else min(reach, max(-(-total // amount), total * loads[0] // sum(loads)))
    least = 1 if total - largest >= amount - 1 else 0
    holding, surplus = [largest] + [least] * (amount - 1), total - largest - least * (amount - 1)
    while surplus > 0:
        free = [i for i in range(1, amount) if holding[i] < largest] or [i for i in range(1, amount) if holding[i] < reach]
        pool, budget = sum([loads[i] for i in free]), surplus
        for i in free:
            more = min(reach - holding[i], max(1, budget * loads[i] // pool), surplus)
            holding[i] = holding[i] + more
            surplus = surplus - more
    return np.array(holding)


def centred(stream_key, extent, spread, reach, cuts=(), kind=jnp.bfloat16):
    values = spread * jax.random.normal(stream_key, extent, jnp.float32)
    if cuts:
        values = values * block_levels(stream_key, extent, cuts, -0.22, 0.18)
    return jnp.clip(values, -reach, reach).astype(kind)


def setup_inputs(seed: int = 0) -> dict:
    streams_of = jax.random.split(jax.random.key(seed), 18)
    volt_init = jnp.clip(0.9 + 0.20000005 * jax.random.uniform(streams_of[0], (2, BUSES, SCEN), jnp.float32) ** block_levels(streams_of[0], (2, BUSES, SCEN), ((1, 64), (2, 8)), -0.2, 0.2), 0.9, 1.1)
    line_dual = centred(streams_of[1], (4, LINES, SCEN), 0.2, 1.0, ((1, 64), (2, 8)), jnp.float32)
    conductance = jnp.clip(jnp.exp(math.log(2.0) - 2.3025851 * jax.random.uniform(streams_of[2], (LINES,), jnp.float32) ** block_levels(streams_of[2], (LINES,), ((0, 64),), -0.2, 0.2)), 0.2, 2.0)
    susceptance = jnp.clip(-6.0 + 5.0 * jax.random.uniform(streams_of[3], (LINES,), jnp.float32) ** block_levels(streams_of[3], (LINES,), ((0, 64),), -0.2, 0.2), -6.0, -1.0)
    endpoint_owner_keys = jax.random.split(jax.random.fold_in(streams_of[4], 1), (2 * LINES) // (2 * LCAP))
    endpoint_owner_turns = jax.random.permutation(jax.random.fold_in(streams_of[4], 3), (2 * LINES) // (2 * LCAP))
    endpoint_owner = jax.vmap(lambda own, number: assign_block(jax.random.fold_in(streams_of[4], 2), own, number, 2 * LCAP, N_GRID, 1, CAP, 2))(endpoint_owner_keys, endpoint_owner_turns).reshape((2 * LINES, 1))
    endpoint_bus = with_ends(jax.random.randint(streams_of[5], (2 * LINES,), 0, BUS_DEV), jax.random.fold_in(streams_of[5], 1), 0, BUS_DEV - 1).astype(jnp.int32)
    line_count = draw_line_count(jax.random.fold_in(streams_of[17], 71), 0)
    bus_region = with_ends(jax.random.randint(streams_of[7], (BUSES,), 0, REGIONS), jax.random.fold_in(streams_of[7], 1), 0, REGIONS - 1).astype(jnp.int32)
    vm_set = jnp.clip(1.0 + 0.03 * jax.random.normal(streams_of[8], (BUSES,), jnp.float32), 0.85, 1.15)
    stiffness = jnp.clip(jnp.exp(math.log(2.0) - 2.3025851 * jax.random.uniform(streams_of[9], (BUSES,), jnp.float32) ** block_levels(streams_of[9], (BUSES,), ((0, 64),), -0.2, 0.2)), 0.2, 2.0)
    load = centred(streams_of[10], (BUSES, SCEN), 1.0, 6.0, ((0, 64), (1, 8)), jnp.float32)
    price_init = centred(streams_of[11], (BUSES, SCEN), 0.5, 3.0, ((0, 64), (1, 8)), jnp.float32)
    na_dual_init = centred(streams_of[12], (BUSES, SCEN), 0.3, 2.0, ((0, 64), (1, 8)), jnp.float32)
    commit_init = jnp.clip(2.0 * jax.random.uniform(streams_of[13], (BUSES,), jnp.float32) ** block_levels(streams_of[13], (BUSES,), ((0, 64),), -0.2, 0.2), 0.0, 2.0)
    cost_quad = jnp.clip(jnp.exp(math.log(1.0) - 2.3025851 * jax.random.uniform(streams_of[14], (BUSES,), jnp.float32) ** block_levels(streams_of[14], (BUSES,), ((0, 64),), -0.2, 0.2)), 0.1, 1.0)
    cost_lin = jnp.clip(jax.random.uniform(streams_of[15], (BUSES,), jnp.float32, -1.0, 1.0) * block_levels(streams_of[15], (BUSES,), ((0, 64),), -0.4, 0.0), -1.0, 1.0)
    pmax = jnp.clip(jnp.exp(math.log(4.0) - 2.0794415 * jax.random.uniform(streams_of[16], (BUSES,), jnp.float32) ** block_levels(streams_of[16], (BUSES,), ((0, 64),), -0.2, 0.2)), 0.5, 4.0)
    return {"volt_init": volt_init, "line_dual": line_dual, "conductance": conductance, "susceptance": susceptance, "endpoint_owner": endpoint_owner, "endpoint_bus": endpoint_bus, "line_count": line_count, "bus_region": bus_region, "vm_set": vm_set, "stiffness": stiffness, "load": load, "price_init": price_init, "na_dual_init": na_dual_init, "commit_init": commit_init, "cost_quad": cost_quad, "cost_lin": cost_lin, "pmax": pmax}


penalty_line = 1.0
region_gain = 10.0

def cholesky_solve(hess, grad):
    lower = {}
    for row in range(4):
        for column in range(row + 1):
            total = hess[row][column]
            for inner in range(column):
                total = total - lower[row, inner] * lower[column, inner]
            if row == column:
                lower[row, row] = jnp.sqrt(total)
            else:
                lower[row, column] = total / lower[column, column]
    forward = []
    for row in range(4):
        total = grad[row]
        for inner in range(row):
            total = total - lower[row, inner] * forward[inner]
        forward.append(total / lower[row, row])
    answer = [None] * 4
    for row in range(3, -1, -1):
        total = forward[row]
        for inner in range(row + 1, 4):
            total = total - lower[inner, row] * answer[inner]
        answer[row] = total / lower[row, row]
    return answer

def branch_newton(center, cond, susc):
    state = list(center)
    for sweep in range(NEWTON):
        from_mag, from_ang, to_mag, to_ang = state
        cos_f = jnp.cos(from_ang)
        sin_f = jnp.sin(from_ang)
        cos_t = jnp.cos(to_ang)
        sin_t = jnp.sin(to_ang)
        real_gap = from_mag * cos_f - to_mag * cos_t
        imag_gap = from_mag * sin_f - to_mag * sin_t
        first = [cos_f, -from_mag * sin_f, -cos_t, to_mag * sin_t]
        second = [sin_f, from_mag * cos_f, -sin_t, -to_mag * cos_t]
        twice = 2.0 * cond
        grad = [twice * (first[row] * real_gap + second[row] * imag_gap) + penalty_line * (state[row] - center[row]) for row in range(4)]
        hess = [[twice * (first[row] * first[column] + second[row] * second[column]) + (penalty_line if row == column else 0.0) for column in range(4)] for row in range(4)]
        update = cholesky_solve(hess, grad)
        state = [state[row] - update[row] for row in range(4)]
    from_mag, from_ang, to_mag, to_ang = state
    angle_gap = from_ang - to_ang
    product = from_mag * to_mag
    cos_d = jnp.cos(angle_gap)
    sin_d = jnp.sin(angle_gap)
    flow_from = cond * from_mag * from_mag - product * (cond * cos_d + susc * sin_d)
    flow_to = cond * to_mag * to_mag - product * (cond * cos_d - susc * sin_d)
    return (state, flow_from, flow_to)

def reference(volt_init, line_dual, conductance, susceptance, endpoint_owner, endpoint_bus, line_count, bus_region, vm_set, stiffness, load, price_init, na_dual_init, commit_init, cost_quad, cost_lin, pmax):
    ends = (endpoint_owner[:, 0] * BUS_DEV + endpoint_bus).reshape(N_GRID, 2, LCAP)
    from_id = ends[:, 0, :].reshape(LINES).astype(jnp.int32)
    to_id = ends[:, 1, :].reshape(LINES).astype(jnp.int32)
    live = (jnp.arange(LCAP)[None, :] < line_count[:, None]).astype(jnp.float32).reshape(LINES)
    degree = jnp.zeros((BUSES,), jnp.float32).at[from_id].add(live).at[to_id].add(live)
    blocks = SCEN // SCEN_DEV
    cond = conductance[:, None]
    susc = susceptance[:, None]
    live_col = live[:, None]

    def split(arr):
        return jnp.moveaxis(arr.reshape(arr.shape[:-1] + (blocks, SCEN_DEV)), -2, 0)

    def join(arr):
        return jnp.moveaxis(arr, 0, -2).reshape(arr.shape[1:-1] + (SCEN,))

    def line_block(inputs, first_turn):
        volt_blk, dual_blk, prev_blk = inputs
        near = jnp.stack([volt_blk[0][from_id], volt_blk[1][from_id], volt_blk[0][to_id], volt_blk[1][to_id]])
        if not first_turn:
            dual_blk = jnp.where(live_col[None] > 0, dual_blk + prev_blk - near, dual_blk)
        center = near - dual_blk
        state, flow_from, flow_to = branch_newton([center[row] for row in range(4)], cond, susc)
        solved = jnp.stack(state)
        from_terms = jnp.stack([live_col * (solved[0] + dual_blk[0]), live_col * (solved[1] + dual_blk[1]), live_col * flow_from])
        to_terms = jnp.stack([live_col * (solved[2] + dual_blk[2]), live_col * (solved[3] + dual_blk[3]), live_col * flow_to])
        summed = jnp.zeros((3, BUSES, SCEN_DEV), jnp.float32).at[:, from_id, :].add(from_terms).at[:, to_id, :].add(to_terms)
        return (dual_blk, solved, summed)
    volt = volt_init
    dual = line_dual
    previous = jnp.zeros_like(line_dual)
    price = price_init
    nadual = na_dual_init
    commit = commit_init
    member = (bus_region[:, None] == jnp.arange(REGIONS, dtype=jnp.int32)[None, :]).astype(jnp.float32)
    dispatch = jnp.zeros_like(load)
    for turn in range(ITERS):
        outputs = lax.map(partial(line_block, first_turn=turn == 0), (split(volt), split(dual), split(previous)))
        dual = join(outputs[0])
        previous = join(outputs[1])
        summed = join(outputs[2])
        weight = stiffness[:, None]
        target = jnp.stack([jnp.broadcast_to(vm_set[:, None], (BUSES, SCEN)), volt[1]])
        volt = (penalty_line * summed[0:2] + weight * target) / (penalty_line * degree[:, None] + weight)
        net = summed[2]
        dispatch = (load + net - price - cost_lin[:, None] + (commit[:, None] - nadual)) / (2.0 * cost_quad[:, None] + 2.0)
        dispatch = jnp.clip(dispatch, 0.0, pmax[:, None])
        mismatch = dispatch - load - net
        regional = jnp.einsum('br,bs->rs', member, mismatch, precision=lax.Precision.HIGHEST)
        adder = jnp.dot(member, regional, precision=lax.Precision.HIGHEST) * (region_gain * REGIONS / BUSES)
        commit = lax.optimization_barrier(jnp.sum(dispatch + nadual, axis=1)) / SCEN
        nadual = nadual + dispatch - commit[:, None]
        price = price + mismatch + adder
    return (volt, dual, dispatch, price, commit)
```

```python
import functools

import jax
import jax.numpy as jnp
from jax import lax
from jax.experimental import pallas as pl
from jax.experimental.pallas import tpu as pltpu
from jax.sharding import PartitionSpec as P

NEWTON = 3
REGIONS = 16
CAP = 16
LANES = 128
REGION_GAIN = 10.0
BLOCK = 32

F32 = jnp.float32
BF16 = jnp.bfloat16
SMEM = pltpu.SMEM
VMEM = pltpu.VMEM


def smem():
    return pl.BlockSpec(memory_space=SMEM)


def vmem():
    return pl.BlockSpec(memory_space=VMEM)


def pieces(x, count):
    parts = []
    for _ in range(count - 1):
        head = x.astype(BF16)
        parts.append(head)
        x = x - head.astype(F32)
    parts.append(x.astype(BF16))
    return parts


def picked(selector, x, count):
    total = None
    for part in pieces(x, count):
        term = jnp.dot(selector, part, preferred_element_type=F32)
        total = term if total is None else total + term
    return total


def dot_lanes(a, b):
    return lax.dot_general(a, b, (((1,), (1,)), ((), ())), preferred_element_type=F32)


def plan_kernel(count_ref, owner_ref, bus_ref, slot_ref, request_ref):
    ends = owner_ref.shape[1]
    owners = request_ref.shape[0]
    owner = owner_ref[...]
    end_id = lax.broadcasted_iota(jnp.int32, (1, ends), 1)
    live = lax.rem(end_id, ends // 2) < count_ref[0]
    code = jnp.where(live, bus_ref[...] + 1, 0).astype(F32)
    hits = lax.broadcasted_iota(jnp.int32, (owners, ends), 0) == owner
    hits = hits.astype(F32)
    before = lax.broadcasted_iota(jnp.int32, (ends, ends), 0) < lax.broadcasted_iota(
        jnp.int32, (ends, ends), 1
    )
    earlier = jnp.dot(hits.astype(BF16), before.astype(BF16), preferred_element_type=F32)
    rank = jnp.sum(hits * earlier, axis=0, keepdims=True).astype(jnp.int32)
    slot_ref[...] = owner * CAP + rank
    ranks = lax.broadcasted_iota(jnp.int32, (LANES, ends), 0) == rank
    table = dot_lanes((hits * code).astype(BF16), ranks.astype(BF16))
    request_ref[...] = table.astype(jnp.int32)


def send_rows(asked_ref, volt_ref, out_ref):
    def step(o, carry):
        for r in range(CAP):
            bus = jnp.maximum(asked_ref[o, r] - 1, 0)
            for c in range(2):
                out_ref[o, c * CAP + r : c * CAP + r + 1, :] = volt_ref[c, pl.ds(bus, 1), :]
        return carry

    lax.fori_loop(0, out_ref.shape[0], step, 0)


def first_send_kernel(asked_ref, volt_ref, out_ref):
    send_rows(asked_ref, volt_ref, out_ref)


def sin_cos(x):
    turns = jnp.floor(x * 0.636619772367581343 + 0.5)
    r = x - turns * 1.5703125
    r = r - turns * 4.83751296997070312e-04
    r = r - turns * 7.54978995489188216e-08
    n = turns.astype(jnp.int32)
    z = r * r
    s = ((-1.9515295891e-4 * z + 8.3321608736e-3) * z - 1.6666654611e-1) * z * r + r
    c = ((2.443315711809948e-5 * z - 1.388731625493765e-3) * z + 4.166664568298827e-2) * z * z
    c = c - 0.5 * z + 1.0
    odd = (n & 1) == 1
    sine = jnp.where(odd, c, s)
    cosine = jnp.where(odd, s, c)
    sine = jnp.where((n & 2) == 2, -sine, sine)
    cosine = jnp.where(((n + 1) & 2) == 2, -cosine, cosine)
    return sine, cosine


def branch_newton(center, cond, susc):
    k = 2.0 * cond
    vf, af, vt, at = center
    for step in range(NEWTON):
        s, c = sin_cos(af - at)
        w0 = vf - vt * c
        w1 = vt * s
        if step > 0:
            r0, r1, r2, r3 = vf - center[0], af - center[1], vt - center[2], at - center[3]
            r3 = vt * r3
            w0 = w0 - r0 + r2 * c + r3 * s
            w1 = w1 - r1 * vf - r2 * s + r3 * c
        ss, cc, tt = s * s, c * c, vt * vt
        m00 = 1.0 + k * (1.0 + cc + tt * ss)
        m11 = 1.0 + k * (vf * vf + ss + tt * cc)
        m01 = k * (s * c * (tt - 1.0))
        scale = k / (m00 * m11 - m01 * m01)
        z0 = (m11 * w0 - m01 * w1) * scale
        z1 = (m00 * w1 - m01 * w0) * scale
        new = (
            center[0] - z0,
            center[1] - vf * z1,
            center[2] + (c * z0 - s * z1),
            center[3] + vt * (s * z0 + c * z1),
        )
        vf, af, vt, at = new
    s, c = sin_cos(af - at)
    product = vf * vt
    flow_from = cond * vf * vf - product * (cond * c + susc * s)
    flow_to = cond * vt * vt - product * (cond * c - susc * s)
    return (vf, af, vt, at), flow_from, flow_to


def line_kernel(second, count_ref, slot_ref, arrived_ref, dual_ref, *refs):
    if second:
        previous_ref, param_ref, out_ref, dual_out_ref, near_ref, term_ref = refs
    else:
        param_ref, out_ref, state_ref, near_ref, term_ref = refs
    lines = dual_ref.shape[1]

    def step(block, carry):
        base = pl.multiple_of(block * BLOCK, BLOCK)
        rows = pl.ds(base, BLOCK)
        starts = []
        for end in range(2):
            for j in range(BLOCK):
                slot = slot_ref[end * lines + base + j]
                high = slot & -CAP
                starts.append((slot + high, slot + high + high))
        for end in range(2):
            for j in range(BLOCK):
                start = starts[end * BLOCK + j][0]
                for c in range(2):
                    near_ref[2 * end + c, j : j + 1, :] = arrived_ref[pl.ds(start + c * CAP, 1), :]
        near = [near_ref[i] for i in range(4)]
        dual = [dual_ref[i, rows, :] for i in range(4)]
        line_id = lax.broadcasted_iota(jnp.int32, (BLOCK, LANES), 0) + base
        live = line_id < count_ref[0]
        if second:
            dual = [
                jnp.where(live, dual[i] + previous_ref[i, rows, :] - near[i], dual[i])
                for i in range(4)
            ]
            for i in range(4):
                dual_out_ref[i, rows, :] = dual[i]
        center = [near[i] - dual[i] for i in range(4)]
        param = param_ref[rows, :]
        cond = jnp.broadcast_to(param[:, 0:1], (BLOCK, LANES))
        susc = jnp.broadcast_to(param[:, 1:2], (BLOCK, LANES))
        state, flow_from, flow_to = branch_newton(center, cond, susc)
        if not second:
            for i in range(4):
                state_ref[i, rows, :] = state[i]
        terms = [
            state[0] + dual[0], state[1] + dual[1], flow_from,
            state[2] + dual[2], state[3] + dual[3], flow_to,
        ]
        for i in range(6):
            term_ref[i] = jnp.where(live, terms[i], 0.0)
        for end in range(2):
            for j in range(BLOCK):
                start = starts[end * BLOCK + j][1]
                for c in range(3):
                    out_ref[pl.ds(start + c * CAP, 1), :] = term_ref[3 * end + c, j : j + 1, :]
        return carry

    out_ref[...] = jnp.zeros_like(out_ref)
    lax.fori_loop(0, lines // BLOCK, step, 0)


def column(param, index):
    return jnp.broadcast_to(param[:, index : index + 1], (param.shape[0], LANES))


def region_term(param, regional, buses_all):
    width = regional.shape[0]
    share = width // REGIONS
    ids = lax.broadcasted_iota(jnp.int32, (param.shape[0], width), 1)
    member = ids == param[:, 6:7].astype(jnp.int32) * share
    total = picked(member.astype(BF16), regional, 3)
    return total * (REGION_GAIN * REGIONS / buses_all)


def owner_kernel(second, buses_all, scen_all, asked_ref, row_ref, recv_ref, volt_ref, param_ref,
                 region_ref, load_ref, price_ref, nadual_ref, *refs):
    if second:
        (disp1_ref, mism1_ref, regional_ref, totals_ref,
         volt_out, disp_out, part_out, total_out, price_out) = refs
    else:
        volt_out, disp_out, mism_out, part_out, total_out, send_out = refs
    buses = volt_ref.shape[1]
    devices = recv_ref.shape[0]
    slots = devices * CAP
    ids = lax.broadcasted_iota(jnp.int32, (buses, slots), 0) + 1
    hits = (ids == row_ref[...]).astype(BF16)
    rows = [recv_ref[:, c * CAP : (c + 1) * CAP, :].reshape(slots, LANES) for c in range(3)]
    pair = picked(hits, jnp.concatenate(rows[:2], axis=1), 2)
    flows = pieces(rows[2], 2)
    ones = jnp.ones((slots, LANES), BF16)
    last = jnp.dot(hits, jnp.concatenate([flows[0], ones], axis=1), preferred_element_type=F32)
    net = last[:, :LANES] + jnp.dot(hits, flows[1], preferred_element_type=F32)
    degree = last[:, LANES:]
    param = param_ref[...]
    weight = column(param, 0)
    inverse = 1.0 / (degree + weight)
    volt_out[0] = (pair[:, :LANES] + weight * column(param, 1)) * inverse
    volt_out[1] = (pair[:, LANES:] + weight * volt_ref[1]) * inverse
    if not second:
        send_rows(asked_ref, volt_out, send_out)
    load, price, nadual = load_ref[...], price_ref[...], nadual_ref[...]
    if second:
        commit = jnp.sum(jnp.transpose(totals_ref[...]), axis=1, keepdims=True) / scen_all
        commit = jnp.broadcast_to(commit, (buses, LANES))
        nadual = nadual + disp1_ref[...] - commit
        price = price + mism1_ref[...] + region_term(param, regional_ref[...], buses_all)
    else:
        commit = column(param, 5)
    want = (load + net - price - column(param, 3) + (commit - nadual)) / (
        2.0 * column(param, 2) + 2.0
    )
    dispatch = jnp.clip(want, 0.0, column(param, 4))
    mismatch = dispatch - load - net
    disp_out[...] = dispatch
    if second:
        price_out[...] = price + mismatch
    else:
        mism_out[...] = mismatch
    width = part_out.shape[0]
    share = width // REGIONS
    region = lax.broadcasted_iota(jnp.int32, (width, buses), 0) // share == region_ref[...]
    part_out[...] = picked(region.astype(BF16), mismatch, 3)
    total = None
    ones = jnp.ones((total_out.shape[0], LANES), BF16)
    for piece in pieces(dispatch + nadual, 3):
        term = dot_lanes(ones, piece)
        total = term if total is None else total + term
    total_out[...] = total


def close_kernel(buses_all, param_ref, regional_ref, price_ref, out_ref):
    out_ref[...] = price_ref[...] + region_term(param_ref[...], regional_ref[...], buses_all)


def on_device(
    volt_init,
    line_dual,
    conductance,
    susceptance,
    endpoint_owner,
    endpoint_bus,
    line_count,
    bus_region,
    vm_set,
    stiffness,
    load,
    price_init,
    na_dual_init,
    commit_init,
    cost_quad,
    cost_lin,
    pmax,
):
    ngrid = lax.axis_size("grid")
    nscen = lax.axis_size("scen")
    lines = conductance.shape[0]
    ends = 2 * lines
    buses = vm_set.shape[0]
    scen = load.shape[1]
    buses_all = buses * ngrid
    shape = jax.ShapeDtypeStruct

    def exchange(x):
        return lax.all_to_all(x, "grid", split_axis=0, concat_axis=0, tiled=True)

    slot, request = pl.pallas_call(
        plan_kernel,
        out_shape=(shape((1, ends), jnp.int32), shape((ngrid, LANES), jnp.int32)),
        in_specs=[smem(), vmem(), vmem()],
        out_specs=(vmem(), vmem()),
        name="plan",
    )(line_count, endpoint_owner.reshape(1, ends), endpoint_bus.reshape(1, ends))
    slot = slot.reshape(ends)
    asked = exchange(request)
    asked_row = asked[:, :CAP].reshape(1, ngrid * CAP)

    line_param = jnp.stack([conductance, susceptance], axis=1)
    bus_param = jnp.stack(
        [stiffness, vm_set, cost_quad, cost_lin, pmax, commit_init, bus_region.astype(F32),
         jnp.zeros_like(pmax)],
        axis=1,
    )
    region_row = bus_region.reshape(1, buses)
    send_shape = shape((ngrid, 2 * CAP, LANES), F32)
    bus_shape = shape((buses, LANES), F32)

    sent = pl.pallas_call(
        first_send_kernel,
        out_shape=send_shape,
        in_specs=[smem(), vmem()],
        out_specs=vmem(),
        name="first_send",
    )(asked, volt_init)

    def line_call(second, arrived, previous):
        outs = [shape((ngrid * 3 * CAP, LANES), F32), shape((4, lines, LANES), F32)]
        args = [line_count, slot, arrived.reshape(ngrid * 2 * CAP, LANES), line_dual]
        if second:
            args.append(previous)
        args.append(line_param)
        out, other = pl.pallas_call(
            functools.partial(line_kernel, second),
            out_shape=outs,
            in_specs=[smem(), smem()] + [vmem()] * (len(args) - 2),
            out_specs=[vmem(), vmem()],
            scratch_shapes=[VMEM((4, BLOCK, LANES), F32), VMEM((6, BLOCK, LANES), F32)],
            name="lines2" if second else "lines1",
        )(*args)
        return out.reshape(ngrid, 3 * CAP, LANES), other

    def owner_call(second, received, volt, extra):
        outs = [shape((2, buses, LANES), F32), bus_shape]
        if not second:
            outs.append(bus_shape)
        outs += [shape((ngrid, LANES), F32), shape((nscen, buses), F32)]
        outs.append(bus_shape if second else send_shape)
        args = [asked, asked_row, received, volt, bus_param, region_row, load, price_init,
                na_dual_init] + list(extra)
        return pl.pallas_call(
            functools.partial(owner_kernel, second, buses_all, scen * nscen),
            out_shape=outs,
            in_specs=[smem()] + [vmem()] * (len(args) - 1),
            out_specs=[vmem()] * len(outs),
            name="owner2" if second else "owner1",
        )(*args)

    def regional_sum(part):
        own = jnp.sum(exchange(part), axis=0, keepdims=True)
        return exchange(jnp.broadcast_to(own, (ngrid, LANES)))

    def scenario_parts(total):
        return lax.all_to_all(total, "scen", split_axis=0, concat_axis=0, tiled=True)

    out, state = line_call(False, exchange(sent), None)
    volt, disp1, mism1, part, total, sent = owner_call(False, exchange(out), volt_init, ())
    regional = regional_sum(part)
    totals = scenario_parts(total)
    out, dual = line_call(True, exchange(sent), state)
    volt, dispatch, part, total, price = owner_call(
        True, exchange(out), volt, (disp1, mism1, regional, totals)
    )
    regional = regional_sum(part)
    commit = jnp.sum(scenario_parts(total), axis=0) / (scen * nscen)
    price = pl.pallas_call(
        functools.partial(close_kernel, buses_all),
        out_shape=bus_shape,
        in_specs=[vmem()] * 3,
        out_specs=vmem(),
        name="close",
    )(bus_param, regional, price)
    return (volt, dual, dispatch, price, commit)


def solution(mesh):
    in_specs = (
        P(None, "grid", "scen"),
        P(None, "grid", "scen"),
        P("grid"),
        P("grid"),
        P("grid", None),
        P("grid"),
        P("grid"),
        P("grid"),
        P("grid"),
        P("grid"),
        P("grid", "scen"),
        P("grid", "scen"),
        P("grid", "scen"),
        P("grid"),
        P("grid"),
        P("grid"),
        P("grid"),
    )
    out_specs = (
        P(None, "grid", "scen"),
        P(None, "grid", "scen"),
        P("grid", "scen"),
        P("grid", "scen"),
        P("grid"),
    )
    return jax.shard_map(
        on_device, mesh=mesh, in_specs=in_specs, out_specs=out_specs, check_vma=False
    )
```

```python
import functools

import jax
import jax.numpy as jnp
from jax import lax
from jax.experimental import pallas as pl
from jax.experimental.pallas import tpu as pltpu
from jax.sharding import PartitionSpec as P

NEWTON = 3
REGIONS = 16
CAP = 16
LANES = 128
REGION_GAIN = 10.0
BLOCK = 32
NEAR = 4
GRANT = 16 * 2**20

F32 = jnp.float32
BF16 = jnp.bfloat16
SMEM = pltpu.SMEM
VMEM = pltpu.VMEM


def smem():
    return pl.BlockSpec(memory_space=SMEM)


def vmem():
    return pl.BlockSpec(memory_space=VMEM)


def pieces(x, count):
    parts = []
    for _ in range(count - 1):
        head = x.astype(BF16)
        parts.append(head)
        x = x - head.astype(F32)
    parts.append(x.astype(BF16))
    return parts


def picked(selector, x, count):
    total = None
    for part in pieces(x, count):
        term = jnp.dot(selector, part, preferred_element_type=F32)
        total = term if total is None else total + term
    return total


def dot_lanes(a, b):
    return lax.dot_general(a, b, (((1,), (1,)), ((), ())), preferred_element_type=F32)


def plan_kernel(count_ref, owner_ref, bus_ref, slot_ref, request_ref):
    ends = owner_ref.shape[1]
    owners = request_ref.shape[0]
    owner = owner_ref[...]
    end_id = lax.broadcasted_iota(jnp.int32, (1, ends), 1)
    live = lax.rem(end_id, ends // 2) < count_ref[0]
    code = jnp.where(live, bus_ref[...] + 1, 0).astype(F32)
    hits = lax.broadcasted_iota(jnp.int32, (owners, ends), 0) == owner
    hits = hits.astype(F32)
    before = lax.broadcasted_iota(jnp.int32, (ends, ends), 0) < lax.broadcasted_iota(
        jnp.int32, (ends, ends), 1
    )
    earlier = jnp.dot(hits.astype(BF16), before.astype(BF16), preferred_element_type=F32)
    rank = jnp.sum(hits * earlier, axis=0, keepdims=True).astype(jnp.int32)
    slot_ref[...] = owner * CAP + rank
    ranks = lax.broadcasted_iota(jnp.int32, (LANES, ends), 0) == rank
    table = dot_lanes((hits * code).astype(BF16), ranks.astype(BF16))
    request_ref[...] = table.astype(jnp.int32)


def send_rows(asked_ref, volt_ref, out_ref):
    def step(o, carry):
        for r in range(CAP):
            bus = jnp.maximum(asked_ref[o, r] - 1, 0)
            for c in range(2):
                out_ref[o, c * CAP + r : c * CAP + r + 1, :] = volt_ref[c, pl.ds(bus, 1), :]
        return carry

    lax.fori_loop(0, out_ref.shape[0], step, 0)


def first_send_kernel(asked_ref, volt_ref, out_ref):
    send_rows(asked_ref, volt_ref, out_ref)


def sin_cos(x):
    turns = jnp.floor(x * 0.636619772367581343 + 0.5)
    r = x - turns * 1.5703125
    r = r - turns * 4.83751296997070312e-04
    r = r - turns * 7.54978995489188216e-08
    n = turns.astype(jnp.int32)
    z = r * r
    s = ((-1.9515295891e-4 * z + 8.3321608736e-3) * z - 1.6666654611e-1) * z * r + r
    c = ((2.443315711809948e-5 * z - 1.388731625493765e-3) * z + 4.166664568298827e-2) * z * z
    c = c - 0.5 * z + 1.0
    odd = (n & 1) == 1
    sine = jnp.where(odd, c, s)
    cosine = jnp.where(odd, s, c)
    sine = jnp.where((n & 2) == 2, -sine, sine)
    cosine = jnp.where(((n + 1) & 2) == 2, -cosine, cosine)
    return sine, cosine


def branch_newton(center, cond, susc):
    k = 2.0 * cond
    vf, af, vt, at = center
    for step in range(NEWTON):
        s, c = sin_cos(af - at)
        w0 = vf - vt * c
        w1 = vt * s
        if step > 0:
            r0, r1, r2, r3 = vf - center[0], af - center[1], vt - center[2], at - center[3]
            r3 = vt * r3
            w0 = w0 - r0 + r2 * c + r3 * s
            w1 = w1 - r1 * vf - r2 * s + r3 * c
        ss, cc, tt = s * s, c * c, vt * vt
        m00 = 1.0 + k * (1.0 + cc + tt * ss)
        m11 = 1.0 + k * (vf * vf + ss + tt * cc)
        m01 = k * (s * c * (tt - 1.0))
        scale = k / (m00 * m11 - m01 * m01)
        z0 = (m11 * w0 - m01 * w1) * scale
        z1 = (m00 * w1 - m01 * w0) * scale
        new = (
            center[0] - z0,
            center[1] - vf * z1,
            center[2] + (c * z0 - s * z1),
            center[3] + vt * (s * z0 + c * z1),
        )
        vf, af, vt, at = new
    s, c = sin_cos(af - at)
    product = vf * vt
    flow_from = cond * vf * vf - product * (cond * c + susc * s)
    flow_to = cond * vt * vt - product * (cond * c - susc * s)
    return (vf, af, vt, at), flow_from, flow_to


def line_kernel(second, count_ref, slot_ref, arrived_ref, dual_ref, *refs):
    if second:
        previous_ref, param_ref, out_ref, dual_out_ref, near_ref, term_ref = refs
    else:
        param_ref, out_ref, state_ref, near_ref, term_ref = refs
    lines = dual_ref.shape[1]

    def step(block, carry):
        base = pl.multiple_of(block * BLOCK, BLOCK)
        rows = pl.ds(base, BLOCK)
        starts = []
        for end in range(2):
            for j in range(BLOCK):
                slot = slot_ref[end * lines + base + j]
                high = slot & -CAP
                starts.append((slot + high, slot + high + high))
        for end in range(2):
            for j in range(BLOCK):
                start = starts[end * BLOCK + j][0]
                for c in range(2):
                    near_ref[2 * end + c, j : j + 1, :] = arrived_ref[pl.ds(start + c * CAP, 1), :]
        near = [near_ref[i] for i in range(4)]
        dual = [dual_ref[i, rows, :] for i in range(4)]
        line_id = lax.broadcasted_iota(jnp.int32, (BLOCK, LANES), 0) + base
        live = line_id < count_ref[0]
        if second:
            dual = [
                jnp.where(live, dual[i] + previous_ref[i, rows, :] - near[i], dual[i])
                for i in range(4)
            ]
            for i in range(4):
                dual_out_ref[i, rows, :] = dual[i]
        center = [near[i] - dual[i] for i in range(4)]
        param = param_ref[rows, :]
        cond = jnp.broadcast_to(param[:, 0:1], (BLOCK, LANES))
        susc = jnp.broadcast_to(param[:, 1:2], (BLOCK, LANES))
        state, flow_from, flow_to = branch_newton(center, cond, susc)
        if not second:
            for i in range(4):
                state_ref[i, rows, :] = state[i]
        terms = [
            state[0] + dual[0], state[1] + dual[1], flow_from,
            state[2] + dual[2], state[3] + dual[3], flow_to,
        ]
        for i in range(6):
            term_ref[i] = jnp.where(live, terms[i], 0.0)
        for end in range(2):
            for j in range(BLOCK):
                start = starts[end * BLOCK + j][1]
                for c in range(3):
                    out_ref[pl.ds(start + c * CAP, 1), :] = term_ref[3 * end + c, j : j + 1, :]
        return carry

    out_ref[...] = jnp.zeros_like(out_ref)
    lax.fori_loop(0, lines // BLOCK, step, 0)


def column(param, index):
    return jnp.broadcast_to(param[:, index : index + 1], (param.shape[0], LANES))


def region_term(param, regional, buses_all):
    ids = lax.broadcasted_iota(jnp.int32, (param.shape[0], REGIONS), 1)
    member = ids == param[:, 6:7].astype(jnp.int32)
    total = picked(member.astype(BF16), regional, 3)
    return total * (REGION_GAIN * REGIONS / buses_all)


def owner_kernel(second, buses_all, scen_all, asked_ref, row_ref, recv_ref, volt_ref, param_ref,
                 region_ref, load_ref, price_ref, nadual_ref, *refs):
    if second:
        (disp1_ref, mism1_ref, regional_ref, totals_ref,
         volt_out, disp_out, part_out, total_out, price_out) = refs
    else:
        volt_out, disp_out, mism_out, part_out, total_out, send_out = refs
    buses = volt_ref.shape[1]
    devices = recv_ref.shape[0]
    slots = devices * CAP
    ids = lax.broadcasted_iota(jnp.int32, (buses, slots), 0) + 1
    hits = (ids == row_ref[...]).astype(BF16)
    rows = [recv_ref[:, c * CAP : (c + 1) * CAP, :].reshape(slots, LANES) for c in range(3)]
    pair = picked(hits, jnp.concatenate(rows[:2], axis=1), 2)
    flows = pieces(rows[2], 2)
    ones = jnp.ones((slots, LANES), BF16)
    last = jnp.dot(hits, jnp.concatenate([flows[0], ones], axis=1), preferred_element_type=F32)
    net = last[:, :LANES] + jnp.dot(hits, flows[1], preferred_element_type=F32)
    degree = last[:, LANES:]
    param = param_ref[...]
    weight = column(param, 0)
    inverse = 1.0 / (degree + weight)
    volt_out[0] = (pair[:, :LANES] + weight * column(param, 1)) * inverse
    volt_out[1] = (pair[:, LANES:] + weight * volt_ref[1]) * inverse
    if not second:
        send_rows(asked_ref, volt_out, send_out)
    load, price, nadual = load_ref[...], price_ref[...], nadual_ref[...]
    if second:
        commit = jnp.transpose(totals_ref[...])[:, 0:1] / scen_all
        commit = jnp.broadcast_to(commit, (buses, LANES))
        nadual = nadual + disp1_ref[...] - commit
        price = price + mism1_ref[...] + region_term(param, regional_ref[...], buses_all)
    else:
        commit = column(param, 5)
    want = (load + net - price - column(param, 3) + (commit - nadual)) / (
        2.0 * column(param, 2) + 2.0
    )
    dispatch = jnp.clip(want, 0.0, column(param, 4))
    mismatch = dispatch - load - net
    disp_out[...] = dispatch
    if second:
        price_out[...] = price + mismatch
    else:
        mism_out[...] = mismatch
    region = lax.broadcasted_iota(jnp.int32, (REGIONS, buses), 0) == region_ref[...]
    part = picked(region.astype(BF16), mismatch, 3)
    for copy in range(part_out.shape[0] // REGIONS):
        part_out[copy * REGIONS : (copy + 1) * REGIONS, :] = part
    total = None
    ones = jnp.ones((total_out.shape[0], LANES), BF16)
    for piece in pieces(dispatch + nadual, 3):
        term = dot_lanes(ones, piece)
        total = term if total is None else total + term
    total_out[...] = total


def close_kernel(buses_all, param_ref, regional_ref, price_ref, out_ref):
    regional = regional_ref[0:REGIONS, :]
    for part in range(1, regional_ref.shape[0] // REGIONS):
        regional = regional + regional_ref[part * REGIONS : (part + 1) * REGIONS, :]
    out_ref[...] = price_ref[...] + region_term(param_ref[...], regional, buses_all)


def on_device(
    volt_init,
    line_dual,
    conductance,
    susceptance,
    endpoint_owner,
    endpoint_bus,
    line_count,
    bus_region,
    vm_set,
    stiffness,
    load,
    price_init,
    na_dual_init,
    commit_init,
    cost_quad,
    cost_lin,
    pmax,
):
    ngrid = lax.axis_size("grid")
    nscen = lax.axis_size("scen")
    lines = conductance.shape[0]
    ends = 2 * lines
    buses = vm_set.shape[0]
    scen = load.shape[1]
    buses_all = buses * ngrid
    shape = jax.ShapeDtypeStruct

    def exchange(x):
        return lax.all_to_all(x, "grid", split_axis=0, concat_axis=0, tiled=True)

    slot, request = pl.pallas_call(
        plan_kernel,
        out_shape=(shape((1, ends), jnp.int32), shape((ngrid, LANES), jnp.int32)),
        in_specs=[smem(), vmem(), vmem()],
        out_specs=(vmem(), vmem()),
        compiler_params=pltpu.CompilerParams(vmem_limit_bytes=GRANT),
        name="plan",
    )(line_count, endpoint_owner.reshape(1, ends), endpoint_bus.reshape(1, ends))
    slot = slot.reshape(ends)
    asked = exchange(request)
    asked_row = asked[:, :CAP].reshape(1, ngrid * CAP)

    line_param = jnp.stack([conductance, susceptance], axis=1)
    bus_param = jnp.stack(
        [stiffness, vm_set, cost_quad, cost_lin, pmax, commit_init, bus_region.astype(F32),
         jnp.zeros_like(pmax)],
        axis=1,
    )
    region_row = bus_region.reshape(1, buses)
    send_shape = shape((ngrid, 2 * CAP, LANES), F32)
    bus_shape = shape((buses, LANES), F32)

    sent = pl.pallas_call(
        first_send_kernel,
        out_shape=send_shape,
        in_specs=[smem(), vmem()],
        out_specs=vmem(),
        compiler_params=pltpu.CompilerParams(vmem_limit_bytes=GRANT),
        name="first_send",
    )(asked, volt_init)

    def line_call(second, arrived, previous):
        outs = [shape((ngrid * 3 * CAP, LANES), F32), shape((4, lines, LANES), F32)]
        args = [line_count, slot, arrived.reshape(ngrid * 2 * CAP, LANES), line_dual]
        if second:
            args.append(previous)
        args.append(line_param)
        out, other = pl.pallas_call(
            functools.partial(line_kernel, second),
            out_shape=outs,
            in_specs=[smem(), smem()] + [vmem()] * (len(args) - 2),
            out_specs=[vmem(), vmem()],
            scratch_shapes=[VMEM((4, BLOCK, LANES), F32), VMEM((6, BLOCK, LANES), F32)],
            compiler_params=pltpu.CompilerParams(vmem_limit_bytes=GRANT),
            name="lines2" if second else "lines1",
        )(*args)
        return out.reshape(ngrid, 3 * CAP, LANES), other

    def owner_call(second, received, volt, extra):
        outs = [shape((2, buses, LANES), F32), bus_shape]
        if not second:
            outs.append(bus_shape)
        copies = NEAR if second else 1
        outs += [shape((copies * REGIONS, LANES), F32), shape((8, buses), F32)]
        outs.append(bus_shape if second else send_shape)
        args = [asked, asked_row, received, volt, bus_param, region_row, load, price_init,
                na_dual_init] + list(extra)
        return pl.pallas_call(
            functools.partial(owner_kernel, second, buses_all, scen * nscen),
            out_shape=outs,
            in_specs=[smem()] + [vmem()] * (len(args) - 1),
            out_specs=[vmem()] * len(outs),
            compiler_params=pltpu.CompilerParams(vmem_limit_bytes=GRANT),
            name="owner2" if second else "owner1",
        )(*args)

    def doubling_sum(x, axis, size):
        step = 1
        while step < size:
            x = x + lax.ppermute(x, axis, [(i, i ^ step) for i in range(size)])
            step *= 2
        return x

    out, state = line_call(False, exchange(sent), None)
    volt, disp1, mism1, part, total, sent = owner_call(False, exchange(out), volt_init, ())
    arrived = exchange(sent)
    totals = doubling_sum(total, "scen", nscen)
    regional = doubling_sum(part, "grid", ngrid)
    out, dual = line_call(True, arrived, state)
    volt, dispatch, part, total, price = owner_call(
        True, exchange(out), volt, (disp1, mism1, regional, totals)
    )
    commit = doubling_sum(total, "scen", nscen)[0] / (scen * nscen)
    near = [[i * NEAR + j for j in range(NEAR)] for i in range(ngrid // NEAR)]
    far = [[i * NEAR + j for i in range(ngrid // NEAR)] for j in range(NEAR)]
    part = lax.all_to_all(part, "grid", 0, 0, axis_index_groups=near, tiled=True)
    part = jnp.sum(part.reshape(NEAR, REGIONS, LANES), axis=0)
    part = jnp.broadcast_to(part[None], (ngrid // NEAR, REGIONS, LANES))
    parts = lax.all_to_all(part, "grid", 0, 0, axis_index_groups=far, tiled=True)
    price = pl.pallas_call(
        functools.partial(close_kernel, buses_all),
        out_shape=bus_shape,
        in_specs=[vmem()] * 3,
        out_specs=vmem(),
        compiler_params=pltpu.CompilerParams(vmem_limit_bytes=GRANT),
        name="close",
    )(bus_param, parts.reshape(ngrid // NEAR * REGIONS, LANES), price)
    return (volt, dual, dispatch, price, commit)


def solution(mesh):
    in_specs = (
        P(None, "grid", "scen"),
        P(None, "grid", "scen"),
        P("grid"),
        P("grid"),
        P("grid", None),
        P("grid"),
        P("grid"),
        P("grid"),
        P("grid"),
        P("grid"),
        P("grid", "scen"),
        P("grid", "scen"),
        P("grid", "scen"),
        P("grid"),
        P("grid"),
        P("grid"),
        P("grid"),
    )
    out_specs = (
        P(None, "grid", "scen"),
        P(None, "grid", "scen"),
        P("grid", "scen"),
        P("grid", "scen"),
        P("grid"),
    )
    return jax.shard_map(
        on_device, mesh=mesh, in_specs=in_specs, out_specs=out_specs, check_vma=False
    )
```

```python
import functools

import jax
import jax.numpy as jnp
from jax import lax
from jax.experimental import pallas as pl
from jax.experimental.pallas import tpu as pltpu
from jax.sharding import PartitionSpec as P

NEWTON = 3
REGIONS = 16
CAP = 16
LANES = 128
REGION_GAIN = 10.0
BLOCK = 32
NEAR = 4
GRANT = 16 * 2**20

F32 = jnp.float32
BF16 = jnp.bfloat16
SMEM = pltpu.SMEM
VMEM = pltpu.VMEM


def smem():
    return pl.BlockSpec(memory_space=SMEM)


def vmem():
    return pl.BlockSpec(memory_space=VMEM)


def pieces(x, count):
    parts = []
    for _ in range(count - 1):
        head = x.astype(BF16)
        parts.append(head)
        x = x - head.astype(F32)
    parts.append(x.astype(BF16))
    return parts


def picked(selector, x, count):
    total = None
    for part in pieces(x, count):
        term = jnp.dot(selector, part, preferred_element_type=F32)
        total = term if total is None else total + term
    return total


def dot_lanes(a, b):
    return lax.dot_general(a, b, (((1,), (1,)), ((), ())), preferred_element_type=F32)


def plan_kernel(count_ref, owner_ref, bus_ref, slot_ref, request_ref):
    ends = owner_ref.shape[1]
    owners = request_ref.shape[0]
    owner = owner_ref[...]
    end_id = lax.broadcasted_iota(jnp.int32, (1, ends), 1)
    live = lax.rem(end_id, ends // 2) < count_ref[0]
    code = jnp.where(live, bus_ref[...] + 1, 0).astype(F32)
    hits = lax.broadcasted_iota(jnp.int32, (owners, ends), 0) == owner
    hits = hits.astype(F32)
    before = lax.broadcasted_iota(jnp.int32, (ends, ends), 0) < lax.broadcasted_iota(
        jnp.int32, (ends, ends), 1
    )
    earlier = jnp.dot(hits.astype(BF16), before.astype(BF16), preferred_element_type=F32)
    rank = jnp.sum(hits * earlier, axis=0, keepdims=True).astype(jnp.int32)
    slot_ref[...] = owner * CAP + rank
    ranks = lax.broadcasted_iota(jnp.int32, (LANES, ends), 0) == rank
    table = dot_lanes((hits * code).astype(BF16), ranks.astype(BF16))
    request_ref[...] = table.astype(jnp.int32)


def send_rows(asked_ref, volt_ref, out_ref):
    def step(o, carry):
        for r in range(CAP):
            bus = jnp.maximum(asked_ref[o, r] - 1, 0)
            for c in range(2):
                out_ref[o, c * CAP + r : c * CAP + r + 1, :] = volt_ref[c, pl.ds(bus, 1), :]
        return carry

    lax.fori_loop(0, out_ref.shape[0], step, 0)


def first_send_kernel(asked_ref, volt_ref, out_ref):
    send_rows(asked_ref, volt_ref, out_ref)


def sin_cos(x):
    turns = jnp.floor(x * 0.636619772367581343 + 0.5)
    r = x - turns * 1.5703125
    r = r - turns * 4.83751296997070312e-04
    r = r - turns * 7.54978995489188216e-08
    n = turns.astype(jnp.int32)
    z = r * r
    s = ((-1.9515295891e-4 * z + 8.3321608736e-3) * z - 1.6666654611e-1) * z * r + r
    c = ((2.443315711809948e-5 * z - 1.388731625493765e-3) * z + 4.166664568298827e-2) * z * z
    c = c - 0.5 * z + 1.0
    odd = (n & 1) == 1
    sine = jnp.where(odd, c, s)
    cosine = jnp.where(odd, s, c)
    sine = jnp.where((n & 2) == 2, -sine, sine)
    cosine = jnp.where(((n + 1) & 2) == 2, -cosine, cosine)
    return sine, cosine


def branch_newton(center, cond, susc):
    k = 2.0 * cond
    vf, af, vt, at = center
    for step in range(NEWTON):
        s, c = sin_cos(af - at)
        w0 = vf - vt * c
        w1 = vt * s
        if step > 0:
            r0, r1, r2, r3 = vf - center[0], af - center[1], vt - center[2], at - center[3]
            r3 = vt * r3
            w0 = w0 - r0 + r2 * c + r3 * s
            w1 = w1 - r1 * vf - r2 * s + r3 * c
        ss, cc, tt = s * s, c * c, vt * vt
        m00 = 1.0 + k * (1.0 + cc + tt * ss)
        m11 = 1.0 + k * (vf * vf + ss + tt * cc)
        m01 = k * (s * c * (tt - 1.0))
        scale = k / (m00 * m11 - m01 * m01)
        z0 = (m11 * w0 - m01 * w1) * scale
        z1 = (m00 * w1 - m01 * w0) * scale
        new = (
            center[0] - z0,
            center[1] - vf * z1,
            center[2] + (c * z0 - s * z1),
            center[3] + vt * (s * z0 + c * z1),
        )
        vf, af, vt, at = new
    s, c = sin_cos(af - at)
    product = vf * vt
    flow_from = cond * vf * vf - product * (cond * c + susc * s)
    flow_to = cond * vt * vt - product * (cond * c - susc * s)
    return (vf, af, vt, at), flow_from, flow_to


def line_kernel(second, count_ref, slot_ref, arrived_ref, dual_ref, *refs):
    if second:
        previous_ref, param_ref, out_ref, dual_out_ref, near_ref, term_ref = refs
    else:
        param_ref, out_ref, state_ref, near_ref, term_ref = refs
    lines = dual_ref.shape[1]

    def step(block, carry):
        base = pl.multiple_of(block * BLOCK, BLOCK)
        rows = pl.ds(base, BLOCK)
        starts = []
        for end in range(2):
            for j in range(BLOCK):
                slot = slot_ref[end * lines + base + j]
                high = slot & -CAP
                starts.append((slot + high, slot + high + high))
        for end in range(2):
            for j in range(BLOCK):
                start = starts[end * BLOCK + j][0]
                for c in range(2):
                    near_ref[2 * end + c, j : j + 1, :] = arrived_ref[pl.ds(start + c * CAP, 1), :]
        near = [near_ref[i] for i in range(4)]
        dual = [dual_ref[i, rows, :] for i in range(4)]
        line_id = lax.broadcasted_iota(jnp.int32, (BLOCK, LANES), 0) + base
        live = line_id < count_ref[0]
        if second:
            dual = [
                jnp.where(live, dual[i] + previous_ref[i, rows, :] - near[i], dual[i])
                for i in range(4)
            ]
            for i in range(4):
                dual_out_ref[i, rows, :] = dual[i]
        center = [near[i] - dual[i] for i in range(4)]
        param = param_ref[rows, :]
        cond = jnp.broadcast_to(param[:, 0:1], (BLOCK, LANES))
        susc = jnp.broadcast_to(param[:, 1:2], (BLOCK, LANES))
        state, flow_from, flow_to = branch_newton(center, cond, susc)
        if not second:
            for i in range(4):
                state_ref[i, rows, :] = state[i]
        terms = [
            state[0] + dual[0], state[1] + dual[1], flow_from,
            state[2] + dual[2], state[3] + dual[3], flow_to,
        ]
        for i in range(6):
            term_ref[i] = jnp.where(live, terms[i], 0.0)
        for end in range(2):
            for j in range(BLOCK):
                start = starts[end * BLOCK + j][1]
                for c in range(3):
                    out_ref[pl.ds(start + c * CAP, 1), :] = term_ref[3 * end + c, j : j + 1, :]
        return carry

    out_ref[...] = jnp.zeros_like(out_ref)
    lax.fori_loop(0, lines // BLOCK, step, 0)


def column(param, index):
    return jnp.broadcast_to(param[:, index : index + 1], (param.shape[0], LANES))


def region_term(param, regional, buses_all):
    ids = lax.broadcasted_iota(jnp.int32, (param.shape[0], REGIONS), 1)
    member = ids == param[:, 6:7].astype(jnp.int32)
    total = picked(member.astype(BF16), regional, 3)
    return total * (REGION_GAIN * REGIONS / buses_all)


def owner_kernel(second, buses_all, scen_all, asked_ref, row_ref, recv_ref, volt_ref, param_ref,
                 region_ref, load_ref, price_ref, nadual_ref, *refs):
    if second:
        (disp1_ref, mism1_ref, regional_ref, totals_ref,
         volt_out, disp_out, part_out, total_out, price_out) = refs
    else:
        volt_out, disp_out, mism_out, part_out, total_out, send_out = refs
    buses = volt_ref.shape[1]
    devices = recv_ref.shape[0]
    slots = devices * CAP
    ids = lax.broadcasted_iota(jnp.int32, (buses, slots), 0) + 1
    hits = (ids == row_ref[...]).astype(BF16)
    rows = [recv_ref[:, c * CAP : (c + 1) * CAP, :].reshape(slots, LANES) for c in range(3)]
    pair = picked(hits, jnp.concatenate(rows[:2], axis=1), 2)
    flows = pieces(rows[2], 2)
    ones = jnp.ones((slots, LANES), BF16)
    last = jnp.dot(hits, jnp.concatenate([flows[0], ones], axis=1), preferred_element_type=F32)
    net = last[:, :LANES] + jnp.dot(hits, flows[1], preferred_element_type=F32)
    degree = last[:, LANES:]
    param = param_ref[...]
    weight = column(param, 0)
    inverse = 1.0 / (degree + weight)
    volt_out[0] = (pair[:, :LANES] + weight * column(param, 1)) * inverse
    volt_out[1] = (pair[:, LANES:] + weight * volt_ref[1]) * inverse
    if not second:
        send_rows(asked_ref, volt_out, send_out)
    load, price, nadual = load_ref[...], price_ref[...], nadual_ref[...]
    if second:
        commit = jnp.transpose(totals_ref[...])[:, 0:1] / scen_all
        commit = jnp.broadcast_to(commit, (buses, LANES))
        nadual = nadual + disp1_ref[...] - commit
        price = price + mism1_ref[...] + region_term(param, regional_ref[...], buses_all)
    else:
        commit = column(param, 5)
    want = (load + net - price - column(param, 3) + (commit - nadual)) / (
        2.0 * column(param, 2) + 2.0
    )
    dispatch = jnp.clip(want, 0.0, column(param, 4))
    mismatch = dispatch - load - net
    disp_out[...] = dispatch
    if second:
        price_out[...] = price + mismatch
    else:
        mism_out[...] = mismatch
    region = lax.broadcasted_iota(jnp.int32, (REGIONS, buses), 0) == region_ref[...]
    part = picked(region.astype(BF16), mismatch, 3)
    for copy in range(part_out.shape[0] // REGIONS):
        part_out[copy * REGIONS : (copy + 1) * REGIONS, :] = part
    total = None
    ones = jnp.ones((total_out.shape[0], LANES), BF16)
    for piece in pieces(dispatch + nadual, 3):
        term = dot_lanes(ones, piece)
        total = term if total is None else total + term
    total_out[...] = total


def close_kernel(buses_all, param_ref, regional_ref, price_ref, out_ref):
    regional = regional_ref[0:REGIONS, :]
    for part in range(1, regional_ref.shape[0] // REGIONS):
        regional = regional + regional_ref[part * REGIONS : (part + 1) * REGIONS, :]
    out_ref[...] = price_ref[...] + region_term(param_ref[...], regional, buses_all)


def on_device(
    volt_init,
    line_dual,
    conductance,
    susceptance,
    endpoint_owner,
    endpoint_bus,
    line_count,
    bus_region,
    vm_set,
    stiffness,
    load,
    price_init,
    na_dual_init,
    commit_init,
    cost_quad,
    cost_lin,
    pmax,
):
    ngrid = lax.axis_size("grid")
    nscen = lax.axis_size("scen")
    lines = conductance.shape[0]
    ends = 2 * lines
    buses = vm_set.shape[0]
    scen = load.shape[1]
    buses_all = buses * ngrid
    shape = jax.ShapeDtypeStruct

    def exchange(x):
        return lax.all_to_all(x, "grid", split_axis=0, concat_axis=0, tiled=True)

    slot, request = pl.pallas_call(
        plan_kernel,
        out_shape=(shape((1, ends), jnp.int32), shape((ngrid, LANES), jnp.int32)),
        in_specs=[smem(), vmem(), vmem()],
        out_specs=(vmem(), vmem()),
        compiler_params=pltpu.CompilerParams(vmem_limit_bytes=GRANT),
        name="plan",
    )(line_count, endpoint_owner.reshape(1, ends), endpoint_bus.reshape(1, ends))
    slot = slot.reshape(ends)
    asked = exchange(request)
    asked_row = asked[:, :CAP].reshape(1, ngrid * CAP)

    line_param = jnp.stack([conductance, susceptance], axis=1)
    bus_param = jnp.stack(
        [stiffness, vm_set, cost_quad, cost_lin, pmax, commit_init, bus_region.astype(F32),
         jnp.zeros_like(pmax)],
        axis=1,
    )
    region_row = bus_region.reshape(1, buses)
    send_shape = shape((ngrid, 2 * CAP, LANES), F32)
    bus_shape = shape((buses, LANES), F32)

    sent = pl.pallas_call(
        first_send_kernel,
        out_shape=send_shape,
        in_specs=[smem(), vmem()],
        out_specs=vmem(),
        compiler_params=pltpu.CompilerParams(vmem_limit_bytes=GRANT),
        name="first_send",
    )(asked, volt_init)

    def line_call(second, arrived, previous):
        outs = [shape((ngrid * 3 * CAP, LANES), F32), shape((4, lines, LANES), F32)]
        args = [line_count, slot, arrived.reshape(ngrid * 2 * CAP, LANES), line_dual]
        if second:
            args.append(previous)
        args.append(line_param)
        out, other = pl.pallas_call(
            functools.partial(line_kernel, second),
            out_shape=outs,
            in_specs=[smem(), smem()] + [vmem()] * (len(args) - 2),
            out_specs=[vmem(), vmem()],
            scratch_shapes=[VMEM((4, BLOCK, LANES), F32), VMEM((6, BLOCK, LANES), F32)],
            compiler_params=pltpu.CompilerParams(vmem_limit_bytes=GRANT),
            name="lines2" if second else "lines1",
        )(*args)
        return out.reshape(ngrid, 3 * CAP, LANES), other

    def owner_call(second, received, volt, extra):
        outs = [shape((2, buses, LANES), F32), bus_shape]
        if not second:
            outs.append(bus_shape)
        copies = NEAR if second else 1
        outs += [shape((copies * REGIONS, LANES), F32), shape((8, buses), F32)]
        outs.append(bus_shape if second else send_shape)
        args = [asked, asked_row, received, volt, bus_param, region_row, load, price_init,
                na_dual_init] + list(extra)
        return pl.pallas_call(
            functools.partial(owner_kernel, second, buses_all, scen * nscen),
            out_shape=outs,
            in_specs=[smem()] + [vmem()] * (len(args) - 1),
            out_specs=[vmem()] * len(outs),
            compiler_params=pltpu.CompilerParams(vmem_limit_bytes=GRANT),
            name="owner2" if second else "owner1",
        )(*args)

    def near_sum(x, axis, size, step, count):
        parts = [
            lax.ppermute(x, axis, [(i, i ^ (k * step)) for i in range(size)])
            for k in range(1, count)
        ]
        return sum(parts, x)

    def doubling_sum(x, axis, size):
        step = 1
        while step < size:
            x = near_sum(x, axis, size, step, 2)
            step *= 2
        return x

    out, state = line_call(False, exchange(sent), None)
    volt, disp1, mism1, part, total, sent = owner_call(False, exchange(out), volt_init, ())
    arrived = exchange(sent)
    for step in range(1, NEAR):
        if step & (step - 1) == 0:
            part = near_sum(part, "grid", ngrid, step, 2)
    part = near_sum(part, "grid", ngrid, NEAR, NEAR)
    arrived, part = lax.optimization_barrier((arrived, part))
    totals = doubling_sum(total, "scen", nscen)
    regional = near_sum(part, "grid", ngrid, NEAR * NEAR, ngrid // (NEAR * NEAR))
    out, dual = line_call(True, arrived, state)
    volt, dispatch, part, total, price = owner_call(
        True, exchange(out), volt, (disp1, mism1, regional, totals)
    )
    commit = doubling_sum(total, "scen", nscen)[0] / (scen * nscen)
    near = [[i * NEAR + j for j in range(NEAR)] for i in range(ngrid // NEAR)]
    far = [[i * NEAR + j for i in range(ngrid // NEAR)] for j in range(NEAR)]
    part = lax.all_to_all(part, "grid", 0, 0, axis_index_groups=near, tiled=True)
    part = jnp.sum(part.reshape(NEAR, REGIONS, LANES), axis=0)
    part = jnp.broadcast_to(part[None], (ngrid // NEAR, REGIONS, LANES))
    parts = lax.all_to_all(part, "grid", 0, 0, axis_index_groups=far, tiled=True)
    price = pl.pallas_call(
        functools.partial(close_kernel, buses_all),
        out_shape=bus_shape,
        in_specs=[vmem()] * 3,
        out_specs=vmem(),
        compiler_params=pltpu.CompilerParams(vmem_limit_bytes=GRANT),
        name="close",
    )(bus_param, parts.reshape(ngrid // NEAR * REGIONS, LANES), price)
    return (volt, dual, dispatch, price, commit)


def solution(mesh):
    in_specs = (
        P(None, "grid", "scen"),
        P(None, "grid", "scen"),
        P("grid"),
        P("grid"),
        P("grid", None),
        P("grid"),
        P("grid"),
        P("grid"),
        P("grid"),
        P("grid"),
        P("grid", "scen"),
        P("grid", "scen"),
        P("grid", "scen"),
        P("grid"),
        P("grid"),
        P("grid"),
        P("grid"),
    )
    out_specs = (
        P(None, "grid", "scen"),
        P(None, "grid", "scen"),
        P("grid", "scen"),
        P("grid", "scen"),
        P("grid"),
    )
    return jax.shard_map(
        on_device, mesh=mesh, in_specs=in_specs, out_specs=out_specs, check_vma=False
    )
```

```python
import functools

import jax
import jax.numpy as jnp
from jax import lax
from jax.experimental import pallas as pl
from jax.experimental.pallas import tpu as pltpu
from jax.sharding import PartitionSpec as P

NEWTON = 3
REGIONS = 16
CAP = 16
LANES = 128
REGION_GAIN = 10.0
BLOCK = 16
NEAR = 4
GRANT = 16 * 2**20

F32 = jnp.float32
BF16 = jnp.bfloat16
SMEM = pltpu.SMEM
VMEM = pltpu.VMEM


def smem():
    return pl.BlockSpec(memory_space=SMEM)


def vmem():
    return pl.BlockSpec(memory_space=VMEM)


def pieces(x, count):
    parts = []
    for _ in range(count - 1):
        head = x.astype(BF16)
        parts.append(head)
        x = x - head.astype(F32)
    parts.append(x.astype(BF16))
    return parts


def picked(selector, x, count):
    total = None
    for part in pieces(x, count):
        term = jnp.dot(selector, part, preferred_element_type=F32)
        total = term if total is None else total + term
    return total


def dot_lanes(a, b):
    return lax.dot_general(a, b, (((1,), (1,)), ((), ())), preferred_element_type=F32)


def plan_kernel(count_ref, owner_ref, bus_ref, slot_ref, request_ref):
    ends = owner_ref.shape[1]
    owners = request_ref.shape[0]
    owner = owner_ref[...]
    end_id = lax.broadcasted_iota(jnp.int32, (1, ends), 1)
    live = lax.rem(end_id, ends // 2) < count_ref[0]
    code = jnp.where(live, bus_ref[...] + 1, 0).astype(F32)
    hits = lax.broadcasted_iota(jnp.int32, (owners, ends), 0) == owner
    hits = hits.astype(F32)
    before = lax.broadcasted_iota(jnp.int32, (ends, ends), 0) < lax.broadcasted_iota(
        jnp.int32, (ends, ends), 1
    )
    earlier = jnp.dot(hits.astype(BF16), before.astype(BF16), preferred_element_type=F32)
    rank = jnp.sum(hits * earlier, axis=0, keepdims=True).astype(jnp.int32)
    slot_ref[...] = owner * CAP + rank
    ranks = lax.broadcasted_iota(jnp.int32, (LANES, ends), 0) == rank
    table = dot_lanes((hits * code).astype(BF16), ranks.astype(BF16))
    request_ref[...] = table.astype(jnp.int32)


def send_rows(asked_ref, volt_ref, out_ref):
    buses = volt_ref.shape[1]

    def step(o, carry):
        for r in range(CAP):
            bus = (asked_ref[o, r] - 1) & (buses - 1)
            for c in range(2):
                out_ref[o, c * CAP + r : c * CAP + r + 1, :] = volt_ref[c, pl.ds(bus, 1), :]
        return carry

    lax.fori_loop(0, out_ref.shape[0], step, 0, unroll=4)


def first_send_kernel(asked_ref, volt_ref, out_ref):
    send_rows(asked_ref, volt_ref, out_ref)


def sin_cos(x):
    turns = jnp.floor(x * 0.636619772367581343 + 0.5)
    r = x - turns * 1.5703125
    r = r - turns * 4.83751296997070312e-04
    r = r - turns * 7.54978995489188216e-08
    n = turns.astype(jnp.int32)
    z = r * r
    s = ((-1.9515295891e-4 * z + 8.3321608736e-3) * z - 1.6666654611e-1) * z * r + r
    c = ((2.443315711809948e-5 * z - 1.388731625493765e-3) * z + 4.166664568298827e-2) * z * z
    c = c - 0.5 * z + 1.0
    odd = (n & 1) == 1
    sine = jnp.where(odd, c, s)
    cosine = jnp.where(odd, s, c)
    sine = jnp.where((n & 2) == 2, -sine, sine)
    cosine = jnp.where(((n + 1) & 2) == 2, -cosine, cosine)
    return sine, cosine


def branch_newton(center, cond, susc):
    k = 2.0 * cond
    vf, af, vt, at = center
    for step in range(NEWTON):
        s, c = sin_cos(af - at)
        w0 = vf - vt * c
        w1 = vt * s
        if step > 0:
            r0, r1, r2, r3 = vf - center[0], af - center[1], vt - center[2], at - center[3]
            r3 = vt * r3
            w0 = w0 - r0 + r2 * c + r3 * s
            w1 = w1 - r1 * vf - r2 * s + r3 * c
        ss, cc, tt = s * s, c * c, vt * vt
        m00 = 1.0 + k * (1.0 + cc + tt * ss)
        m11 = 1.0 + k * (vf * vf + ss + tt * cc)
        m01 = k * (s * c * (tt - 1.0))
        scale = k / (m00 * m11 - m01 * m01)
        z0 = (m11 * w0 - m01 * w1) * scale
        z1 = (m00 * w1 - m01 * w0) * scale
        new = (
            center[0] - z0,
            center[1] - vf * z1,
            center[2] + (c * z0 - s * z1),
            center[3] + vt * (s * z0 + c * z1),
        )
        vf, af, vt, at = new
    s, c = sin_cos(af - at)
    product = vf * vt
    flow_from = cond * vf * vf - product * (cond * c + susc * s)
    flow_to = cond * vt * vt - product * (cond * c - susc * s)
    return (vf, af, vt, at), flow_from, flow_to


def line_kernel(second, count_ref, slot_ref, arrived_ref, dual_ref, *refs):
    if second:
        previous_ref, param_ref, out_ref, dual_out_ref, *scratch = refs
    else:
        param_ref, out_ref, state_ref, *scratch = refs
    near_refs, term_refs = scratch[:2], scratch[2:]
    lines = dual_ref.shape[1]
    blocks = lines // BLOCK

    def gather(block, near_ref):
        for end in range(2):
            for j in range(BLOCK):
                slot = slot_ref[end * lines + block * BLOCK + j]
                start = slot + (slot & -CAP)
                for c in range(2):
                    near_ref[2 * end + c, j : j + 1, :] = arrived_ref[pl.ds(start + c * CAP, 1), :]

    def scatter(block, term_ref):
        for end in range(2):
            for j in range(BLOCK):
                slot = slot_ref[end * lines + block * BLOCK + j]
                start = slot + 2 * (slot & -CAP)
                for c in range(3):
                    out_ref[pl.ds(start + c * CAP, 1), :] = term_ref[3 * end + c, j : j + 1, :]

    def solve(block, near_ref, term_ref):
        base = pl.multiple_of(block * BLOCK, BLOCK)
        rows = pl.ds(base, BLOCK)
        near = [near_ref[i] for i in range(4)]
        dual = [dual_ref[i, rows, :] for i in range(4)]
        line_id = lax.broadcasted_iota(jnp.int32, (BLOCK, LANES), 0) + base
        live = line_id < count_ref[0]
        if second:
            dual = [
                jnp.where(live, dual[i] + previous_ref[i, rows, :] - near[i], dual[i])
                for i in range(4)
            ]
            for i in range(4):
                dual_out_ref[i, rows, :] = dual[i]
        center = [near[i] - dual[i] for i in range(4)]
        param = param_ref[rows, :]
        cond = jnp.broadcast_to(param[:, 0:1], (BLOCK, LANES))
        susc = jnp.broadcast_to(param[:, 1:2], (BLOCK, LANES))
        state, flow_from, flow_to = branch_newton(center, cond, susc)
        if not second:
            for i in range(4):
                state_ref[i, rows, :] = state[i]
        terms = [
            state[0] + dual[0], state[1] + dual[1], flow_from,
            state[2] + dual[2], state[3] + dual[3], flow_to,
        ]
        for i in range(6):
            term_ref[i] = jnp.where(live, terms[i], 0.0)

    def step(pair, carry):
        block = 2 * pair
        scatter(lax.rem(block + blocks - 1, blocks), term_refs[1])
        gather(block + 1, near_refs[1])
        solve(block, near_refs[0], term_refs[0])
        gather(lax.rem(block + 2, blocks), near_refs[0])
        scatter(block, term_refs[0])
        solve(block + 1, near_refs[1], term_refs[1])
        return carry

    out_ref[...] = jnp.zeros_like(out_ref)
    term_refs[1][...] = jnp.zeros_like(term_refs[1])
    gather(0, near_refs[0])
    lax.fori_loop(0, blocks // 2, step, 0)
    scatter(blocks - 1, term_refs[1])


def column(param, index):
    return jnp.broadcast_to(param[:, index : index + 1], (param.shape[0], LANES))


def region_term(param, regional, buses_all):
    ids = lax.broadcasted_iota(jnp.int32, (param.shape[0], REGIONS), 1)
    member = ids == param[:, 6:7].astype(jnp.int32)
    total = picked(member.astype(BF16), regional, 3)
    return total * (REGION_GAIN * REGIONS / buses_all)


def bus_hits(row_ref, buses):
    slots = row_ref.shape[1]
    ids = lax.broadcasted_iota(jnp.int32, (buses, slots), 0) + 1
    return (ids == row_ref[...]).astype(BF16)


def slot_rows(recv_ref, c):
    return recv_ref[:, c * CAP : (c + 1) * CAP, :].reshape(recv_ref.shape[0] * CAP, LANES)


def volt_kernel(send, asked_ref, row_ref, recv_ref, volt_ref, param_ref, volt_out, *refs):
    hits = bus_hits(row_ref, volt_ref.shape[1])
    rows = jnp.concatenate([slot_rows(recv_ref, 0), slot_rows(recv_ref, 1)], axis=1)
    pair = picked(hits, rows, 2)
    ones = jnp.ones((hits.shape[1], LANES), BF16)
    degree = jnp.dot(hits, ones, preferred_element_type=F32)
    param = param_ref[...]
    weight = column(param, 0)
    inverse = 1.0 / (degree + weight)
    volt_out[0] = (pair[:, :LANES] + weight * column(param, 1)) * inverse
    volt_out[1] = (pair[:, LANES:] + weight * volt_ref[1]) * inverse
    if send:
        send_rows(asked_ref, volt_out, refs[0])


def dispatch_kernel(second, buses_all, scen_all, row_ref, recv_ref, param_ref, region_ref,
                    load_ref, price_ref, nadual_ref, *refs):
    if second:
        (disp1_ref, mism1_ref, regional_ref, totals_ref,
         disp_out, part_out, total_out, price_out) = refs
    else:
        disp_out, mism_out, part_out, total_out = refs
    buses = load_ref.shape[0]
    net = picked(bus_hits(row_ref, buses), slot_rows(recv_ref, 2), 2)
    param = param_ref[...]
    load, price, nadual = load_ref[...], price_ref[...], nadual_ref[...]
    if second:
        commit = jnp.transpose(totals_ref[...])[:, 0:1] / scen_all
        commit = jnp.broadcast_to(commit, (buses, LANES))
        nadual = nadual + disp1_ref[...] - commit
        price = price + mism1_ref[...] + region_term(param, regional_ref[...], buses_all)
    else:
        commit = column(param, 5)
    want = (load + net - price - column(param, 3) + (commit - nadual)) / (
        2.0 * column(param, 2) + 2.0
    )
    dispatch = jnp.clip(want, 0.0, column(param, 4))
    mismatch = dispatch - load - net
    disp_out[...] = dispatch
    if second:
        price_out[...] = price + mismatch
    else:
        mism_out[...] = mismatch
    region = lax.broadcasted_iota(jnp.int32, (REGIONS, buses), 0) == region_ref[...]
    part = picked(region.astype(BF16), mismatch, 3)
    for copy in range(part_out.shape[0] // REGIONS):
        part_out[copy * REGIONS : (copy + 1) * REGIONS, :] = part
    total = None
    ones = jnp.ones((total_out.shape[0], LANES), BF16)
    for piece in pieces(dispatch + nadual, 3):
        term = dot_lanes(ones, piece)
        total = term if total is None else total + term
    total_out[...] = total


def close_kernel(buses_all, param_ref, regional_ref, price_ref, out_ref):
    regional = regional_ref[0:REGIONS, :]
    for part in range(1, regional_ref.shape[0] // REGIONS):
        regional = regional + regional_ref[part * REGIONS : (part + 1) * REGIONS, :]
    out_ref[...] = price_ref[...] + region_term(param_ref[...], regional, buses_all)


def on_device(
    volt_init,
    line_dual,
    conductance,
    susceptance,
    endpoint_owner,
    endpoint_bus,
    line_count,
    bus_region,
    vm_set,
    stiffness,
    load,
    price_init,
    na_dual_init,
    commit_init,
    cost_quad,
    cost_lin,
    pmax,
):
    ngrid = lax.axis_size("grid")
    nscen = lax.axis_size("scen")
    lines = conductance.shape[0]
    ends = 2 * lines
    buses = vm_set.shape[0]
    scen = load.shape[1]
    buses_all = buses * ngrid
    shape = jax.ShapeDtypeStruct

    def exchange(x):
        return lax.all_to_all(x, "grid", split_axis=0, concat_axis=0, tiled=True)

    slot, request = pl.pallas_call(
        plan_kernel,
        out_shape=(shape((1, ends), jnp.int32), shape((ngrid, LANES), jnp.int32)),
        in_specs=[smem(), vmem(), vmem()],
        out_specs=(vmem(), vmem()),
        compiler_params=pltpu.CompilerParams(vmem_limit_bytes=GRANT),
        name="plan",
    )(line_count, endpoint_owner.reshape(1, ends), endpoint_bus.reshape(1, ends))
    slot = slot.reshape(ends)
    asked = exchange(request)
    asked_row = asked[:, :CAP].reshape(1, ngrid * CAP)

    line_param = jnp.stack([conductance, susceptance], axis=1)
    bus_param = jnp.stack(
        [stiffness, vm_set, cost_quad, cost_lin, pmax, commit_init, bus_region.astype(F32),
         jnp.zeros_like(pmax)],
        axis=1,
    )
    region_row = bus_region.reshape(1, buses)
    send_shape = shape((ngrid, 2 * CAP, LANES), F32)
    bus_shape = shape((buses, LANES), F32)

    sent = pl.pallas_call(
        first_send_kernel,
        out_shape=send_shape,
        in_specs=[smem(), vmem()],
        out_specs=vmem(),
        compiler_params=pltpu.CompilerParams(vmem_limit_bytes=GRANT),
        name="first_send",
    )(asked, volt_init)

    def line_call(second, arrived, previous):
        outs = [shape((ngrid * 3 * CAP, LANES), F32), shape((4, lines, LANES), F32)]
        args = [line_count, slot, arrived.reshape(ngrid * 2 * CAP, LANES), line_dual]
        if second:
            args.append(previous)
        args.append(line_param)
        out, other = pl.pallas_call(
            functools.partial(line_kernel, second),
            out_shape=outs,
            in_specs=[smem(), smem()] + [vmem()] * (len(args) - 2),
            out_specs=[vmem(), vmem()],
            scratch_shapes=[VMEM((4, BLOCK, LANES), F32)] * 2 + [VMEM((6, BLOCK, LANES), F32)] * 2,
            compiler_params=pltpu.CompilerParams(vmem_limit_bytes=GRANT),
            name="lines2" if second else "lines1",
        )(*args)
        return out.reshape(ngrid, 3 * CAP, LANES), other

    def volt_call(send, received, volt):
        outs = [shape((2, buses, LANES), F32)] + ([send_shape] if send else [])
        return pl.pallas_call(
            functools.partial(volt_kernel, send),
            out_shape=outs,
            in_specs=[smem()] + [vmem()] * 4,
            out_specs=[vmem()] * len(outs),
            compiler_params=pltpu.CompilerParams(vmem_limit_bytes=GRANT),
            name="volt1" if send else "volt2",
        )(asked, asked_row, received, volt, bus_param)

    def dispatch_call(second, received, extra):
        outs = [bus_shape] if second else [bus_shape] * 2
        copies = NEAR if second else 1
        outs += [shape((copies * REGIONS, LANES), F32), shape((8, buses), F32)]
        if second:
            outs.append(bus_shape)
        args = [asked_row, received, bus_param, region_row, load, price_init, na_dual_init]
        args += list(extra)
        return pl.pallas_call(
            functools.partial(dispatch_kernel, second, buses_all, scen * nscen),
            out_shape=outs,
            in_specs=[vmem()] * len(args),
            out_specs=[vmem()] * len(outs),
            compiler_params=pltpu.CompilerParams(vmem_limit_bytes=GRANT),
            name="dispatch2" if second else "dispatch1",
        )(*args)

    def near_sum(x, axis, size, step, count):
        parts = [
            lax.ppermute(x, axis, [(i, i ^ (k * step)) for i in range(size)])
            for k in range(1, count)
        ]
        return sum(parts, x)

    def doubling_sum(x, axis, count):
        step = 1
        while step < count:
            x = near_sum(x, axis, lax.axis_size(axis), step, 2)
            step *= 2
        return x

    out, state = line_call(False, exchange(sent), None)
    received = exchange(out)
    volt, sent = volt_call(True, received, volt_init)
    arrived = exchange(sent)
    disp1, mism1, part, total = dispatch_call(False, received, ())
    for step in range(1, NEAR):
        if step & (step - 1) == 0:
            part = near_sum(part, "grid", ngrid, step, 2)
    part = near_sum(part, "grid", ngrid, NEAR, NEAR)
    arrived, part = lax.optimization_barrier((arrived, part))
    totals = doubling_sum(total, "scen", nscen)
    regional = near_sum(part, "grid", ngrid, NEAR * NEAR, ngrid // (NEAR * NEAR))
    out, dual = line_call(True, arrived, state)
    received = exchange(out)
    dispatch, part, total, price = dispatch_call(True, received, (disp1, mism1, regional, totals))
    near = [[i * NEAR + j for j in range(NEAR)] for i in range(ngrid // NEAR)]
    far = [[i * NEAR + j for i in range(ngrid // NEAR)] for j in range(NEAR)]
    part = lax.all_to_all(part, "grid", 0, 0, axis_index_groups=near, tiled=True)
    total = doubling_sum(total, "scen", nscen // 2)
    part, total = lax.optimization_barrier((part, total))
    part = jnp.sum(part.reshape(NEAR, REGIONS, LANES), axis=0)
    part = jnp.broadcast_to(part[None], (ngrid // NEAR, REGIONS, LANES))
    parts = lax.all_to_all(part, "grid", 0, 0, axis_index_groups=far, tiled=True)
    commit = near_sum(total, "scen", nscen, nscen // 2, 2)[0] / (scen * nscen)
    (volt,) = volt_call(False, received, volt)
    price = pl.pallas_call(
        functools.partial(close_kernel, buses_all),
        out_shape=bus_shape,
        in_specs=[vmem()] * 3,
        out_specs=vmem(),
        compiler_params=pltpu.CompilerParams(vmem_limit_bytes=GRANT),
        name="close",
    )(bus_param, parts.reshape(ngrid // NEAR * REGIONS, LANES), price)
    return (volt, dual, dispatch, price, commit)


def solution(mesh):
    in_specs = (
        P(None, "grid", "scen"),
        P(None, "grid", "scen"),
        P("grid"),
        P("grid"),
        P("grid", None),
        P("grid"),
        P("grid"),
        P("grid"),
        P("grid"),
        P("grid"),
        P("grid", "scen"),
        P("grid", "scen"),
        P("grid", "scen"),
        P("grid"),
        P("grid"),
        P("grid"),
        P("grid"),
    )
    out_specs = (
        P(None, "grid", "scen"),
        P(None, "grid", "scen"),
        P("grid", "scen"),
        P("grid", "scen"),
        P("grid"),
    )
    return jax.shard_map(
        on_device, mesh=mesh, in_specs=in_specs, out_specs=out_specs, check_vma=False
    )
```

```python
import functools

import jax
import jax.numpy as jnp
from jax import lax
from jax.experimental import pallas as pl
from jax.experimental.pallas import tpu as pltpu
from jax.sharding import PartitionSpec as P

NEWTON = 3
REGIONS = 16
CAP = 16
LANES = 128
REGION_GAIN = 10.0
BLOCK = 16
GROUP = 4
PARTS = 4
NEAR = 4
GRANT = 16 * 2**20

F32 = jnp.float32
BF16 = jnp.bfloat16
SMEM = pltpu.SMEM
VMEM = pltpu.VMEM


def smem():
    return pl.BlockSpec(memory_space=SMEM)


def vmem():
    return pl.BlockSpec(memory_space=VMEM)


def hbm():
    return pl.BlockSpec(memory_space=pltpu.HBM)


def in_hbm(x):
    return pltpu.with_memory_space_constraint(x, pltpu.HBM)


def copies_of(pairs, sem):
    return [pltpu.make_async_copy(a, b, sem.at[i]) for i, (a, b) in enumerate(pairs)]


def start_all(copies):
    for copy in copies:
        copy.start()


def wait_all(copies):
    for copy in copies:
        copy.wait()


def pieces(x, count):
    parts = []
    for _ in range(count - 1):
        head = x.astype(BF16)
        parts.append(head)
        x = x - head.astype(F32)
    parts.append(x.astype(BF16))
    return parts


def picked(selector, x, count):
    total = None
    for part in pieces(x, count):
        term = jnp.dot(selector, part, preferred_element_type=F32)
        total = term if total is None else total + term
    return total


def dot_lanes(a, b):
    return lax.dot_general(a, b, (((1,), (1,)), ((), ())), preferred_element_type=F32)


def plan_kernel(count_ref, owner_hbm, bus_hbm, slot_ref, request_ref, owner_ref, bus_ref, sem):
    fetch = copies_of([(owner_hbm, owner_ref), (bus_hbm, bus_ref)], sem)
    start_all(fetch)
    wait_all(fetch)
    ends = owner_ref.shape[1]
    owners = request_ref.shape[0]
    owner = owner_ref[...]
    end_id = lax.broadcasted_iota(jnp.int32, (1, ends), 1)
    live = lax.rem(end_id, ends // 2) < count_ref[0]
    code = jnp.where(live, bus_ref[...] + 1, 0).astype(F32)
    hits = lax.broadcasted_iota(jnp.int32, (owners, ends), 0) == owner
    hits = hits.astype(F32)
    before = lax.broadcasted_iota(jnp.int32, (ends, ends), 0) < lax.broadcasted_iota(
        jnp.int32, (ends, ends), 1
    )
    earlier = jnp.dot(hits.astype(BF16), before.astype(BF16), preferred_element_type=F32)
    rank = jnp.sum(hits * earlier, axis=0, keepdims=True).astype(jnp.int32)
    slot_ref[...] = owner * CAP + rank
    ranks = lax.broadcasted_iota(jnp.int32, (LANES, ends), 0) == rank
    table = dot_lanes((hits * code).astype(BF16), ranks.astype(BF16))
    request_ref[...] = table.astype(jnp.int32)


def send_rows(asked_ref, volt_ref, out_hbm, row_ref, sem):
    buses = volt_ref.shape[1]
    groups = row_ref.shape[0] // GROUP

    def ship(group):
        part = pl.ds(group * GROUP, GROUP)
        return pltpu.make_async_copy(row_ref.at[part], out_hbm.at[part], sem.at[group])

    def step(group, carry):
        for i in range(GROUP):
            o = group * GROUP + i
            for r in range(CAP):
                bus = (asked_ref[o, r] - 1) & (buses - 1)
                for c in range(2):
                    row_ref[o, c * CAP + r : c * CAP + r + 1, :] = volt_ref[c, pl.ds(bus, 1), :]
        ship(group).start()
        return carry

    def done(group, carry):
        ship(group).wait()
        return carry

    lax.fori_loop(0, groups, step, 0)
    lax.fori_loop(0, groups, done, 0)


def first_send_kernel(asked_ref, volt_hbm, out_hbm, volt_ref, row_ref, volt_sem, sem):
    fetch = copies_of([(volt_hbm.at[c], volt_ref.at[c]) for c in range(2)], volt_sem)
    start_all(fetch)
    wait_all(fetch)
    send_rows(asked_ref, volt_ref, out_hbm, row_ref, sem)


def sin_cos(x):
    turns = jnp.floor(x * 0.636619772367581343 + 0.5)
    r = x - turns * 1.5703125
    r = r - turns * 4.83751296997070312e-04
    r = r - turns * 7.54978995489188216e-08
    n = turns.astype(jnp.int32)
    z = r * r
    s = ((-1.9515295891e-4 * z + 8.3321608736e-3) * z - 1.6666654611e-1) * z * r + r
    c = ((2.443315711809948e-5 * z - 1.388731625493765e-3) * z + 4.166664568298827e-2) * z * z
    c = c - 0.5 * z + 1.0
    odd = (n & 1) == 1
    sine = jnp.where(odd, c, s)
    cosine = jnp.where(odd, s, c)
    sine = jnp.where((n & 2) == 2, -sine, sine)
    cosine = jnp.where(((n + 1) & 2) == 2, -cosine, cosine)
    return sine, cosine


def branch_newton(center, cond, susc):
    k = 2.0 * cond
    vf, af, vt, at = center
    for step in range(NEWTON):
        s, c = sin_cos(af - at)
        w0 = vf - vt * c
        w1 = vt * s
        if step > 0:
            r0, r1, r2, r3 = vf - center[0], af - center[1], vt - center[2], at - center[3]
            r3 = vt * r3
            w0 = w0 - r0 + r2 * c + r3 * s
            w1 = w1 - r1 * vf - r2 * s + r3 * c
        ss, cc, tt = s * s, c * c, vt * vt
        m00 = 1.0 + k * (1.0 + cc + tt * ss)
        m11 = 1.0 + k * (vf * vf + ss + tt * cc)
        m01 = k * (s * c * (tt - 1.0))
        scale = k / (m00 * m11 - m01 * m01)
        z0 = (m11 * w0 - m01 * w1) * scale
        z1 = (m00 * w1 - m01 * w0) * scale
        new = (
            center[0] - z0,
            center[1] - vf * z1,
            center[2] + (c * z0 - s * z1),
            center[3] + vt * (s * z0 + c * z1),
        )
        vf, af, vt, at = new
    s, c = sin_cos(af - at)
    product = vf * vt
    flow_from = cond * vf * vf - product * (cond * c + susc * s)
    flow_to = cond * vt * vt - product * (cond * c - susc * s)
    return (vf, af, vt, at), flow_from, flow_to


def line_kernel(second, count_ref, slot_ref, arrived_ref, dual_ref, *refs):
    if second:
        previous_hbm, *refs = refs
    param_ref, out_hbm, other_hbm, *refs = refs
    near_refs, term_refs = refs[:2], refs[2:4]
    out_ref, other_ref, out_sem, other_sem, *refs = refs[4:]
    if second:
        previous_ref, previous_sem = refs
    lines = dual_ref.shape[1]
    blocks = lines // BLOCK

    def pair_rows(pair):
        return pl.ds(pl.multiple_of(pair * 2 * BLOCK, 2 * BLOCK), 2 * BLOCK)

    def fetch(pair):
        rows = pair_rows(pair)
        return pltpu.make_async_copy(
            previous_hbm.at[:, rows], previous_ref.at[:, rows], previous_sem.at[pair]
        )

    def keep(pair):
        rows = pair_rows(pair)
        return pltpu.make_async_copy(
            other_ref.at[:, rows], other_hbm.at[:, rows], other_sem.at[pair]
        )

    def gather(block, near_ref):
        for end in range(2):
            for j in range(BLOCK):
                slot = slot_ref[end * lines + block * BLOCK + j]
                start = slot + (slot & -CAP)
                for c in range(2):
                    near_ref[2 * end + c, j : j + 1, :] = arrived_ref[pl.ds(start + c * CAP, 1), :]

    def scatter(block, term_ref):
        for end in range(2):
            for j in range(BLOCK):
                slot = slot_ref[end * lines + block * BLOCK + j]
                start = slot + 2 * (slot & -CAP)
                for c in range(3):
                    out_ref[pl.ds(start + c * CAP, 1), :] = term_ref[3 * end + c, j : j + 1, :]

    def solve(block, near_ref, term_ref):
        base = pl.multiple_of(block * BLOCK, BLOCK)
        rows = pl.ds(base, BLOCK)
        near = [near_ref[i] for i in range(4)]
        dual = [dual_ref[i, rows, :] for i in range(4)]
        line_id = lax.broadcasted_iota(jnp.int32, (BLOCK, LANES), 0) + base
        live = line_id < count_ref[0]
        if second:
            dual = [
                jnp.where(live, dual[i] + previous_ref[i, rows, :] - near[i], dual[i])
                for i in range(4)
            ]
            for i in range(4):
                other_ref[i, rows, :] = dual[i]
        center = [near[i] - dual[i] for i in range(4)]
        param = param_ref[rows, :]
        cond = jnp.broadcast_to(param[:, 0:1], (BLOCK, LANES))
        susc = jnp.broadcast_to(param[:, 1:2], (BLOCK, LANES))
        state, flow_from, flow_to = branch_newton(center, cond, susc)
        if not second:
            for i in range(4):
                other_ref[i, rows, :] = state[i]
        terms = [
            state[0] + dual[0], state[1] + dual[1], flow_from,
            state[2] + dual[2], state[3] + dual[3], flow_to,
        ]
        for i in range(6):
            term_ref[i] = jnp.where(live, terms[i], 0.0)

    def step(pair, carry):
        block = 2 * pair
        if second:
            fetch(pair).wait()
        scatter(lax.rem(block + blocks - 1, blocks), term_refs[1])
        gather(block + 1, near_refs[1])
        solve(block, near_refs[0], term_refs[0])
        gather(lax.rem(block + 2, blocks), near_refs[0])
        scatter(block, term_refs[0])
        solve(block + 1, near_refs[1], term_refs[1])
        keep(pair).start()
        return carry

    if second:
        for pair in range(blocks // 2):
            fetch(pair).start()
    out_ref[...] = jnp.zeros_like(out_ref)
    term_refs[1][...] = jnp.zeros_like(term_refs[1])
    gather(0, near_refs[0])
    lax.fori_loop(0, blocks // 2, step, 0)
    scatter(blocks - 1, term_refs[1])
    piece = out_ref.shape[0] // PARTS
    rows = [pl.ds(i * piece, piece) for i in range(PARTS)]
    ship = copies_of([(out_ref.at[r], out_hbm.at[r]) for r in rows], out_sem)
    start_all(ship)
    for pair in range(blocks // 2):
        keep(pair).wait()
    wait_all(ship)


def column(param, index):
    return jnp.broadcast_to(param[:, index : index + 1], (param.shape[0], LANES))


def region_term(param, regional, buses_all):
    ids = lax.broadcasted_iota(jnp.int32, (param.shape[0], REGIONS), 1)
    member = ids == param[:, 6:7].astype(jnp.int32)
    total = picked(member.astype(BF16), regional, 3)
    return total * (REGION_GAIN * REGIONS / buses_all)


def bus_hits(row_ref, buses):
    slots = row_ref.shape[1]
    ids = lax.broadcasted_iota(jnp.int32, (buses, slots), 0) + 1
    return (ids == row_ref[...]).astype(BF16)


def slot_rows(recv_ref, c):
    return recv_ref[:, c * CAP : (c + 1) * CAP, :].reshape(recv_ref.shape[0] * CAP, LANES)


def volt_kernel(send, asked_ref, row_ref, recv_ref, volt_ref, param_ref, volt_hbm, *refs):
    if send:
        send_hbm, volt_out, rows_ref, volt_sem, sem = refs
    else:
        volt_out = volt_hbm
    hits = bus_hits(row_ref, volt_ref.shape[1])
    rows = jnp.concatenate([slot_rows(recv_ref, 0), slot_rows(recv_ref, 1)], axis=1)
    pair = picked(hits, rows, 2)
    ones = jnp.ones((hits.shape[1], LANES), BF16)
    degree = jnp.dot(hits, ones, preferred_element_type=F32)
    param = param_ref[...]
    weight = column(param, 0)
    inverse = 1.0 / (degree + weight)
    volt_out[0] = (pair[:, :LANES] + weight * column(param, 1)) * inverse
    volt_out[1] = (pair[:, LANES:] + weight * volt_ref[1]) * inverse
    if send:
        keep = pltpu.make_async_copy(volt_out, volt_hbm, volt_sem)
        keep.start()
        send_rows(asked_ref, volt_out, send_hbm, rows_ref, sem)
        keep.wait()


def dispatch_kernel(second, buses_all, scen_all, row_ref, recv_ref, param_ref, region_ref,
                    load_ref, price_ref, nadual_ref, *refs):
    if second:
        (disp1_ref, mism1_ref, regional_ref, totals_ref,
         disp_out, part_out, total_out, price_out) = refs
    else:
        disp_out, mism_out, part_out, total_out = refs
    buses = load_ref.shape[0]
    net = picked(bus_hits(row_ref, buses), slot_rows(recv_ref, 2), 2)
    param = param_ref[...]
    load, price, nadual = load_ref[...], price_ref[...], nadual_ref[...]
    if second:
        commit = jnp.transpose(totals_ref[...])[:, 0:1] / scen_all
        commit = jnp.broadcast_to(commit, (buses, LANES))
        nadual = nadual + disp1_ref[...] - commit
        price = price + mism1_ref[...] + region_term(param, regional_ref[...], buses_all)
    else:
        commit = column(param, 5)
    want = (load + net - price - column(param, 3) + (commit - nadual)) / (
        2.0 * column(param, 2) + 2.0
    )
    dispatch = jnp.clip(want, 0.0, column(param, 4))
    mismatch = dispatch - load - net
    disp_out[...] = dispatch
    if second:
        price_out[...] = price + mismatch
    else:
        mism_out[...] = mismatch
    region = lax.broadcasted_iota(jnp.int32, (REGIONS, buses), 0) == region_ref[...]
    part = picked(region.astype(BF16), mismatch, 3)
    for copy in range(part_out.shape[0] // REGIONS):
        part_out[copy * REGIONS : (copy + 1) * REGIONS, :] = part
    total = None
    ones = jnp.ones((total_out.shape[0], LANES), BF16)
    for piece in pieces(dispatch + nadual, 3):
        term = dot_lanes(ones, piece)
        total = term if total is None else total + term
    total_out[...] = total


def close_kernel(buses_all, param_ref, regional_ref, price_ref, out_ref):
    regional = regional_ref[0:REGIONS, :]
    for part in range(1, regional_ref.shape[0] // REGIONS):
        regional = regional + regional_ref[part * REGIONS : (part + 1) * REGIONS, :]
    out_ref[...] = price_ref[...] + region_term(param_ref[...], regional, buses_all)


def on_device(
    volt_init,
    line_dual,
    conductance,
    susceptance,
    endpoint_owner,
    endpoint_bus,
    line_count,
    bus_region,
    vm_set,
    stiffness,
    load,
    price_init,
    na_dual_init,
    commit_init,
    cost_quad,
    cost_lin,
    pmax,
):
    ngrid = lax.axis_size("grid")
    nscen = lax.axis_size("scen")
    lines = conductance.shape[0]
    ends = 2 * lines
    buses = vm_set.shape[0]
    scen = load.shape[1]
    buses_all = buses * ngrid
    shape = jax.ShapeDtypeStruct

    def exchange(x):
        return lax.all_to_all(x, "grid", split_axis=0, concat_axis=0, tiled=True)

    slot, request = pl.pallas_call(
        plan_kernel,
        out_shape=(shape((1, ends), jnp.int32), shape((ngrid, LANES), jnp.int32)),
        in_specs=[smem(), hbm(), hbm()],
        out_specs=(vmem(), vmem()),
        scratch_shapes=[VMEM((1, ends), jnp.int32)] * 2 + [pltpu.SemaphoreType.DMA((2,))],
        compiler_params=pltpu.CompilerParams(vmem_limit_bytes=GRANT),
        name="plan",
    )(line_count, in_hbm(endpoint_owner.reshape(1, ends)), in_hbm(endpoint_bus.reshape(1, ends)))
    slot = slot.reshape(ends)
    asked = exchange(request)
    asked_row = asked[:, :CAP].reshape(1, ngrid * CAP)

    line_param = jnp.stack([conductance, susceptance], axis=1)
    bus_param = jnp.stack(
        [stiffness, vm_set, cost_quad, cost_lin, pmax, commit_init, bus_region.astype(F32),
         jnp.zeros_like(pmax)],
        axis=1,
    )
    region_row = bus_region.reshape(1, buses)
    send_shape = (ngrid, 2 * CAP, LANES)
    send_hbm = pltpu.HBM(send_shape, F32)
    bus_shape = shape((buses, LANES), F32)

    sent = pl.pallas_call(
        first_send_kernel,
        out_shape=send_hbm,
        in_specs=[smem(), hbm()],
        out_specs=hbm(),
        scratch_shapes=[VMEM((2, buses, LANES), F32), VMEM(send_shape, F32),
                        pltpu.SemaphoreType.DMA((2,)), pltpu.SemaphoreType.DMA((ngrid // GROUP,))],
        compiler_params=pltpu.CompilerParams(vmem_limit_bytes=GRANT),
        name="first_send",
    )(asked, in_hbm(volt_init))

    def line_call(second, arrived, previous):
        outs = [pltpu.HBM((ngrid * 3 * CAP, LANES), F32), pltpu.HBM((4, lines, LANES), F32)]
        args = [line_count, slot, arrived.reshape(ngrid * 2 * CAP, LANES), line_dual]
        if second:
            args.append(in_hbm(previous))
        args.append(line_param)
        pair_sem = pltpu.SemaphoreType.DMA((lines // (2 * BLOCK),))
        held = VMEM((4, lines, LANES), F32)
        specs = [smem(), smem(), vmem(), vmem()] + [hbm()] * second + [vmem()]
        scratch = [VMEM((4, BLOCK, LANES), F32)] * 2 + [VMEM((6, BLOCK, LANES), F32)] * 2
        scratch += [VMEM(outs[0].shape, F32), held, pltpu.SemaphoreType.DMA((PARTS,)), pair_sem]
        scratch += [held, pair_sem] * second
        out, other = pl.pallas_call(
            functools.partial(line_kernel, second),
            out_shape=outs,
            in_specs=specs,
            out_specs=[hbm(), hbm()],
            scratch_shapes=scratch,
            compiler_params=pltpu.CompilerParams(vmem_limit_bytes=GRANT),
            name="lines2" if second else "lines1",
        )(*args)
        return out.reshape(ngrid, 3 * CAP, LANES), other

    def volt_call(send, received, volt):
        volt_shape = (2, buses, LANES)
        outs = [pltpu.HBM(volt_shape, F32), send_hbm] if send else [shape(volt_shape, F32)]
        return pl.pallas_call(
            functools.partial(volt_kernel, send),
            out_shape=outs,
            in_specs=[smem()] + [vmem()] * 4,
            out_specs=[hbm()] * 2 if send else [vmem()],
            scratch_shapes=[VMEM(outs[0].shape, F32), VMEM(send_shape, F32),
                            pltpu.SemaphoreType.DMA,
                            pltpu.SemaphoreType.DMA((ngrid // GROUP,))] if send else [],
            compiler_params=pltpu.CompilerParams(vmem_limit_bytes=GRANT),
            name="volt1" if send else "volt2",
        )(asked, asked_row, received, volt, bus_param)

    def dispatch_call(second, received, extra):
        outs = [bus_shape] if second else [bus_shape] * 2
        copies = NEAR if second else 1
        outs += [shape((copies * REGIONS, LANES), F32), shape((8, buses), F32)]
        if second:
            outs.append(bus_shape)
        args = [asked_row, received, bus_param, region_row, load, price_init, na_dual_init]
        args += list(extra)
        return pl.pallas_call(
            functools.partial(dispatch_kernel, second, buses_all, scen * nscen),
            out_shape=outs,
            in_specs=[vmem()] * len(args),
            out_specs=[vmem()] * len(outs),
            compiler_params=pltpu.CompilerParams(vmem_limit_bytes=GRANT),
            name="dispatch2" if second else "dispatch1",
        )(*args)

    def near_sum(x, axis, size, step, count):
        parts = [
            lax.ppermute(x, axis, [(i, i ^ (k * step)) for i in range(size)])
            for k in range(1, count)
        ]
        return sum(parts, x)

    def doubling_sum(x, axis, count, step=1):
        while step < count:
            x = near_sum(x, axis, count, step, 2)
            step *= 2
        return x

    out, state = line_call(False, exchange(sent), None)
    received = exchange(out)
    volt, sent = volt_call(True, received, volt_init)
    arrived = exchange(sent)
    disp1, mism1, part, total = dispatch_call(False, received, ())
    for step in range(1, NEAR):
        if step & (step - 1) == 0:
            part = near_sum(part, "grid", ngrid, step, 2)
    part = near_sum(part, "grid", ngrid, NEAR, NEAR)
    arrived, part = lax.optimization_barrier((arrived, part))
    totals = doubling_sum(total, "scen", nscen)
    regional = near_sum(part, "grid", ngrid, NEAR * NEAR, ngrid // (NEAR * NEAR))
    out, dual = line_call(True, arrived, state)
    received = exchange(out)
    dispatch, part, total, price = dispatch_call(True, received, (disp1, mism1, regional, totals))
    near = [[i * NEAR + j for j in range(NEAR)] for i in range(ngrid // NEAR)]
    far = [[i * NEAR + j for i in range(ngrid // NEAR)] for j in range(NEAR)]
    part = lax.all_to_all(part, "grid", 0, 0, axis_index_groups=near, tiled=True)
    total = near_sum(total, "scen", nscen, 1, 2)
    part, total = lax.optimization_barrier((part, total))
    part = jnp.sum(part.reshape(NEAR, REGIONS, LANES), axis=0)
    part = jnp.broadcast_to(part[None], (ngrid // NEAR, REGIONS, LANES))
    parts = lax.all_to_all(part, "grid", 0, 0, axis_index_groups=far, tiled=True)
    commit = doubling_sum(total, "scen", nscen, 2)[0] / (scen * nscen)
    (volt,) = volt_call(False, received, volt)
    price = pl.pallas_call(
        functools.partial(close_kernel, buses_all),
        out_shape=bus_shape,
        in_specs=[vmem()] * 3,
        out_specs=vmem(),
        compiler_params=pltpu.CompilerParams(vmem_limit_bytes=GRANT),
        name="close",
    )(bus_param, parts.reshape(ngrid // NEAR * REGIONS, LANES), price)
    return (volt, dual, dispatch, price, commit)


def solution(mesh):
    in_specs = (
        P(None, "grid", "scen"),
        P(None, "grid", "scen"),
        P("grid"),
        P("grid"),
        P("grid", None),
        P("grid"),
        P("grid"),
        P("grid"),
        P("grid"),
        P("grid"),
        P("grid", "scen"),
        P("grid", "scen"),
        P("grid", "scen"),
        P("grid"),
        P("grid"),
        P("grid"),
        P("grid"),
    )
    out_specs = (
        P(None, "grid", "scen"),
        P(None, "grid", "scen"),
        P("grid", "scen"),
        P("grid", "scen"),
        P("grid"),
    )
    return jax.shard_map(
        on_device, mesh=mesh, in_specs=in_specs, out_specs=out_specs, check_vma=False
    )
```

```python
import functools

import jax
import jax.numpy as jnp
from jax import lax
from jax.experimental import pallas as pl
from jax.experimental.pallas import tpu as pltpu
from jax.sharding import PartitionSpec as P

NEWTON = 3
REGIONS = 16
CAP = 16
LANES = 128
REGION_GAIN = 10.0
BLOCK = 16
GROUP = 4
PARTS = 4
NEAR = 4
GRANT = 16 * 2**20

F32 = jnp.float32
BF16 = jnp.bfloat16
SMEM = pltpu.SMEM
VMEM = pltpu.VMEM


def smem():
    return pl.BlockSpec(memory_space=SMEM)


def vmem():
    return pl.BlockSpec(memory_space=VMEM)


def anywhere():
    return pl.BlockSpec(memory_space=pl.ANY)


def hbm():
    return pl.BlockSpec(memory_space=pltpu.HBM)


def in_hbm(x):
    return pltpu.with_memory_space_constraint(x, pltpu.HBM)


def copies_of(pairs, sem):
    return [pltpu.make_async_copy(a, b, sem.at[i]) for i, (a, b) in enumerate(pairs)]


def start_all(copies):
    for copy in copies:
        copy.start()


def wait_all(copies):
    for copy in copies:
        copy.wait()


def pieces(x, count):
    parts = []
    for _ in range(count - 1):
        head = x.astype(BF16)
        parts.append(head)
        x = x - head.astype(F32)
    parts.append(x.astype(BF16))
    return parts


def picked(selector, x, count):
    total = None
    for part in pieces(x, count):
        term = jnp.dot(selector, part, preferred_element_type=F32)
        total = term if total is None else total + term
    return total


def dot_lanes(a, b):
    return lax.dot_general(a, b, (((1,), (1,)), ((), ())), preferred_element_type=F32)


def plan_kernel(count_ref, owner_hbm, bus_hbm, near_ref, term_ref, request_ref, owner_ref, bus_ref, sem):
    fetch = copies_of([(owner_hbm, owner_ref), (bus_hbm, bus_ref)], sem)
    start_all(fetch)
    wait_all(fetch)
    ends = owner_ref.shape[1]
    owners = request_ref.shape[0]
    owner = owner_ref[...]
    end_id = lax.broadcasted_iota(jnp.int32, (1, ends), 1)
    live = lax.rem(end_id, ends // 2) < count_ref[0]
    code = jnp.where(live, bus_ref[...] + 1, 0).astype(F32)
    hits = lax.broadcasted_iota(jnp.int32, (owners, ends), 0) == owner
    hits = hits.astype(F32)
    before = lax.broadcasted_iota(jnp.int32, (ends, ends), 0) < lax.broadcasted_iota(
        jnp.int32, (ends, ends), 1
    )
    earlier = jnp.dot(hits.astype(BF16), before.astype(BF16), preferred_element_type=F32)
    rank = jnp.sum(hits * earlier, axis=0, keepdims=True).astype(jnp.int32)
    near_ref[...] = owner * (2 * CAP) + rank
    term_ref[...] = owner * (3 * CAP) + rank
    ranks = lax.broadcasted_iota(jnp.int32, (LANES, ends), 0) == rank
    table = dot_lanes((hits * code).astype(BF16), ranks.astype(BF16))
    request_ref[...] = table.astype(jnp.int32)


def send_rows(asked_ref, volt_ref, out_hbm, row_ref, sem):
    buses = volt_ref.shape[1]
    groups = row_ref.shape[0] // GROUP

    def ship(group):
        part = pl.ds(group * GROUP, GROUP)
        return pltpu.make_async_copy(row_ref.at[part], out_hbm.at[part], sem.at[group])

    def step(group, carry):
        for i in range(GROUP):
            o = group * GROUP + i
            for r in range(CAP):
                bus = (asked_ref[o, r] - 1) & (buses - 1)
                for c in range(2):
                    row_ref[o, c * CAP + r : c * CAP + r + 1, :] = volt_ref[c, pl.ds(bus, 1), :]
        ship(group).start()
        return carry

    def done(group, carry):
        ship(group).wait()
        return carry

    lax.fori_loop(0, groups, step, 0)
    lax.fori_loop(0, groups, done, 0)


def first_send_kernel(asked_any, volt_hbm, out_hbm, asked_ref, volt_ref, row_ref, in_sem, sem):
    fetch = copies_of(
        [(asked_any, asked_ref)] + [(volt_hbm.at[c], volt_ref.at[c]) for c in range(2)], in_sem
    )
    start_all(fetch)
    wait_all(fetch)
    send_rows(asked_ref, volt_ref, out_hbm, row_ref, sem)


def sin_cos(x):
    turns = jnp.floor(x * 0.636619772367581343 + 0.5)
    r = x - turns * 1.5703125
    r = r - turns * 4.83751296997070312e-04
    r = r - turns * 7.54978995489188216e-08
    n = turns.astype(jnp.int32)
    z = r * r
    s = ((-1.9515295891e-4 * z + 8.3321608736e-3) * z - 1.6666654611e-1) * z * r + r
    c = ((2.443315711809948e-5 * z - 1.388731625493765e-3) * z + 4.166664568298827e-2) * z * z
    c = c - 0.5 * z + 1.0
    odd = (n & 1) == 1
    sine = jnp.where(odd, c, s)
    cosine = jnp.where(odd, s, c)
    sine = jnp.where((n & 2) == 2, -sine, sine)
    cosine = jnp.where(((n + 1) & 2) == 2, -cosine, cosine)
    return sine, cosine


def branch_newton(center, cond, susc):
    k = 2.0 * cond
    vf, af, vt, at = center
    for step in range(NEWTON):
        s, c = sin_cos(af - at)
        w0 = vf - vt * c
        w1 = vt * s
        if step > 0:
            r0, r1, r2, r3 = vf - center[0], af - center[1], vt - center[2], at - center[3]
            r3 = vt * r3
            w0 = w0 - r0 + r2 * c + r3 * s
            w1 = w1 - r1 * vf - r2 * s + r3 * c
        ss, cc, tt = s * s, c * c, vt * vt
        m00 = 1.0 + k * (1.0 + cc + tt * ss)
        m11 = 1.0 + k * (vf * vf + ss + tt * cc)
        m01 = k * (s * c * (tt - 1.0))
        scale = k / (m00 * m11 - m01 * m01)
        z0 = (m11 * w0 - m01 * w1) * scale
        z1 = (m00 * w1 - m01 * w0) * scale
        new = (
            center[0] - z0,
            center[1] - vf * z1,
            center[2] + (c * z0 - s * z1),
            center[3] + vt * (s * z0 + c * z1),
        )
        vf, af, vt, at = new
    s, c = sin_cos(af - at)
    product = vf * vt
    flow_from = cond * vf * vf - product * (cond * c + susc * s)
    flow_to = cond * vt * vt - product * (cond * c - susc * s)
    return (vf, af, vt, at), flow_from, flow_to


def line_kernel(second, count_ref, near_any, term_any, arrived_ref, dual_ref, *refs):
    if second:
        previous_hbm, *refs = refs
    param_ref, out_hbm, other_hbm, *refs = refs
    near_refs, term_refs = refs[:2], refs[2:4]
    out_ref, other_ref, near_start, term_start, out_sem, other_sem, start_sem, *refs = refs[4:]
    index = copies_of([(near_any, near_start), (term_any, term_start)], start_sem)
    start_all(index)
    if second:
        previous_ref, previous_sem = refs
    lines = dual_ref.shape[1]
    blocks = lines // BLOCK

    def pair_rows(pair):
        return pl.ds(pl.multiple_of(pair * 2 * BLOCK, 2 * BLOCK), 2 * BLOCK)

    def fetch(pair):
        rows = pair_rows(pair)
        return pltpu.make_async_copy(
            previous_hbm.at[:, rows], previous_ref.at[:, rows], previous_sem.at[pair]
        )

    def keep(pair):
        rows = pair_rows(pair)
        return pltpu.make_async_copy(
            other_ref.at[:, rows], other_hbm.at[:, rows], other_sem.at[pair]
        )

    def gather(block, near_ref):
        for end in range(2):
            for j in range(BLOCK):
                start = near_start[0, end * lines + block * BLOCK + j]
                for c in range(2):
                    near_ref[2 * end + c, j : j + 1, :] = arrived_ref[pl.ds(start + c * CAP, 1), :]

    def scatter(block, term_ref):
        for end in range(2):
            for j in range(BLOCK):
                start = term_start[0, end * lines + block * BLOCK + j]
                for c in range(3):
                    out_ref[pl.ds(start + c * CAP, 1), :] = term_ref[3 * end + c, j : j + 1, :]

    def solve(block, near_ref, term_ref):
        base = pl.multiple_of(block * BLOCK, BLOCK)
        rows = pl.ds(base, BLOCK)
        near = [near_ref[i] for i in range(4)]
        dual = [dual_ref[i, rows, :] for i in range(4)]
        line_id = lax.broadcasted_iota(jnp.int32, (BLOCK, LANES), 0) + base
        live = line_id < count_ref[0]
        if second:
            dual = [
                jnp.where(live, dual[i] + previous_ref[i, rows, :] - near[i], dual[i])
                for i in range(4)
            ]
            for i in range(4):
                other_ref[i, rows, :] = dual[i]
        center = [near[i] - dual[i] for i in range(4)]
        param = param_ref[rows, :]
        cond = jnp.broadcast_to(param[:, 0:1], (BLOCK, LANES))
        susc = jnp.broadcast_to(param[:, 1:2], (BLOCK, LANES))
        state, flow_from, flow_to = branch_newton(center, cond, susc)
        if not second:
            for i in range(4):
                other_ref[i, rows, :] = state[i]
        terms = [
            state[0] + dual[0], state[1] + dual[1], flow_from,
            state[2] + dual[2], state[3] + dual[3], flow_to,
        ]
        for i in range(6):
            term_ref[i] = jnp.where(live, terms[i], 0.0)

    def step(pair, carry):
        block = 2 * pair
        if second:
            fetch(pair).wait()
        scatter(lax.rem(block + blocks - 1, blocks), term_refs[1])
        gather(block + 1, near_refs[1])
        solve(block, near_refs[0], term_refs[0])
        gather(lax.rem(block + 2, blocks), near_refs[0])
        scatter(block, term_refs[0])
        solve(block + 1, near_refs[1], term_refs[1])
        keep(pair).start()
        return carry

    if second:
        for pair in range(blocks // 2):
            fetch(pair).start()
    out_ref[...] = jnp.zeros_like(out_ref)
    term_refs[1][...] = jnp.zeros_like(term_refs[1])
    wait_all(index)
    gather(0, near_refs[0])
    lax.fori_loop(0, blocks // 2, step, 0)
    scatter(blocks - 1, term_refs[1])
    piece = out_ref.shape[0] // PARTS
    rows = [pl.ds(i * piece, piece) for i in range(PARTS)]
    ship = copies_of([(out_ref.at[r], out_hbm.at[r]) for r in rows], out_sem)
    start_all(ship)
    for pair in range(blocks // 2):
        keep(pair).wait()
    wait_all(ship)


def column(param, index):
    return jnp.broadcast_to(param[:, index : index + 1], (param.shape[0], LANES))


def region_term(param, regional, buses_all):
    ids = lax.broadcasted_iota(jnp.int32, (param.shape[0], REGIONS), 1)
    member = ids == param[:, 6:7].astype(jnp.int32)
    total = picked(member.astype(BF16), regional, 3)
    return total * (REGION_GAIN * REGIONS / buses_all)


def bus_hits(row_ref, buses):
    slots = row_ref.shape[1]
    ids = lax.broadcasted_iota(jnp.int32, (buses, slots), 0) + 1
    return (ids == row_ref[...]).astype(BF16)


def slot_rows(recv_ref, c):
    return recv_ref[:, c * CAP : (c + 1) * CAP, :].reshape(recv_ref.shape[0] * CAP, LANES)


def volt_kernel(send, asked_any, row_ref, recv_ref, volt_ref, param_ref, volt_hbm, *refs):
    if send:
        send_hbm, asked_ref, volt_out, rows_ref, asked_sem, volt_sem, sem = refs
        index = pltpu.make_async_copy(asked_any, asked_ref, asked_sem)
        index.start()
    else:
        volt_out = volt_hbm
    hits = bus_hits(row_ref, volt_ref.shape[1])
    rows = jnp.concatenate([slot_rows(recv_ref, 0), slot_rows(recv_ref, 1)], axis=1)
    pair = picked(hits, rows, 2)
    ones = jnp.ones((hits.shape[1], LANES), BF16)
    degree = jnp.dot(hits, ones, preferred_element_type=F32)
    param = param_ref[...]
    weight = column(param, 0)
    inverse = 1.0 / (degree + weight)
    volt_out[0] = (pair[:, :LANES] + weight * column(param, 1)) * inverse
    volt_out[1] = (pair[:, LANES:] + weight * volt_ref[1]) * inverse
    if send:
        keep = pltpu.make_async_copy(volt_out, volt_hbm, volt_sem)
        keep.start()
        index.wait()
        send_rows(asked_ref, volt_out, send_hbm, rows_ref, sem)
        keep.wait()


def dispatch_kernel(second, buses_all, scen_all, row_ref, recv_ref, param_ref, region_ref,
                    load_ref, price_ref, nadual_ref, *refs):
    if second:
        (disp1_ref, mism1_ref, regional_ref, totals_ref,
         disp_out, part_out, total_out, price_out) = refs
    else:
        disp_out, mism_out, part_out, total_out = refs
    buses = load_ref.shape[0]
    net = picked(bus_hits(row_ref, buses), slot_rows(recv_ref, 2), 2)
    param = param_ref[...]
    load, price, nadual = load_ref[...], price_ref[...], nadual_ref[...]
    if second:
        commit = jnp.transpose(totals_ref[...])[:, 0:1] / scen_all
        commit = jnp.broadcast_to(commit, (buses, LANES))
        nadual = nadual + disp1_ref[...] - commit
        price = price + mism1_ref[...] + region_term(param, regional_ref[...], buses_all)
    else:
        commit = column(param, 5)
    want = (load + net - price - column(param, 3) + (commit - nadual)) / (
        2.0 * column(param, 2) + 2.0
    )
    dispatch = jnp.clip(want, 0.0, column(param, 4))
    mismatch = dispatch - load - net
    disp_out[...] = dispatch
    if second:
        price_out[...] = price + mismatch
    else:
        mism_out[...] = mismatch
    region = lax.broadcasted_iota(jnp.int32, (REGIONS, buses), 0) == region_ref[...]
    part = picked(region.astype(BF16), mismatch, 3)
    for copy in range(part_out.shape[0] // REGIONS):
        part_out[copy * REGIONS : (copy + 1) * REGIONS, :] = part
    total = None
    ones = jnp.ones((total_out.shape[0], LANES), BF16)
    for piece in pieces(dispatch + nadual, 3):
        term = dot_lanes(ones, piece)
        total = term if total is None else total + term
    total_out[...] = total


def close_kernel(buses_all, param_ref, regional_ref, price_ref, out_ref):
    regional = regional_ref[0:REGIONS, :]
    for part in range(1, regional_ref.shape[0] // REGIONS):
        regional = regional + regional_ref[part * REGIONS : (part + 1) * REGIONS, :]
    out_ref[...] = price_ref[...] + region_term(param_ref[...], regional, buses_all)


def on_device(
    volt_init,
    line_dual,
    conductance,
    susceptance,
    endpoint_owner,
    endpoint_bus,
    line_count,
    bus_region,
    vm_set,
    stiffness,
    load,
    price_init,
    na_dual_init,
    commit_init,
    cost_quad,
    cost_lin,
    pmax,
):
    ngrid = lax.axis_size("grid")
    nscen = lax.axis_size("scen")
    lines = conductance.shape[0]
    ends = 2 * lines
    buses = vm_set.shape[0]
    scen = load.shape[1]
    buses_all = buses * ngrid
    shape = jax.ShapeDtypeStruct

    def exchange(x):
        return lax.all_to_all(x, "grid", split_axis=0, concat_axis=0, tiled=True)

    *starts, request = pl.pallas_call(
        plan_kernel,
        out_shape=[shape((1, ends), jnp.int32)] * 2 + [shape((ngrid, LANES), jnp.int32)],
        in_specs=[smem(), hbm(), hbm()],
        out_specs=[vmem()] * 3,
        scratch_shapes=[VMEM((1, ends), jnp.int32)] * 2 + [pltpu.SemaphoreType.DMA((2,))],
        compiler_params=pltpu.CompilerParams(vmem_limit_bytes=GRANT),
        name="plan",
    )(line_count, in_hbm(endpoint_owner.reshape(1, ends)), in_hbm(endpoint_bus.reshape(1, ends)))
    asked = exchange(request)
    asked_row = asked[:, :CAP].reshape(1, ngrid * CAP)

    line_param = jnp.stack([conductance, susceptance], axis=1)
    bus_param = jnp.stack(
        [stiffness, vm_set, cost_quad, cost_lin, pmax, commit_init, bus_region.astype(F32),
         jnp.zeros_like(pmax)],
        axis=1,
    )
    region_row = bus_region.reshape(1, buses)
    send_shape = (ngrid, 2 * CAP, LANES)
    send_hbm = pltpu.HBM(send_shape, F32)
    bus_shape = shape((buses, LANES), F32)

    sent = pl.pallas_call(
        first_send_kernel,
        out_shape=send_hbm,
        in_specs=[anywhere(), hbm()],
        out_specs=hbm(),
        scratch_shapes=[SMEM(request.shape, jnp.int32), VMEM((2, buses, LANES), F32),
                        VMEM(send_shape, F32), pltpu.SemaphoreType.DMA((3,)),
                        pltpu.SemaphoreType.DMA((ngrid // GROUP,))],
        compiler_params=pltpu.CompilerParams(vmem_limit_bytes=GRANT),
        name="first_send",
    )(asked, in_hbm(volt_init))

    def line_call(second, arrived, previous):
        outs = [pltpu.HBM((ngrid * 3 * CAP, LANES), F32), pltpu.HBM((4, lines, LANES), F32)]
        args = [line_count, *starts, arrived.reshape(ngrid * 2 * CAP, LANES), line_dual]
        if second:
            args.append(in_hbm(previous))
        args.append(line_param)
        pair_sem = pltpu.SemaphoreType.DMA((lines // (2 * BLOCK),))
        held = VMEM((4, lines, LANES), F32)
        specs = [smem(), anywhere(), anywhere(), vmem(), vmem()] + [hbm()] * second + [vmem()]
        scratch = [VMEM((4, BLOCK, LANES), F32)] * 2 + [VMEM((6, BLOCK, LANES), F32)] * 2
        scratch += [VMEM((ngrid * 3 * CAP, LANES), F32), held]
        scratch += [SMEM((1, ends), jnp.int32)] * 2
        scratch += [pltpu.SemaphoreType.DMA((PARTS,)), pair_sem, pltpu.SemaphoreType.DMA((2,))]
        scratch += [held, pair_sem] * second
        out, other = pl.pallas_call(
            functools.partial(line_kernel, second),
            out_shape=outs,
            in_specs=specs,
            out_specs=[hbm(), hbm()],
            scratch_shapes=scratch,
            compiler_params=pltpu.CompilerParams(vmem_limit_bytes=GRANT),
            name="lines2" if second else "lines1",
        )(*args)
        return out.reshape(ngrid, 3 * CAP, LANES), other

    def volt_call(send, received, volt):
        volt_shape = (2, buses, LANES)
        outs = [pltpu.HBM(volt_shape, F32), send_hbm] if send else [shape(volt_shape, F32)]
        return pl.pallas_call(
            functools.partial(volt_kernel, send),
            out_shape=outs,
            in_specs=[anywhere()] + [vmem()] * 4,
            out_specs=[hbm()] * 2 if send else [vmem()],
            scratch_shapes=[SMEM(asked.shape, jnp.int32), VMEM(volt_shape, F32),
                            VMEM(send_shape, F32), pltpu.SemaphoreType.DMA,
                            pltpu.SemaphoreType.DMA,
                            pltpu.SemaphoreType.DMA((ngrid // GROUP,))] if send else [],
            compiler_params=pltpu.CompilerParams(vmem_limit_bytes=GRANT),
            name="volt1" if send else "volt2",
        )(asked, asked_row, received, volt, bus_param)

    def dispatch_call(second, received, extra):
        outs = [bus_shape] if second else [bus_shape] * 2
        copies = NEAR if second else 1
        outs += [shape((copies * REGIONS, LANES), F32), shape((8, buses), F32)]
        if second:
            outs.append(bus_shape)
        args = [asked_row, received, bus_param, region_row, load, price_init, na_dual_init]
        args += list(extra)
        return pl.pallas_call(
            functools.partial(dispatch_kernel, second, buses_all, scen * nscen),
            out_shape=outs,
            in_specs=[vmem()] * len(args),
            out_specs=[vmem()] * len(outs),
            compiler_params=pltpu.CompilerParams(vmem_limit_bytes=GRANT),
            name="dispatch2" if second else "dispatch1",
        )(*args)

    def near_sum(x, axis, size, step, count):
        parts = [
            lax.ppermute(x, axis, [(i, i ^ (k * step)) for i in range(size)])
            for k in range(1, count)
        ]
        return sum(parts, x)

    def doubling_sum(x, axis, count, step=1):
        while step < count:
            x = near_sum(x, axis, count, step, 2)
            step *= 2
        return x

    out, state = line_call(False, exchange(sent), None)
    received = exchange(out)
    volt, sent = volt_call(True, received, volt_init)
    arrived = exchange(sent)
    disp1, mism1, part, total = dispatch_call(False, received, ())
    for step in range(1, NEAR):
        if step & (step - 1) == 0:
            part = near_sum(part, "grid", ngrid, step, 2)
    part = near_sum(part, "grid", ngrid, NEAR, NEAR)
    arrived, part = lax.optimization_barrier((arrived, part))
    totals = doubling_sum(total, "scen", nscen)
    regional = near_sum(part, "grid", ngrid, NEAR * NEAR, ngrid // (NEAR * NEAR))
    out, dual = line_call(True, arrived, state)
    received = exchange(out)
    dispatch, part, total, price = dispatch_call(True, received, (disp1, mism1, regional, totals))
    near = [[i * NEAR + j for j in range(NEAR)] for i in range(ngrid // NEAR)]
    far = [[i * NEAR + j for i in range(ngrid // NEAR)] for j in range(NEAR)]
    part = lax.all_to_all(part, "grid", 0, 0, axis_index_groups=near, tiled=True)
    total = near_sum(total, "scen", nscen, 1, 2)
    part, total = lax.optimization_barrier((part, total))
    part = jnp.sum(part.reshape(NEAR, REGIONS, LANES), axis=0)
    part = jnp.broadcast_to(part[None], (ngrid // NEAR, REGIONS, LANES))
    parts = lax.all_to_all(part, "grid", 0, 0, axis_index_groups=far, tiled=True)
    commit = doubling_sum(total, "scen", nscen, 2)[0] / (scen * nscen)
    (volt,) = volt_call(False, received, volt)
    price = pl.pallas_call(
        functools.partial(close_kernel, buses_all),
        out_shape=bus_shape,
        in_specs=[vmem()] * 3,
        out_specs=vmem(),
        compiler_params=pltpu.CompilerParams(vmem_limit_bytes=GRANT),
        name="close",
    )(bus_param, parts.reshape(ngrid // NEAR * REGIONS, LANES), price)
    return (volt, dual, dispatch, price, commit)


def solution(mesh):
    in_specs = (
        P(None, "grid", "scen"),
        P(None, "grid", "scen"),
        P("grid"),
        P("grid"),
        P("grid", None),
        P("grid"),
        P("grid"),
        P("grid"),
        P("grid"),
        P("grid"),
        P("grid", "scen"),
        P("grid", "scen"),
        P("grid", "scen"),
        P("grid"),
        P("grid"),
        P("grid"),
        P("grid"),
    )
    out_specs = (
        P(None, "grid", "scen"),
        P(None, "grid", "scen"),
        P("grid", "scen"),
        P("grid", "scen"),
        P("grid"),
    )
    return jax.shard_map(
        on_device, mesh=mesh, in_specs=in_specs, out_specs=out_specs, check_vma=False
    )
```

```python
import functools

import jax
import jax.numpy as jnp
from jax import lax
from jax.experimental import pallas as pl
from jax.experimental.pallas import tpu as pltpu
from jax.sharding import PartitionSpec as P

NEWTON = 3
REGIONS = 16
CAP = 16
LANES = 128
REGION_GAIN = 10.0
BLOCK = 16
GROUP = 4
NEAR = 4
GRANT = 16 * 2**20

F32 = jnp.float32
BF16 = jnp.bfloat16
SMEM = pltpu.SMEM
VMEM = pltpu.VMEM


def smem():
    return pl.BlockSpec(memory_space=SMEM)


def vmem():
    return pl.BlockSpec(memory_space=VMEM)


def anywhere():
    return pl.BlockSpec(memory_space=pl.ANY)


def hbm():
    return pl.BlockSpec(memory_space=pltpu.HBM)


def in_hbm(x):
    return pltpu.with_memory_space_constraint(x, pltpu.HBM)


def copies_of(pairs, sem):
    return [pltpu.make_async_copy(a, b, sem.at[i]) for i, (a, b) in enumerate(pairs)]


def start_all(copies):
    for copy in copies:
        copy.start()


def wait_all(copies):
    for copy in copies:
        copy.wait()


def pieces(x, count):
    parts = []
    for _ in range(count - 1):
        head = x.astype(BF16)
        parts.append(head)
        x = x - head.astype(F32)
    parts.append(x.astype(BF16))
    return parts


def picked(selector, x, count):
    total = None
    for part in pieces(x, count):
        term = jnp.dot(selector, part, preferred_element_type=F32)
        total = term if total is None else total + term
    return total


def dot_lanes(a, b):
    return lax.dot_general(a, b, (((1,), (1,)), ((), ())), preferred_element_type=F32)


def plan_kernel(count_ref, owner_hbm, bus_hbm, pair_ref, slot_ref, request_ref, owner_ref, bus_ref, sem):
    fetch = copies_of([(owner_hbm, owner_ref), (bus_hbm, bus_ref)], sem)
    start_all(fetch)
    wait_all(fetch)
    ends = owner_ref.shape[1]
    owners = request_ref.shape[0]
    owner = owner_ref[...]
    end_id = lax.broadcasted_iota(jnp.int32, (1, ends), 1)
    live = lax.rem(end_id, ends // 2) < count_ref[0]
    code = jnp.where(live, bus_ref[...] + 1, 0).astype(F32)
    hits = lax.broadcasted_iota(jnp.int32, (owners, ends), 0) == owner
    hits = hits.astype(F32)
    before = lax.broadcasted_iota(jnp.int32, (ends, ends), 0) < lax.broadcasted_iota(
        jnp.int32, (ends, ends), 1
    )
    earlier = jnp.dot(hits.astype(BF16), before.astype(BF16), preferred_element_type=F32)
    rank = jnp.sum(hits * earlier, axis=0, keepdims=True).astype(jnp.int32)
    pair_ref[...] = owner * (2 * CAP) + rank
    slot_ref[...] = owner * CAP + rank
    ranks = lax.broadcasted_iota(jnp.int32, (LANES, ends), 0) == rank
    table = dot_lanes((hits * code).astype(BF16), ranks.astype(BF16))
    request_ref[...] = table.astype(jnp.int32)


def send_rows(asked_ref, volt_ref, out_hbm, row_ref, sem):
    buses = volt_ref.shape[1]
    groups = row_ref.shape[0] // GROUP

    def ship(group):
        part = pl.ds(group * GROUP, GROUP)
        return pltpu.make_async_copy(row_ref.at[part], out_hbm.at[part], sem.at[group])

    def step(group, carry):
        for i in range(GROUP):
            o = group * GROUP + i
            for r in range(CAP):
                bus = (asked_ref[o, r] - 1) & (buses - 1)
                for c in range(2):
                    row_ref[o, c * CAP + r : c * CAP + r + 1, :] = volt_ref[c, pl.ds(bus, 1), :]
        ship(group).start()
        return carry

    def done(group, carry):
        ship(group).wait()
        return carry

    lax.fori_loop(0, groups, step, 0)
    lax.fori_loop(0, groups, done, 0)


def first_send_kernel(asked_any, volt_hbm, out_hbm, asked_ref, volt_ref, row_ref, in_sem, sem):
    fetch = copies_of(
        [(asked_any, asked_ref)] + [(volt_hbm.at[c], volt_ref.at[c]) for c in range(2)], in_sem
    )
    start_all(fetch)
    wait_all(fetch)
    send_rows(asked_ref, volt_ref, out_hbm, row_ref, sem)


def sin_cos(x):
    turns = jnp.floor(x * 0.636619772367581343 + 0.5)
    r = x - turns * 1.5703125
    r = r - turns * 4.83751296997070312e-04
    r = r - turns * 7.54978995489188216e-08
    n = turns.astype(jnp.int32)
    z = r * r
    s = ((-1.9515295891e-4 * z + 8.3321608736e-3) * z - 1.6666654611e-1) * z * r + r
    c = ((2.443315711809948e-5 * z - 1.388731625493765e-3) * z + 4.166664568298827e-2) * z * z
    c = c - 0.5 * z + 1.0
    odd = (n & 1) == 1
    sine = jnp.where(odd, c, s)
    cosine = jnp.where(odd, s, c)
    sine = jnp.where((n & 2) == 2, -sine, sine)
    cosine = jnp.where(((n + 1) & 2) == 2, -cosine, cosine)
    return sine, cosine


def branch_newton(center, cond, susc):
    k = 2.0 * cond
    vf, af, vt, at = center
    for step in range(NEWTON):
        s, c = sin_cos(af - at)
        w0 = vf - vt * c
        w1 = vt * s
        if step > 0:
            r0, r1, r2, r3 = vf - center[0], af - center[1], vt - center[2], at - center[3]
            r3 = vt * r3
            w0 = w0 - r0 + r2 * c + r3 * s
            w1 = w1 - r1 * vf - r2 * s + r3 * c
        ss, cc, tt = s * s, c * c, vt * vt
        m00 = 1.0 + k * (1.0 + cc + tt * ss)
        m11 = 1.0 + k * (vf * vf + ss + tt * cc)
        m01 = k * (s * c * (tt - 1.0))
        scale = k / (m00 * m11 - m01 * m01)
        z0 = (m11 * w0 - m01 * w1) * scale
        z1 = (m00 * w1 - m01 * w0) * scale
        new = (
            center[0] - z0,
            center[1] - vf * z1,
            center[2] + (c * z0 - s * z1),
            center[3] + vt * (s * z0 + c * z1),
        )
        vf, af, vt, at = new
    s, c = sin_cos(af - at)
    product = vf * vt
    flow_from = cond * vf * vf - product * (cond * c + susc * s)
    flow_to = cond * vt * vt - product * (cond * c - susc * s)
    return (vf, af, vt, at), flow_from, flow_to


def line_kernel(second, count_ref, pair_any, slot_any, arrived_ref, dual_ref, *refs):
    if second:
        previous_hbm, *refs = refs
    count = 3 if second else 2
    param_ref, *refs = refs
    out_hbm, (other_hbm, *refs) = refs[:count], refs[count:]
    near_refs, term_refs, refs = refs[:2], refs[2:4], refs[4:]
    out_refs, (other_ref, pair_start, slot_start, *refs) = refs[:count], refs[count:]
    out_sem, other_sem, start_sem, *refs = refs
    index = copies_of([(pair_any, pair_start), (slot_any, slot_start)], start_sem)
    start_all(index)
    if second:
        previous_ref, previous_sem = refs
    lines = dual_ref.shape[1]
    blocks = lines // BLOCK

    def pair_rows(pair):
        return pl.ds(pl.multiple_of(pair * 2 * BLOCK, 2 * BLOCK), 2 * BLOCK)

    def fetch(pair):
        rows = pair_rows(pair)
        return pltpu.make_async_copy(
            previous_hbm.at[:, rows], previous_ref.at[:, rows], previous_sem.at[pair]
        )

    def keep(pair):
        rows = pair_rows(pair)
        return pltpu.make_async_copy(
            other_ref.at[:, rows], other_hbm.at[:, rows], other_sem.at[pair]
        )

    def gather(block, near_ref):
        for end in range(2):
            for j in range(BLOCK):
                start = pair_start[0, end * lines + block * BLOCK + j]
                for c in range(2):
                    near_ref[2 * end + c, j : j + 1, :] = arrived_ref[pl.ds(start + c * CAP, 1), :]

    def scatter(block, term_ref):
        for end in range(2):
            for j in range(BLOCK):
                slot = slot_start[0, end * lines + block * BLOCK + j]
                if second:
                    places = [(out_refs[c], slot) for c in range(3)]
                else:
                    pair = pair_start[0, end * lines + block * BLOCK + j]
                    places = [(out_refs[0], pair), (out_refs[0], pair + CAP), (out_refs[1], slot)]
                for c, (out_ref, row) in enumerate(places):
                    out_ref[pl.ds(row, 1), :] = term_ref[3 * end + c, j : j + 1, :]

    def solve(block, near_ref, term_ref):
        base = pl.multiple_of(block * BLOCK, BLOCK)
        rows = pl.ds(base, BLOCK)
        near = [near_ref[i] for i in range(4)]
        dual = [dual_ref[i, rows, :] for i in range(4)]
        line_id = lax.broadcasted_iota(jnp.int32, (BLOCK, LANES), 0) + base
        live = line_id < count_ref[0]
        if second:
            dual = [
                jnp.where(live, dual[i] + previous_ref[i, rows, :] - near[i], dual[i])
                for i in range(4)
            ]
            for i in range(4):
                other_ref[i, rows, :] = dual[i]
        center = [near[i] - dual[i] for i in range(4)]
        param = param_ref[rows, :]
        cond = jnp.broadcast_to(param[:, 0:1], (BLOCK, LANES))
        susc = jnp.broadcast_to(param[:, 1:2], (BLOCK, LANES))
        state, flow_from, flow_to = branch_newton(center, cond, susc)
        if not second:
            for i in range(4):
                other_ref[i, rows, :] = state[i]
        terms = [
            state[0] + dual[0], state[1] + dual[1], flow_from,
            state[2] + dual[2], state[3] + dual[3], flow_to,
        ]
        for i in range(6):
            term_ref[i] = jnp.where(live, terms[i], 0.0)

    def step(pair, carry):
        block = 2 * pair
        if second:
            fetch(pair).wait()
        scatter(lax.rem(block + blocks - 1, blocks), term_refs[1])
        gather(block + 1, near_refs[1])
        solve(block, near_refs[0], term_refs[0])
        gather(lax.rem(block + 2, blocks), near_refs[0])
        scatter(block, term_refs[0])
        solve(block + 1, near_refs[1], term_refs[1])
        keep(pair).start()
        return carry

    if second:
        for pair in range(blocks // 2):
            fetch(pair).start()
    for out_ref in out_refs:
        out_ref[...] = jnp.zeros_like(out_ref)
    term_refs[1][...] = jnp.zeros_like(term_refs[1])
    wait_all(index)
    gather(0, near_refs[0])
    lax.fori_loop(0, blocks // 2, step, 0)
    scatter(blocks - 1, term_refs[1])
    ship = copies_of(list(zip(out_refs, out_hbm)), out_sem)
    start_all(ship)
    for pair in range(blocks // 2):
        keep(pair).wait()
    wait_all(ship)


def column(param, index):
    return jnp.broadcast_to(param[:, index : index + 1], (param.shape[0], LANES))


def region_term(param, regional, buses_all):
    ids = lax.broadcasted_iota(jnp.int32, (param.shape[0], REGIONS), 1)
    member = ids == param[:, 6:7].astype(jnp.int32)
    total = picked(member.astype(BF16), regional, 3)
    return total * (REGION_GAIN * REGIONS / buses_all)


def bus_hits(row_ref, buses):
    slots = row_ref.shape[1]
    ids = lax.broadcasted_iota(jnp.int32, (buses, slots), 0) + 1
    return (ids == row_ref[...]).astype(BF16)


def slot_rows(recv_ref, c):
    return recv_ref[:, c * CAP : (c + 1) * CAP, :].reshape(recv_ref.shape[0] * CAP, LANES)


def volt_kernel(send, *refs):
    if send:
        asked_any, row_ref, recv_ref, volt_ref, param_ref, volt_hbm, *refs = refs
        terms = [slot_rows(recv_ref, c) for c in range(2)]
        send_hbm, asked_ref, volt_out, rows_ref, asked_sem, volt_sem, sem = refs
        index = pltpu.make_async_copy(asked_any, asked_ref, asked_sem)
        index.start()
    else:
        row_ref, mag_ref, ang_ref, volt_ref, param_ref, volt_out = refs
        terms = [slot_rows(mag_ref, 0), slot_rows(ang_ref, 0)]
    hits = bus_hits(row_ref, volt_ref.shape[1])
    pair = picked(hits, jnp.concatenate(terms, axis=1), 2)
    ones = jnp.ones((hits.shape[1], LANES), BF16)
    degree = jnp.dot(hits, ones, preferred_element_type=F32)
    param = param_ref[...]
    weight = column(param, 0)
    inverse = 1.0 / (degree + weight)
    volt_out[0] = (pair[:, :LANES] + weight * column(param, 1)) * inverse
    volt_out[1] = (pair[:, LANES:] + weight * volt_ref[1]) * inverse
    if send:
        keep = pltpu.make_async_copy(volt_out, volt_hbm, volt_sem)
        keep.start()
        index.wait()
        send_rows(asked_ref, volt_out, send_hbm, rows_ref, sem)
        keep.wait()


def dispatch_kernel(second, buses_all, scen_all, row_ref, recv_ref, param_ref, region_ref,
                    load_ref, price_ref, nadual_ref, *refs):
    if second:
        (disp1_ref, mism1_ref, regional_ref, totals_ref,
         disp_out, part_out, total_out, price_out) = refs
    else:
        disp_out, mism_out, part_out, total_out = refs
    buses = load_ref.shape[0]
    net = picked(bus_hits(row_ref, buses), slot_rows(recv_ref, 0), 2)
    param = param_ref[...]
    load, price, nadual = load_ref[...], price_ref[...], nadual_ref[...]
    if second:
        commit = jnp.transpose(totals_ref[...])[:, 0:1] / scen_all
        commit = jnp.broadcast_to(commit, (buses, LANES))
        nadual = nadual + disp1_ref[...] - commit
        price = price + mism1_ref[...] + region_term(param, regional_ref[...], buses_all)
    else:
        commit = column(param, 5)
    want = (load + net - price - column(param, 3) + (commit - nadual)) / (
        2.0 * column(param, 2) + 2.0
    )
    dispatch = jnp.clip(want, 0.0, column(param, 4))
    mismatch = dispatch - load - net
    disp_out[...] = dispatch
    if second:
        price_out[...] = price + mismatch
    else:
        mism_out[...] = mismatch
    region = lax.broadcasted_iota(jnp.int32, (REGIONS, buses), 0) == region_ref[...]
    part_out[...] = picked(region.astype(BF16), mismatch, 3)
    total = None
    ones = jnp.ones((total_out.shape[0], LANES), BF16)
    for piece in pieces(dispatch + nadual, 3):
        term = dot_lanes(ones, piece)
        total = term if total is None else total + term
    total_out[...] = total


def close_kernel(buses_all, param_ref, regional_ref, price_ref, out_ref):
    out_ref[...] = price_ref[...] + region_term(param_ref[...], regional_ref[...], buses_all)


def on_device(
    volt_init,
    line_dual,
    conductance,
    susceptance,
    endpoint_owner,
    endpoint_bus,
    line_count,
    bus_region,
    vm_set,
    stiffness,
    load,
    price_init,
    na_dual_init,
    commit_init,
    cost_quad,
    cost_lin,
    pmax,
):
    ngrid = lax.axis_size("grid")
    nscen = lax.axis_size("scen")
    lines = conductance.shape[0]
    ends = 2 * lines
    buses = vm_set.shape[0]
    scen = load.shape[1]
    buses_all = buses * ngrid
    shape = jax.ShapeDtypeStruct

    def exchange(x):
        return lax.all_to_all(x, "grid", split_axis=0, concat_axis=0, tiled=True)

    *starts, request = pl.pallas_call(
        plan_kernel,
        out_shape=[shape((1, ends), jnp.int32)] * 2 + [shape((ngrid, LANES), jnp.int32)],
        in_specs=[smem(), hbm(), hbm()],
        out_specs=[vmem()] * 3,
        scratch_shapes=[VMEM((1, ends), jnp.int32)] * 2 + [pltpu.SemaphoreType.DMA((2,))],
        compiler_params=pltpu.CompilerParams(vmem_limit_bytes=GRANT),
        name="plan",
    )(line_count, in_hbm(endpoint_owner.reshape(1, ends)), in_hbm(endpoint_bus.reshape(1, ends)))
    asked = exchange(request)
    asked_row = asked[:, :CAP].reshape(1, ngrid * CAP)

    line_param = jnp.stack([conductance, susceptance], axis=1)
    bus_param = jnp.stack(
        [stiffness, vm_set, cost_quad, cost_lin, pmax, commit_init, bus_region.astype(F32),
         jnp.zeros_like(pmax)],
        axis=1,
    )
    region_row = bus_region.reshape(1, buses)
    send_shape = (ngrid, 2 * CAP, LANES)
    send_hbm = pltpu.HBM(send_shape, F32)
    bus_shape = shape((buses, LANES), F32)

    sent = pl.pallas_call(
        first_send_kernel,
        out_shape=send_hbm,
        in_specs=[anywhere(), hbm()],
        out_specs=hbm(),
        scratch_shapes=[SMEM(request.shape, jnp.int32), VMEM((2, buses, LANES), F32),
                        VMEM(send_shape, F32), pltpu.SemaphoreType.DMA((3,)),
                        pltpu.SemaphoreType.DMA((ngrid // GROUP,))],
        compiler_params=pltpu.CompilerParams(vmem_limit_bytes=GRANT),
        name="first_send",
    )(asked, in_hbm(volt_init))

    def line_call(second, arrived, previous):
        widths = [1, 1, 1] if second else [2, 1]
        outs = [pltpu.HBM((ngrid * w * CAP, LANES), F32) for w in widths]
        args = [line_count, *starts, arrived.reshape(ngrid * 2 * CAP, LANES), line_dual]
        if second:
            args.append(in_hbm(previous))
        args.append(line_param)
        pair_sem = pltpu.SemaphoreType.DMA((lines // (2 * BLOCK),))
        held = VMEM((4, lines, LANES), F32)
        specs = [smem(), anywhere(), anywhere(), vmem(), vmem()] + [hbm()] * second + [vmem()]
        scratch = [VMEM((4, BLOCK, LANES), F32)] * 2 + [VMEM((6, BLOCK, LANES), F32)] * 2
        scratch += [VMEM((ngrid * w * CAP, LANES), F32) for w in widths] + [held]
        scratch += [SMEM((1, ends), jnp.int32)] * 2
        scratch += [pltpu.SemaphoreType.DMA((len(widths),)), pair_sem,
                    pltpu.SemaphoreType.DMA((2,))]
        scratch += [held, pair_sem] * second
        *terms, other = pl.pallas_call(
            functools.partial(line_kernel, second),
            out_shape=outs + [pltpu.HBM((4, lines, LANES), F32)],
            in_specs=specs,
            out_specs=[hbm()] * (len(outs) + 1),
            scratch_shapes=scratch,
            compiler_params=pltpu.CompilerParams(vmem_limit_bytes=GRANT),
            name="lines2" if second else "lines1",
        )(*args)
        return [t.reshape(ngrid, w * CAP, LANES) for t, w in zip(terms, widths)] + [other]

    def volt_call(send, received, volt):
        volt_shape = (2, buses, LANES)
        args = [asked] * send + [asked_row, *received, volt, bus_param]
        outs = [pltpu.HBM(volt_shape, F32), send_hbm] if send else [shape(volt_shape, F32)]
        return pl.pallas_call(
            functools.partial(volt_kernel, send),
            out_shape=outs,
            in_specs=[anywhere()] * send + [vmem()] * (len(args) - send),
            out_specs=[hbm()] * 2 if send else [vmem()],
            scratch_shapes=[SMEM(asked.shape, jnp.int32), VMEM(volt_shape, F32),
                            VMEM(send_shape, F32), pltpu.SemaphoreType.DMA,
                            pltpu.SemaphoreType.DMA,
                            pltpu.SemaphoreType.DMA((ngrid // GROUP,))] if send else [],
            compiler_params=pltpu.CompilerParams(vmem_limit_bytes=GRANT),
            name="volt1" if send else "volt2",
        )(*args)

    def dispatch_call(second, received, extra):
        outs = [bus_shape] if second else [bus_shape] * 2
        outs += [shape((REGIONS, LANES), F32), shape((8, buses), F32)]
        if second:
            outs.append(bus_shape)
        args = [asked_row, received, bus_param, region_row, load, price_init, na_dual_init]
        args += list(extra)
        return pl.pallas_call(
            functools.partial(dispatch_kernel, second, buses_all, scen * nscen),
            out_shape=outs,
            in_specs=[vmem()] * len(args),
            out_specs=[vmem()] * len(outs),
            compiler_params=pltpu.CompilerParams(vmem_limit_bytes=GRANT),
            name="dispatch2" if second else "dispatch1",
        )(*args)

    def near_sum(x, axis, size, step, count):
        parts = [
            lax.ppermute(x, axis, [(i, i ^ (k * step)) for i in range(size)])
            for k in range(1, count)
        ]
        return sum(parts, x)

    def doubling_sum(x, axis, count, step=1):
        while step < count:
            x = near_sum(x, axis, count, step, 2)
            step *= 2
        return x

    def coarse_sum(part):
        return near_sum(part, "grid", ngrid, NEAR * NEAR, ngrid // (NEAR * NEAR))

    def fine_sum(part):
        for step in range(1, NEAR):
            if step & (step - 1) == 0:
                part = near_sum(part, "grid", ngrid, step, 2)
        return near_sum(part, "grid", ngrid, NEAR, NEAR)

    pair, flow, state = line_call(False, exchange(sent), None)
    pair, flow = lax.optimization_barrier((exchange(pair), flow))
    volt, sent = volt_call(True, [pair], volt_init)
    sent, flow = lax.optimization_barrier((sent, exchange(flow)))
    arrived = exchange(sent)
    disp1, mism1, part, total = dispatch_call(False, flow, ())
    arrived, part, totals = lax.optimization_barrier(
        (arrived, fine_sum(part), doubling_sum(total, "scen", nscen))
    )
    mag, ang, flow, dual = line_call(True, arrived, state)
    flow, regional, mag = lax.optimization_barrier((exchange(flow), coarse_sum(part), mag))
    dispatch, part, total, price = dispatch_call(True, flow, (disp1, mism1, regional, totals))
    mag, part, ang = lax.optimization_barrier((exchange(mag), fine_sum(part), ang))
    ang = exchange(ang)
    commit = doubling_sum(total, "scen", nscen)[0] / (scen * nscen)
    regional = coarse_sum(part)
    (volt,) = volt_call(False, [mag, ang], volt)
    price = pl.pallas_call(
        functools.partial(close_kernel, buses_all),
        out_shape=bus_shape,
        in_specs=[vmem()] * 3,
        out_specs=vmem(),
        compiler_params=pltpu.CompilerParams(vmem_limit_bytes=GRANT),
        name="close",
    )(bus_param, regional, price)
    return (volt, dual, dispatch, price, commit)


def solution(mesh):
    in_specs = (
        P(None, "grid", "scen"),
        P(None, "grid", "scen"),
        P("grid"),
        P("grid"),
        P("grid", None),
        P("grid"),
        P("grid"),
        P("grid"),
        P("grid"),
        P("grid"),
        P("grid", "scen"),
        P("grid", "scen"),
        P("grid", "scen"),
        P("grid"),
        P("grid"),
        P("grid"),
        P("grid"),
    )
    out_specs = (
        P(None, "grid", "scen"),
        P(None, "grid", "scen"),
        P("grid", "scen"),
        P("grid", "scen"),
        P("grid"),
    )
    return jax.shard_map(
        on_device, mesh=mesh, in_specs=in_specs, out_specs=out_specs, check_vma=False
    )
```

```python
import functools

import jax
import jax.numpy as jnp
from jax import lax
from jax.experimental import pallas as pl
from jax.experimental.pallas import tpu as pltpu
from jax.sharding import PartitionSpec as P

NEWTON = 3
REGIONS = 16
CAP = 16
LANES = 128
REGION_GAIN = 10.0
BLOCK = 16
GROUP = 4
SPARE = 8
PARTS = 4
NEAR = 4
GRANT = 16 * 2**20

F32 = jnp.float32
BF16 = jnp.bfloat16
SMEM = pltpu.SMEM
VMEM = pltpu.VMEM


def smem():
    return pl.BlockSpec(memory_space=SMEM)


def vmem():
    return pl.BlockSpec(memory_space=VMEM)


def anywhere():
    return pl.BlockSpec(memory_space=pl.ANY)


def hbm():
    return pl.BlockSpec(memory_space=pltpu.HBM)


def in_hbm(x):
    return pltpu.with_memory_space_constraint(x, pltpu.HBM)


def copies_of(pairs, sem):
    return [pltpu.make_async_copy(a, b, sem.at[i]) for i, (a, b) in enumerate(pairs)]


def start_all(copies):
    for copy in copies:
        copy.start()


def wait_all(copies):
    for copy in copies:
        copy.wait()


def pieces(x, count):
    parts = []
    for _ in range(count - 1):
        head = x.astype(BF16)
        parts.append(head)
        x = x - head.astype(F32)
    parts.append(x.astype(BF16))
    return parts


def picked(selector, x, count):
    total = None
    for part in pieces(x, count):
        term = jnp.dot(selector, part, preferred_element_type=F32)
        total = term if total is None else total + term
    return total


def dot_lanes(a, b):
    return lax.dot_general(a, b, (((1,), (1,)), ((), ())), preferred_element_type=F32)


def plan_kernel(buses, count_ref, owner_hbm, bus_hbm, near_ref, term_ref, request_ref, owner_ref, bus_ref, sem):
    fetch = copies_of([(owner_hbm, owner_ref), (bus_hbm, bus_ref)], sem)
    start_all(fetch)
    wait_all(fetch)
    ends = owner_ref.shape[1]
    owners = request_ref.shape[0]
    owner = owner_ref[...]
    end_id = lax.broadcasted_iota(jnp.int32, (1, ends), 1)
    live = lax.rem(end_id, ends // 2) < count_ref[0]
    code = jnp.where(live, bus_ref[...] - buses, 0).astype(F32)
    hits = lax.broadcasted_iota(jnp.int32, (owners, ends), 0) == owner
    hits = hits.astype(F32)
    before = lax.broadcasted_iota(jnp.int32, (ends, ends), 0) < lax.broadcasted_iota(
        jnp.int32, (ends, ends), 1
    )
    earlier = jnp.dot(hits.astype(BF16), before.astype(BF16), preferred_element_type=F32)
    rank = jnp.sum(hits * earlier, axis=0, keepdims=True).astype(jnp.int32)
    near_ref[...] = owner * (2 * CAP) + rank
    term_ref[...] = owner * (3 * CAP) + rank
    ranks = lax.broadcasted_iota(jnp.int32, (LANES, ends), 0) == rank
    table = dot_lanes((hits * code).astype(BF16), ranks.astype(BF16))
    request_ref[...] = table.astype(jnp.int32) + buses


def send_rows(asked_ref, volt_ref, out_hbm, row_ref, sem):
    groups = row_ref.shape[0] // GROUP

    def ship(group):
        part = pl.ds(group * GROUP, GROUP)
        return pltpu.make_async_copy(row_ref.at[part], out_hbm.at[part], sem.at[group])

    def step(group, carry):
        for i in range(GROUP):
            o = group * GROUP + i
            for r in range(CAP):
                bus = asked_ref[o, r]
                for c in range(2):
                    row_ref[o, c * CAP + r : c * CAP + r + 1, :] = volt_ref[c, pl.ds(bus, 1), :]
        ship(group).start()
        return carry

    def done(group, carry):
        ship(group).wait()
        return carry

    lax.fori_loop(0, groups, step, 0)
    lax.fori_loop(0, groups, done, 0)


def clear_spare(volt_ref, buses):
    volt_ref[:, buses:, :] = jnp.zeros((2, SPARE, LANES), F32)


def first_send_kernel(asked_any, volt_hbm, out_hbm, asked_ref, volt_ref, row_ref, in_sem, sem):
    buses = volt_hbm.shape[1]
    fetch = copies_of(
        [(asked_any, asked_ref)] + [(volt_hbm.at[c], volt_ref.at[c, 0:buses]) for c in range(2)], in_sem
    )
    start_all(fetch)
    clear_spare(volt_ref, buses)
    wait_all(fetch)
    send_rows(asked_ref, volt_ref, out_hbm, row_ref, sem)


def sin_cos(x):
    turns = jnp.floor(x * 0.636619772367581343 + 0.5)
    r = x - turns * 1.5703125
    r = r - turns * 4.83751296997070312e-04
    r = r - turns * 7.54978995489188216e-08
    n = turns.astype(jnp.int32)
    z = r * r
    s = ((-1.9515295891e-4 * z + 8.3321608736e-3) * z - 1.6666654611e-1) * z * r + r
    c = ((2.443315711809948e-5 * z - 1.388731625493765e-3) * z + 4.166664568298827e-2) * z * z
    c = c - 0.5 * z + 1.0
    odd = (n & 1) == 1
    sine = jnp.where(odd, c, s)
    cosine = jnp.where(odd, s, c)
    sine = jnp.where((n & 2) == 2, -sine, sine)
    cosine = jnp.where(((n + 1) & 2) == 2, -cosine, cosine)
    return sine, cosine


def branch_newton(center, cond, susc):
    k = 2.0 * cond
    vf, af, vt, at = center
    for step in range(NEWTON):
        s, c = sin_cos(af - at)
        w0 = vf - vt * c
        w1 = vt * s
        if step > 0:
            r0, r1, r2, r3 = vf - center[0], af - center[1], vt - center[2], at - center[3]
            r3 = vt * r3
            w0 = w0 - r0 + r2 * c + r3 * s
            w1 = w1 - r1 * vf - r2 * s + r3 * c
        ss, cc, tt = s * s, c * c, vt * vt
        m00 = 1.0 + k * (1.0 + cc + tt * ss)
        m11 = 1.0 + k * (vf * vf + ss + tt * cc)
        m01 = k * (s * c * (tt - 1.0))
        scale = k / (m00 * m11 - m01 * m01)
        z0 = (m11 * w0 - m01 * w1) * scale
        z1 = (m00 * w1 - m01 * w0) * scale
        new = (
            center[0] - z0,
            center[1] - vf * z1,
            center[2] + (c * z0 - s * z1),
            center[3] + vt * (s * z0 + c * z1),
        )
        vf, af, vt, at = new
    s, c = sin_cos(af - at)
    product = vf * vt
    flow_from = cond * vf * vf - product * (cond * c + susc * s)
    flow_to = cond * vt * vt - product * (cond * c - susc * s)
    return (vf, af, vt, at), flow_from, flow_to


def line_kernel(second, count_ref, near_any, term_any, arrived_ref, dual_ref, *refs):
    if second:
        previous_hbm, *refs = refs
    param_ref, out_hbm, other_hbm, *refs = refs
    near_refs, term_refs = refs[:2], refs[2:4]
    out_ref, other_ref, near_start, term_start, out_sem, other_sem, start_sem, *refs = refs[4:]
    index = copies_of([(near_any, near_start), (term_any, term_start)], start_sem)
    start_all(index)
    if second:
        previous_ref, previous_sem = refs
    lines = dual_ref.shape[1]
    blocks = lines // BLOCK

    def pair_rows(pair):
        return pl.ds(pl.multiple_of(pair * 2 * BLOCK, 2 * BLOCK), 2 * BLOCK)

    def fetch(pair):
        rows = pair_rows(pair)
        return pltpu.make_async_copy(
            previous_hbm.at[:, rows], previous_ref.at[:, rows], previous_sem.at[pair]
        )

    def keep(pair):
        rows = pair_rows(pair)
        return pltpu.make_async_copy(
            other_ref.at[:, rows], other_hbm.at[:, rows], other_sem.at[pair]
        )

    def gather(block, near_ref):
        for end in range(2):
            for j in range(BLOCK):
                start = near_start[0, end * lines + block * BLOCK + j]
                for c in range(2):
                    near_ref[2 * end + c, j : j + 1, :] = arrived_ref[pl.ds(start + c * CAP, 1), :]

    def scatter(block, term_ref):
        for end in range(2):
            for j in range(BLOCK):
                start = term_start[0, end * lines + block * BLOCK + j]
                for c in range(3):
                    out_ref[pl.ds(start + c * CAP, 1), :] = term_ref[3 * end + c, j : j + 1, :]

    def solve(block, near_ref, term_ref):
        base = pl.multiple_of(block * BLOCK, BLOCK)
        rows = pl.ds(base, BLOCK)
        near = [near_ref[i] for i in range(4)]
        dual = [dual_ref[i, rows, :] for i in range(4)]
        line_id = lax.broadcasted_iota(jnp.int32, (BLOCK, LANES), 0) + base
        live = line_id < count_ref[0]
        if second:
            dual = [
                jnp.where(live, dual[i] + previous_ref[i, rows, :] - near[i], dual[i])
                for i in range(4)
            ]
            for i in range(4):
                other_ref[i, rows, :] = dual[i]
        center = [near[i] - dual[i] for i in range(4)]
        param = param_ref[rows, :]
        cond = jnp.broadcast_to(param[:, 0:1], (BLOCK, LANES))
        susc = jnp.broadcast_to(param[:, 1:2], (BLOCK, LANES))
        state, flow_from, flow_to = branch_newton(center, cond, susc)
        if not second:
            for i in range(4):
                other_ref[i, rows, :] = state[i]
        terms = [
            state[0] + dual[0], state[1] + dual[1], flow_from,
            state[2] + dual[2], state[3] + dual[3], flow_to,
        ]
        for i in range(6):
            term_ref[i] = jnp.where(live, terms[i], 0.0)

    def step(pair, carry):
        block = 2 * pair
        if second:
            fetch(pair).wait()
        scatter(lax.rem(block + blocks - 1, blocks), term_refs[1])
        gather(block + 1, near_refs[1])
        solve(block, near_refs[0], term_refs[0])
        gather(lax.rem(block + 2, blocks), near_refs[0])
        scatter(block, term_refs[0])
        solve(block + 1, near_refs[1], term_refs[1])
        keep(pair).start()
        return carry

    if second:
        for pair in range(blocks // 2):
            fetch(pair).start()
    out_ref[...] = jnp.zeros_like(out_ref)
    term_refs[1][...] = jnp.zeros_like(term_refs[1])
    wait_all(index)
    gather(0, near_refs[0])
    lax.fori_loop(0, blocks // 2, step, 0)
    scatter(blocks - 1, term_refs[1])
    piece = out_ref.shape[0] // PARTS
    rows = [pl.ds(i * piece, piece) for i in range(PARTS)]
    ship = copies_of([(out_ref.at[r], out_hbm.at[r]) for r in rows], out_sem)
    start_all(ship)
    for pair in range(blocks // 2):
        keep(pair).wait()
    wait_all(ship)


def column(param, index):
    return jnp.broadcast_to(param[:, index : index + 1], (param.shape[0], LANES))


def region_term(param, regional, buses_all):
    ids = lax.broadcasted_iota(jnp.int32, (param.shape[0], REGIONS), 1)
    member = ids == param[:, 6:7].astype(jnp.int32)
    total = picked(member.astype(BF16), regional, 3)
    return total * (REGION_GAIN * REGIONS / buses_all)


def bus_hits(row_ref, buses):
    slots = row_ref.shape[1]
    ids = lax.broadcasted_iota(jnp.int32, (buses, slots), 0)
    return (ids == row_ref[...]).astype(BF16)


def slot_rows(recv_ref, c):
    return recv_ref[:, c * CAP : (c + 1) * CAP, :].reshape(recv_ref.shape[0] * CAP, LANES)


def volt_kernel(send, asked_any, row_ref, recv_ref, volt_ref, param_ref, volt_hbm, *refs):
    if send:
        send_hbm, asked_ref, volt_out, rows_ref, asked_sem, volt_sem, sem = refs
        index = pltpu.make_async_copy(asked_any, asked_ref, asked_sem)
        index.start()
    else:
        volt_out = volt_hbm
    hits = bus_hits(row_ref, volt_ref.shape[1])
    rows = jnp.concatenate([slot_rows(recv_ref, 0), slot_rows(recv_ref, 1)], axis=1)
    pair = picked(hits, rows, 2)
    ones = jnp.ones((hits.shape[1], LANES), BF16)
    degree = jnp.dot(hits, ones, preferred_element_type=F32)
    param = param_ref[...]
    weight = column(param, 0)
    inverse = 1.0 / (degree + weight)
    buses = volt_ref.shape[1]
    volt_out[0, 0:buses, :] = (pair[:, :LANES] + weight * column(param, 1)) * inverse
    volt_out[1, 0:buses, :] = (pair[:, LANES:] + weight * volt_ref[1]) * inverse
    if send:
        keep = pltpu.make_async_copy(volt_out.at[:, 0:buses], volt_hbm, volt_sem)
        keep.start()
        clear_spare(volt_out, buses)
        index.wait()
        send_rows(asked_ref, volt_out, send_hbm, rows_ref, sem)
        keep.wait()


def dispatch_kernel(second, buses_all, scen_all, row_ref, recv_ref, param_ref, region_ref,
                    load_ref, price_ref, nadual_ref, *refs):
    if second:
        (disp1_ref, mism1_ref, regional_ref, totals_ref,
         disp_out, part_out, total_out, price_out) = refs
    else:
        disp_out, mism_out, part_out, total_out = refs
    buses = load_ref.shape[0]
    net = picked(bus_hits(row_ref, buses), slot_rows(recv_ref, 2), 2)
    param = param_ref[...]
    load, price, nadual = load_ref[...], price_ref[...], nadual_ref[...]
    if second:
        commit = jnp.transpose(totals_ref[...])[:, 0:1] / scen_all
        commit = jnp.broadcast_to(commit, (buses, LANES))
        nadual = nadual + disp1_ref[...] - commit
        price = price + mism1_ref[...] + region_term(param, regional_ref[...], buses_all)
    else:
        commit = column(param, 5)
    want = (load + net - price - column(param, 3) + (commit - nadual)) / (
        2.0 * column(param, 2) + 2.0
    )
    dispatch = jnp.clip(want, 0.0, column(param, 4))
    mismatch = dispatch - load - net
    disp_out[...] = dispatch
    if second:
        price_out[...] = price + mismatch
    else:
        mism_out[...] = mismatch
    region = lax.broadcasted_iota(jnp.int32, (REGIONS, buses), 0) == region_ref[...]
    part = picked(region.astype(BF16), mismatch, 3)
    for copy in range(part_out.shape[0] // REGIONS):
        part_out[copy * REGIONS : (copy + 1) * REGIONS, :] = part
    total = None
    ones = jnp.ones((total_out.shape[0], LANES), BF16)
    for piece in pieces(dispatch + nadual, 3):
        term = dot_lanes(ones, piece)
        total = term if total is None else total + term
    total_out[...] = total


def close_kernel(buses_all, param_ref, regional_ref, price_ref, out_ref):
    regional = regional_ref[0:REGIONS, :]
    for part in range(1, regional_ref.shape[0] // REGIONS):
        regional = regional + regional_ref[part * REGIONS : (part + 1) * REGIONS, :]
    out_ref[...] = price_ref[...] + region_term(param_ref[...], regional, buses_all)


def on_device(
    volt_init,
    line_dual,
    conductance,
    susceptance,
    endpoint_owner,
    endpoint_bus,
    line_count,
    bus_region,
    vm_set,
    stiffness,
    load,
    price_init,
    na_dual_init,
    commit_init,
    cost_quad,
    cost_lin,
    pmax,
):
    ngrid = lax.axis_size("grid")
    nscen = lax.axis_size("scen")
    lines = conductance.shape[0]
    ends = 2 * lines
    buses = vm_set.shape[0]
    scen = load.shape[1]
    buses_all = buses * ngrid
    shape = jax.ShapeDtypeStruct

    def exchange(x):
        return lax.all_to_all(x, "grid", split_axis=0, concat_axis=0, tiled=True)

    *starts, request = pl.pallas_call(
        functools.partial(plan_kernel, buses),
        out_shape=[shape((1, ends), jnp.int32)] * 2 + [shape((ngrid, LANES), jnp.int32)],
        in_specs=[smem(), hbm(), hbm()],
        out_specs=[vmem()] * 3,
        scratch_shapes=[VMEM((1, ends), jnp.int32)] * 2 + [pltpu.SemaphoreType.DMA((2,))],
        compiler_params=pltpu.CompilerParams(vmem_limit_bytes=GRANT),
        name="plan",
    )(line_count, in_hbm(endpoint_owner.reshape(1, ends)), in_hbm(endpoint_bus.reshape(1, ends)))
    asked = exchange(request)
    asked_row = asked[:, :CAP].reshape(1, ngrid * CAP)

    line_param = jnp.stack([conductance, susceptance], axis=1)
    bus_param = jnp.stack(
        [stiffness, vm_set, cost_quad, cost_lin, pmax, commit_init, bus_region.astype(F32),
         jnp.zeros_like(pmax)],
        axis=1,
    )
    region_row = bus_region.reshape(1, buses)
    send_shape = (ngrid, 2 * CAP, LANES)
    send_hbm = pltpu.HBM(send_shape, F32)
    bus_shape = shape((buses, LANES), F32)

    sent = pl.pallas_call(
        first_send_kernel,
        out_shape=send_hbm,
        in_specs=[anywhere(), hbm()],
        out_specs=hbm(),
        scratch_shapes=[SMEM(request.shape, jnp.int32), VMEM((2, buses + SPARE, LANES), F32),
                        VMEM(send_shape, F32), pltpu.SemaphoreType.DMA((3,)),
                        pltpu.SemaphoreType.DMA((ngrid // GROUP,))],
        compiler_params=pltpu.CompilerParams(vmem_limit_bytes=GRANT),
        name="first_send",
    )(asked, in_hbm(volt_init))

    def line_call(second, arrived, previous):
        outs = [pltpu.HBM((ngrid * 3 * CAP, LANES), F32), pltpu.HBM((4, lines, LANES), F32)]
        args = [line_count, *starts, arrived.reshape(ngrid * 2 * CAP, LANES), line_dual]
        if second:
            args.append(in_hbm(previous))
        args.append(line_param)
        pair_sem = pltpu.SemaphoreType.DMA((lines // (2 * BLOCK),))
        held = VMEM((4, lines, LANES), F32)
        specs = [smem(), anywhere(), anywhere(), vmem(), vmem()] + [hbm()] * second + [vmem()]
        scratch = [VMEM((4, BLOCK, LANES), F32)] * 2 + [VMEM((6, BLOCK, LANES), F32)] * 2
        scratch += [VMEM((ngrid * 3 * CAP, LANES), F32), held]
        scratch += [SMEM((1, ends), jnp.int32)] * 2
        scratch += [pltpu.SemaphoreType.DMA((PARTS,)), pair_sem, pltpu.SemaphoreType.DMA((2,))]
        scratch += [held, pair_sem] * second
        out, other = pl.pallas_call(
            functools.partial(line_kernel, second),
            out_shape=outs,
            in_specs=specs,
            out_specs=[hbm(), hbm()],
            scratch_shapes=scratch,
            compiler_params=pltpu.CompilerParams(vmem_limit_bytes=GRANT),
            name="lines2" if second else "lines1",
        )(*args)
        return out.reshape(ngrid, 3 * CAP, LANES), other

    def volt_call(send, received, volt):
        volt_shape = (2, buses, LANES)
        outs = [pltpu.HBM(volt_shape, F32), send_hbm] if send else [shape(volt_shape, F32)]
        return pl.pallas_call(
            functools.partial(volt_kernel, send),
            out_shape=outs,
            in_specs=[anywhere()] + [vmem()] * 4,
            out_specs=[hbm()] * 2 if send else [vmem()],
            scratch_shapes=[SMEM(asked.shape, jnp.int32),
                            VMEM((2, buses + SPARE, LANES), F32),
                            VMEM(send_shape, F32), pltpu.SemaphoreType.DMA,
                            pltpu.SemaphoreType.DMA,
                            pltpu.SemaphoreType.DMA((ngrid // GROUP,))] if send else [],
            compiler_params=pltpu.CompilerParams(vmem_limit_bytes=GRANT),
            name="volt1" if send else "volt2",
        )(asked, asked_row, received, volt, bus_param)

    def dispatch_call(second, received, extra):
        outs = [bus_shape] if second else [bus_shape] * 2
        copies = NEAR if second else 1
        outs += [shape((copies * REGIONS, LANES), F32), shape((8, buses), F32)]
        if second:
            outs.append(bus_shape)
        args = [asked_row, received, bus_param, region_row, load, price_init, na_dual_init]
        args += list(extra)
        return pl.pallas_call(
            functools.partial(dispatch_kernel, second, buses_all, scen * nscen),
            out_shape=outs,
            in_specs=[vmem()] * len(args),
            out_specs=[vmem()] * len(outs),
            compiler_params=pltpu.CompilerParams(vmem_limit_bytes=GRANT),
            name="dispatch2" if second else "dispatch1",
        )(*args)

    def near_sum(x, axis, size, step, count):
        parts = [
            lax.ppermute(x, axis, [(i, i ^ (k * step)) for i in range(size)])
            for k in range(1, count)
        ]
        return sum(parts, x)

    def doubling_sum(x, axis, count, step=1):
        while step < count:
            x = near_sum(x, axis, count, step, 2)
            step *= 2
        return x

    out, state = line_call(False, exchange(sent), None)
    received = exchange(out)
    volt, sent = volt_call(True, received, volt_init)
    arrived = exchange(sent)
    disp1, mism1, part, total = dispatch_call(False, received, ())
    for step in range(1, NEAR):
        if step & (step - 1) == 0:
            part = near_sum(part, "grid", ngrid, step, 2)
    part = near_sum(part, "grid", ngrid, NEAR, NEAR)
    arrived, part = lax.optimization_barrier((arrived, part))
    totals = doubling_sum(total, "scen", nscen)
    regional = near_sum(part, "grid", ngrid, NEAR * NEAR, ngrid // (NEAR * NEAR))
    out, dual = line_call(True, arrived, state)
    received = exchange(out)
    dispatch, part, total, price = dispatch_call(True, received, (disp1, mism1, regional, totals))
    near = [[i * NEAR + j for j in range(NEAR)] for i in range(ngrid // NEAR)]
    far = [[i * NEAR + j for i in range(ngrid // NEAR)] for j in range(NEAR)]
    part = lax.all_to_all(part, "grid", 0, 0, axis_index_groups=near, tiled=True)
    total = near_sum(total, "scen", nscen, 1, 2)
    part, total = lax.optimization_barrier((part, total))
    part = jnp.sum(part.reshape(NEAR, REGIONS, LANES), axis=0)
    part = jnp.broadcast_to(part[None], (ngrid // NEAR, REGIONS, LANES))
    parts = lax.all_to_all(part, "grid", 0, 0, axis_index_groups=far, tiled=True)
    commit = doubling_sum(total, "scen", nscen, 2)[0] / (scen * nscen)
    (volt,) = volt_call(False, received, volt)
    price = pl.pallas_call(
        functools.partial(close_kernel, buses_all),
        out_shape=bus_shape,
        in_specs=[vmem()] * 3,
        out_specs=vmem(),
        compiler_params=pltpu.CompilerParams(vmem_limit_bytes=GRANT),
        name="close",
    )(bus_param, parts.reshape(ngrid // NEAR * REGIONS, LANES), price)
    return (volt, dual, dispatch, price, commit)


def solution(mesh):
    in_specs = (
        P(None, "grid", "scen"),
        P(None, "grid", "scen"),
        P("grid"),
        P("grid"),
        P("grid", None),
        P("grid"),
        P("grid"),
        P("grid"),
        P("grid"),
        P("grid"),
        P("grid", "scen"),
        P("grid", "scen"),
        P("grid", "scen"),
        P("grid"),
        P("grid"),
        P("grid"),
        P("grid"),
    )
    out_specs = (
        P(None, "grid", "scen"),
        P(None, "grid", "scen"),
        P("grid", "scen"),
        P("grid", "scen"),
        P("grid"),
    )
    return jax.shard_map(
        on_device, mesh=mesh, in_specs=in_specs, out_specs=out_specs, check_vma=False
    )
```

```python
import functools

import jax
import jax.numpy as jnp
from jax import lax
from jax.experimental import pallas as pl
from jax.experimental.pallas import tpu as pltpu
from jax.sharding import PartitionSpec as P

NEWTON = 3
REGIONS = 16
CAP = 16
LANES = 128
REGION_GAIN = 10.0
BLOCK = 16
GROUP = 4
SPARE = 8
PARTS = 4
NEAR = 4
GRANT = 16 * 2**20

F32 = jnp.float32
BF16 = jnp.bfloat16
SMEM = pltpu.SMEM
VMEM = pltpu.VMEM


def smem():
    return pl.BlockSpec(memory_space=SMEM)


def vmem():
    return pl.BlockSpec(memory_space=VMEM)


def anywhere():
    return pl.BlockSpec(memory_space=pl.ANY)


def hbm():
    return pl.BlockSpec(memory_space=pltpu.HBM)


def in_hbm(x):
    return pltpu.with_memory_space_constraint(x, pltpu.HBM)


def copies_of(pairs, sem):
    return [pltpu.make_async_copy(a, b, sem.at[i]) for i, (a, b) in enumerate(pairs)]


def start_all(copies):
    for copy in copies:
        copy.start()


def wait_all(copies):
    for copy in copies:
        copy.wait()


def pieces(x, count):
    parts = []
    for _ in range(count - 1):
        head = x.astype(BF16)
        parts.append(head)
        x = x - head.astype(F32)
    parts.append(x.astype(BF16))
    return parts


def picked(selector, x, count):
    total = None
    for part in pieces(x, count):
        term = jnp.dot(selector, part, preferred_element_type=F32)
        total = term if total is None else total + term
    return total


def dot_lanes(a, b):
    return lax.dot_general(a, b, (((1,), (1,)), ((), ())), preferred_element_type=F32)


def plan_kernel(buses, count_ref, owner_hbm, bus_hbm, near_ref, term_ref, request_ref, owner_ref, bus_ref, sem):
    fetch = copies_of([(owner_hbm, owner_ref), (bus_hbm, bus_ref)], sem)
    start_all(fetch)
    wait_all(fetch)
    ends = owner_ref.shape[1]
    owners = request_ref.shape[0]
    owner = owner_ref[...]
    end_id = lax.broadcasted_iota(jnp.int32, (1, ends), 1)
    live = lax.rem(end_id, ends // 2) < count_ref[0]
    code = jnp.where(live, bus_ref[...] - buses, 0).astype(F32)
    hits = lax.broadcasted_iota(jnp.int32, (owners, ends), 0) == owner
    hits = hits.astype(F32)
    before = lax.broadcasted_iota(jnp.int32, (ends, ends), 0) < lax.broadcasted_iota(
        jnp.int32, (ends, ends), 1
    )
    earlier = jnp.dot(hits.astype(BF16), before.astype(BF16), preferred_element_type=F32)
    rank = jnp.sum(hits * earlier, axis=0, keepdims=True).astype(jnp.int32)
    near_ref[...] = owner * (2 * CAP) + rank
    term_ref[...] = owner * (3 * CAP) + rank
    ranks = lax.broadcasted_iota(jnp.int32, (LANES, ends), 0) == rank
    table = dot_lanes((hits * code).astype(BF16), ranks.astype(BF16))
    request_ref[...] = table.astype(jnp.int32) + buses


def send_rows(asked_ref, volt_ref, out_hbm, row_ref, sem):
    groups = row_ref.shape[0] // GROUP

    def ship(group):
        part = pl.ds(group * GROUP, GROUP)
        return pltpu.make_async_copy(row_ref.at[part], out_hbm.at[part], sem.at[group])

    def step(group, carry):
        for i in range(GROUP):
            o = group * GROUP + i
            for r in range(CAP):
                bus = asked_ref[o, r]
                for c in range(2):
                    row_ref[o, c * CAP + r : c * CAP + r + 1, :] = volt_ref[c, pl.ds(bus, 1), :]
        ship(group).start()
        return carry

    def done(group, carry):
        ship(group).wait()
        return carry

    lax.fori_loop(0, groups, step, 0)
    lax.fori_loop(0, groups, done, 0)


def clear_spare(volt_ref, buses):
    volt_ref[:, buses:, :] = jnp.zeros((2, SPARE, LANES), F32)


def first_send_kernel(asked_any, volt_hbm, out_hbm, asked_ref, volt_ref, row_ref, in_sem, sem):
    buses = volt_hbm.shape[1]
    fetch = copies_of(
        [(asked_any, asked_ref)] + [(volt_hbm.at[c], volt_ref.at[c, 0:buses]) for c in range(2)], in_sem
    )
    start_all(fetch)
    clear_spare(volt_ref, buses)
    wait_all(fetch)
    send_rows(asked_ref, volt_ref, out_hbm, row_ref, sem)


def sin_cos(x):
    turns = jnp.floor(x * 0.636619772367581343 + 0.5)
    r = x - turns * 1.5703125
    r = r - turns * 4.83751296997070312e-04
    r = r - turns * 7.54978995489188216e-08
    n = turns.astype(jnp.int32)
    z = r * r
    s = ((-1.9515295891e-4 * z + 8.3321608736e-3) * z - 1.6666654611e-1) * z * r + r
    c = ((2.443315711809948e-5 * z - 1.388731625493765e-3) * z + 4.166664568298827e-2) * z * z
    c = c - 0.5 * z + 1.0
    odd = (n & 1) == 1
    sine = jnp.where(odd, c, s)
    cosine = jnp.where(odd, s, c)
    sine = jnp.where((n & 2) == 2, -sine, sine)
    cosine = jnp.where(((n + 1) & 2) == 2, -cosine, cosine)
    return sine, cosine


def branch_newton(center, cond, susc):
    k = 2.0 * cond
    vf, af, vt, at = center
    for step in range(NEWTON):
        s, c = sin_cos(af - at)
        w0 = vf - vt * c
        w1 = vt * s
        if step > 0:
            r0, r1, r2, r3 = vf - center[0], af - center[1], vt - center[2], at - center[3]
            r3 = vt * r3
            w0 = w0 - r0 + r2 * c + r3 * s
            w1 = w1 - r1 * vf - r2 * s + r3 * c
        ss, cc, tt = s * s, c * c, vt * vt
        m00 = 1.0 + k * (1.0 + cc + tt * ss)
        m11 = 1.0 + k * (vf * vf + ss + tt * cc)
        m01 = k * (s * c * (tt - 1.0))
        scale = k / (m00 * m11 - m01 * m01)
        z0 = (m11 * w0 - m01 * w1) * scale
        z1 = (m00 * w1 - m01 * w0) * scale
        new = (
            center[0] - z0,
            center[1] - vf * z1,
            center[2] + (c * z0 - s * z1),
            center[3] + vt * (s * z0 + c * z1),
        )
        vf, af, vt, at = new
    s, c = sin_cos(af - at)
    product = vf * vt
    flow_from = cond * vf * vf - product * (cond * c + susc * s)
    flow_to = cond * vt * vt - product * (cond * c - susc * s)
    return (vf, af, vt, at), flow_from, flow_to


def line_kernel(second, count_ref, near_any, term_any, arrived_ref, dual_ref, *refs):
    if second:
        previous_hbm, *refs = refs
    param_ref, out_hbm, other_hbm, *refs = refs
    near_refs, term_refs = refs[:2], refs[2:4]
    out_ref, other_ref, near_start, term_start, out_sem, other_sem, start_sem, *refs = refs[4:]
    index = copies_of([(near_any, near_start), (term_any, term_start)], start_sem)
    start_all(index)
    if second:
        previous_ref, previous_sem = refs
    lines = dual_ref.shape[1]
    blocks = lines // BLOCK

    def pair_rows(pair):
        return pl.ds(pl.multiple_of(pair * 2 * BLOCK, 2 * BLOCK), 2 * BLOCK)

    def fetch(pair):
        rows = pair_rows(pair)
        return pltpu.make_async_copy(
            previous_hbm.at[:, rows], previous_ref.at[:, rows], previous_sem.at[pair]
        )

    def keep(pair):
        rows = pair_rows(pair)
        return pltpu.make_async_copy(
            other_ref.at[:, rows], other_hbm.at[:, rows], other_sem.at[pair]
        )

    def gather(block, near_ref):
        for end in range(2):
            for j in range(BLOCK):
                start = near_start[0, end * lines + block * BLOCK + j]
                for c in range(2):
                    near_ref[2 * end + c, j : j + 1, :] = arrived_ref[pl.ds(start + c * CAP, 1), :]

    def scatter(block, term_ref):
        for end in range(2):
            for j in range(BLOCK):
                start = term_start[0, end * lines + block * BLOCK + j]
                for c in range(3):
                    out_ref[pl.ds(start + c * CAP, 1), :] = term_ref[3 * end + c, j : j + 1, :]

    def solve(block, near_ref, term_ref):
        base = pl.multiple_of(block * BLOCK, BLOCK)
        rows = pl.ds(base, BLOCK)
        near = [near_ref[i] for i in range(4)]
        dual = [dual_ref[i, rows, :] for i in range(4)]
        line_id = lax.broadcasted_iota(jnp.int32, (BLOCK, LANES), 0) + base
        live = line_id < count_ref[0]
        if second:
            dual = [
                jnp.where(live, dual[i] + previous_ref[i, rows, :] - near[i], dual[i])
                for i in range(4)
            ]
            for i in range(4):
                other_ref[i, rows, :] = dual[i]
        center = [near[i] - dual[i] for i in range(4)]
        param = param_ref[rows, :]
        cond = jnp.broadcast_to(param[:, 0:1], (BLOCK, LANES))
        susc = jnp.broadcast_to(param[:, 1:2], (BLOCK, LANES))
        state, flow_from, flow_to = branch_newton(center, cond, susc)
        if not second:
            for i in range(4):
                other_ref[i, rows, :] = state[i]
        terms = [
            state[0] + dual[0], state[1] + dual[1], flow_from,
            state[2] + dual[2], state[3] + dual[3], flow_to,
        ]
        for i in range(6):
            term_ref[i] = jnp.where(live, terms[i], 0.0)

    def step(pair, carry):
        block = 2 * pair
        if second:
            fetch(pair).wait()
        scatter(lax.rem(block + blocks - 1, blocks), term_refs[1])
        gather(block + 1, near_refs[1])
        solve(block, near_refs[0], term_refs[0])
        gather(lax.rem(block + 2, blocks), near_refs[0])
        scatter(block, term_refs[0])
        solve(block + 1, near_refs[1], term_refs[1])
        keep(pair).start()
        return carry

    if second:
        for pair in range(blocks // 2):
            fetch(pair).start()
    out_ref[...] = jnp.zeros_like(out_ref)
    term_refs[1][...] = jnp.zeros_like(term_refs[1])
    wait_all(index)
    gather(0, near_refs[0])
    lax.fori_loop(0, blocks // 2, step, 0)
    scatter(blocks - 1, term_refs[1])
    piece = out_ref.shape[0] // PARTS
    rows = [pl.ds(i * piece, piece) for i in range(PARTS)]
    ship = copies_of([(out_ref.at[r], out_hbm.at[r]) for r in rows], out_sem)
    start_all(ship)
    for pair in range(blocks // 2):
        keep(pair).wait()
    wait_all(ship)


def column(param, index):
    return jnp.broadcast_to(param[:, index : index + 1], (param.shape[0], LANES))


def region_term(param, regional, buses_all):
    ids = lax.broadcasted_iota(jnp.int32, (param.shape[0], REGIONS), 1)
    member = ids == param[:, 6:7].astype(jnp.int32)
    total = picked(member.astype(BF16), regional, 3)
    return total * (REGION_GAIN * REGIONS / buses_all)


def bus_hits(row_ref, buses):
    slots = row_ref.shape[1]
    ids = lax.broadcasted_iota(jnp.int32, (buses, slots), 0)
    return (ids == row_ref[...]).astype(BF16)


def slot_rows(recv_ref, c):
    return recv_ref[:, c * CAP : (c + 1) * CAP, :].reshape(recv_ref.shape[0] * CAP, LANES)


def volt_kernel(send, asked_any, row_ref, recv_ref, volt_ref, param_ref, volt_hbm, *refs):
    if send:
        send_hbm, asked_ref, volt_out, rows_ref, asked_sem, volt_sem, sem = refs
        index = pltpu.make_async_copy(asked_any, asked_ref, asked_sem)
        index.start()
    else:
        volt_out = volt_hbm
    hits = bus_hits(row_ref, volt_ref.shape[1])
    rows = jnp.concatenate([slot_rows(recv_ref, 0), slot_rows(recv_ref, 1)], axis=1)
    pair = picked(hits, rows, 2)
    ones = jnp.ones((hits.shape[1], LANES), BF16)
    degree = jnp.dot(hits, ones, preferred_element_type=F32)
    param = param_ref[...]
    weight = column(param, 0)
    inverse = 1.0 / (degree + weight)
    buses = volt_ref.shape[1]
    volt_out[0, 0:buses, :] = (pair[:, :LANES] + weight * column(param, 1)) * inverse
    volt_out[1, 0:buses, :] = (pair[:, LANES:] + weight * volt_ref[1]) * inverse
    if send:
        keep = pltpu.make_async_copy(volt_out.at[:, 0:buses], volt_hbm, volt_sem)
        keep.start()
        clear_spare(volt_out, buses)
        index.wait()
        send_rows(asked_ref, volt_out, send_hbm, rows_ref, sem)
        keep.wait()


def dispatch_kernel(second, buses_all, scen_all, row_ref, recv_ref, param_ref, region_ref,
                    load_ref, price_ref, nadual_ref, *refs):
    if second:
        (disp1_ref, mism1_ref, regional_ref, totals_ref,
         disp_out, part_out, total_out, price_out) = refs
    else:
        disp_out, mism_out, part_out, total_out = refs
    buses = load_ref.shape[0]
    net = picked(bus_hits(row_ref, buses), slot_rows(recv_ref, 2), 2)
    param = param_ref[...]
    load, price, nadual = load_ref[...], price_ref[...], nadual_ref[...]
    if second:
        commit = jnp.transpose(totals_ref[...])[:, 0:1] / scen_all
        commit = jnp.broadcast_to(commit, (buses, LANES))
        nadual = nadual + disp1_ref[...] - commit
        price = price + mism1_ref[...] + region_term(param, regional_ref[...], buses_all)
    else:
        commit = column(param, 5)
    want = (load + net - price - column(param, 3) + (commit - nadual)) / (
        2.0 * column(param, 2) + 2.0
    )
    dispatch = jnp.clip(want, 0.0, column(param, 4))
    mismatch = dispatch - load - net
    disp_out[...] = dispatch
    if second:
        price_out[...] = price + mismatch
    else:
        mism_out[...] = mismatch
    region = lax.broadcasted_iota(jnp.int32, (REGIONS, buses), 0) == region_ref[...]
    part = picked(region.astype(BF16), mismatch, 3)
    for copy in range(part_out.shape[0] // REGIONS):
        part_out[copy * REGIONS : (copy + 1) * REGIONS, :] = part
    total = None
    ones = jnp.ones((total_out.shape[0], LANES), BF16)
    for piece in pieces(dispatch + nadual, 3):
        term = dot_lanes(ones, piece)
        total = term if total is None else total + term
    total_out[...] = total


def close_kernel(buses_all, param_ref, regional_ref, price_ref, out_ref):
    regional = regional_ref[0:REGIONS, :]
    for part in range(1, regional_ref.shape[0] // REGIONS):
        regional = regional + regional_ref[part * REGIONS : (part + 1) * REGIONS, :]
    out_ref[...] = price_ref[...] + region_term(param_ref[...], regional, buses_all)


def on_device(
    volt_init,
    line_dual,
    conductance,
    susceptance,
    endpoint_owner,
    endpoint_bus,
    line_count,
    bus_region,
    vm_set,
    stiffness,
    load,
    price_init,
    na_dual_init,
    commit_init,
    cost_quad,
    cost_lin,
    pmax,
):
    ngrid = lax.axis_size("grid")
    nscen = lax.axis_size("scen")
    lines = conductance.shape[0]
    ends = 2 * lines
    buses = vm_set.shape[0]
    scen = load.shape[1]
    buses_all = buses * ngrid
    shape = jax.ShapeDtypeStruct

    def exchange(x):
        return lax.all_to_all(x, "grid", split_axis=0, concat_axis=0, tiled=True)

    *starts, request = pl.pallas_call(
        functools.partial(plan_kernel, buses),
        out_shape=[shape((1, ends), jnp.int32)] * 2 + [shape((ngrid, LANES), jnp.int32)],
        in_specs=[smem(), hbm(), hbm()],
        out_specs=[vmem()] * 3,
        scratch_shapes=[VMEM((1, ends), jnp.int32)] * 2 + [pltpu.SemaphoreType.DMA((2,))],
        compiler_params=pltpu.CompilerParams(vmem_limit_bytes=GRANT),
        name="plan",
    )(line_count, in_hbm(endpoint_owner.reshape(1, ends)), in_hbm(endpoint_bus.reshape(1, ends)))
    asked = exchange(request)
    asked_row = asked[:, :CAP].reshape(1, ngrid * CAP)

    line_param = jnp.stack([conductance, susceptance], axis=1)
    bus_param = jnp.stack(
        [stiffness, vm_set, cost_quad, cost_lin, pmax, commit_init, bus_region.astype(F32),
         jnp.zeros_like(pmax)],
        axis=1,
    )
    region_row = bus_region.reshape(1, buses)
    send_shape = (ngrid, 2 * CAP, LANES)
    send_hbm = pltpu.HBM(send_shape, F32)
    bus_shape = shape((buses, LANES), F32)

    sent = pl.pallas_call(
        first_send_kernel,
        out_shape=send_hbm,
        in_specs=[anywhere(), hbm()],
        out_specs=hbm(),
        scratch_shapes=[SMEM(request.shape, jnp.int32), VMEM((2, buses + SPARE, LANES), F32),
                        VMEM(send_shape, F32), pltpu.SemaphoreType.DMA((3,)),
                        pltpu.SemaphoreType.DMA((ngrid // GROUP,))],
        compiler_params=pltpu.CompilerParams(vmem_limit_bytes=GRANT),
        name="first_send",
    )(asked, in_hbm(volt_init))

    def line_call(second, arrived, previous):
        outs = [pltpu.HBM((ngrid * 3 * CAP, LANES), F32), pltpu.HBM((4, lines, LANES), F32)]
        args = [line_count, *starts, arrived.reshape(ngrid * 2 * CAP, LANES), line_dual]
        if second:
            args.append(in_hbm(previous))
        args.append(line_param)
        pair_sem = pltpu.SemaphoreType.DMA((lines // (2 * BLOCK),))
        held = VMEM((4, lines, LANES), F32)
        specs = [smem(), anywhere(), anywhere(), vmem(), vmem()] + [hbm()] * second + [vmem()]
        scratch = [VMEM((4, BLOCK, LANES), F32)] * 2 + [VMEM((6, BLOCK, LANES), F32)] * 2
        scratch += [VMEM((ngrid * 3 * CAP, LANES), F32), held]
        scratch += [SMEM((1, ends), jnp.int32)] * 2
        scratch += [pltpu.SemaphoreType.DMA((PARTS,)), pair_sem, pltpu.SemaphoreType.DMA((2,))]
        scratch += [held, pair_sem] * second
        out, other = pl.pallas_call(
            functools.partial(line_kernel, second),
            out_shape=outs,
            in_specs=specs,
            out_specs=[hbm(), hbm()],
            scratch_shapes=scratch,
            compiler_params=pltpu.CompilerParams(vmem_limit_bytes=GRANT),
            name="lines2" if second else "lines1",
        )(*args)
        return out.reshape(ngrid, 3 * CAP, LANES), other

    def volt_call(send, received, volt):
        volt_shape = (2, buses, LANES)
        outs = [pltpu.HBM(volt_shape, F32), send_hbm] if send else [shape(volt_shape, F32)]
        return pl.pallas_call(
            functools.partial(volt_kernel, send),
            out_shape=outs,
            in_specs=[anywhere()] + [vmem()] * 4,
            out_specs=[hbm()] * 2 if send else [vmem()],
            scratch_shapes=[SMEM(asked.shape, jnp.int32),
                            VMEM((2, buses + SPARE, LANES), F32),
                            VMEM(send_shape, F32), pltpu.SemaphoreType.DMA,
                            pltpu.SemaphoreType.DMA,
                            pltpu.SemaphoreType.DMA((ngrid // GROUP,))] if send else [],
            compiler_params=pltpu.CompilerParams(vmem_limit_bytes=GRANT),
            name="volt1" if send else "volt2",
        )(asked, asked_row, received, volt, bus_param)

    def dispatch_call(second, received, extra):
        outs = [bus_shape] if second else [bus_shape] * 2
        copies = NEAR if second else 1
        outs += [shape((copies * REGIONS, LANES), F32), shape((8, buses), F32)]
        if second:
            outs.append(bus_shape)
        args = [asked_row, received, bus_param, region_row, load, price_init, na_dual_init]
        args += list(extra)
        return pl.pallas_call(
            functools.partial(dispatch_kernel, second, buses_all, scen * nscen),
            out_shape=outs,
            in_specs=[vmem()] * len(args),
            out_specs=[vmem()] * len(outs),
            compiler_params=pltpu.CompilerParams(vmem_limit_bytes=GRANT),
            name="dispatch2" if second else "dispatch1",
        )(*args)

    def near_sum(x, axis, size, step, count):
        parts = [
            lax.ppermute(x, axis, [(i, i ^ (k * step)) for i in range(size)])
            for k in range(1, count)
        ]
        return sum(parts, x)

    def doubling_sum(x, axis, count, step=1):
        while step < count:
            x = near_sum(x, axis, count, step, 2)
            step *= 2
        return x

    out, state = line_call(False, exchange(sent), None)
    received = exchange(out)
    volt, sent = volt_call(True, received, volt_init)
    arrived = exchange(sent)
    disp1, mism1, part, total = dispatch_call(False, received, ())
    for step in range(1, NEAR):
        if step & (step - 1) == 0:
            part = near_sum(part, "grid", ngrid, step, 2)
    part = near_sum(part, "grid", ngrid, NEAR, NEAR)
    totals = doubling_sum(total, "scen", nscen)
    arrived, part, totals = lax.optimization_barrier((arrived, part, totals))
    regional = near_sum(part, "grid", ngrid, NEAR * NEAR, ngrid // (NEAR * NEAR))
    out, dual = line_call(True, arrived, state)
    received = exchange(out)
    dispatch, part, total, price = dispatch_call(True, received, (disp1, mism1, regional, totals))
    near = [[i * NEAR + j for j in range(NEAR)] for i in range(ngrid // NEAR)]
    far = [[i * NEAR + j for i in range(ngrid // NEAR)] for j in range(NEAR)]
    part = lax.all_to_all(part, "grid", 0, 0, axis_index_groups=near, tiled=True)
    total = near_sum(total, "scen", nscen, 1, 2)
    part, total = lax.optimization_barrier((part, total))
    part = jnp.sum(part.reshape(NEAR, REGIONS, LANES), axis=0)
    part = jnp.broadcast_to(part[None], (ngrid // NEAR, REGIONS, LANES))
    parts = lax.all_to_all(part, "grid", 0, 0, axis_index_groups=far, tiled=True)
    commit = doubling_sum(total, "scen", nscen, 2)[0] / (scen * nscen)
    (volt,) = volt_call(False, received, volt)
    price = pl.pallas_call(
        functools.partial(close_kernel, buses_all),
        out_shape=bus_shape,
        in_specs=[vmem()] * 3,
        out_specs=vmem(),
        compiler_params=pltpu.CompilerParams(vmem_limit_bytes=GRANT),
        name="close",
    )(bus_param, parts.reshape(ngrid // NEAR * REGIONS, LANES), price)
    return (volt, dual, dispatch, price, commit)


def solution(mesh):
    in_specs = (
        P(None, "grid", "scen"),
        P(None, "grid", "scen"),
        P("grid"),
        P("grid"),
        P("grid", None),
        P("grid"),
        P("grid"),
        P("grid"),
        P("grid"),
        P("grid"),
        P("grid", "scen"),
        P("grid", "scen"),
        P("grid", "scen"),
        P("grid"),
        P("grid"),
        P("grid"),
        P("grid"),
    )
    out_specs = (
        P(None, "grid", "scen"),
        P(None, "grid", "scen"),
        P("grid", "scen"),
        P("grid", "scen"),
        P("grid"),
    )
    return jax.shard_map(
        on_device, mesh=mesh, in_specs=in_specs, out_specs=out_specs, check_vma=False
    )
```

```python
import functools

import jax
import jax.numpy as jnp
from jax import lax
from jax.experimental import pallas as pl
from jax.experimental.pallas import tpu as pltpu
from jax.sharding import PartitionSpec as P

NEWTON = 3
REGIONS = 16
CAP = 16
LANES = 128
REGION_GAIN = 10.0
BLOCK = 16
GROUP = 4
SPARE = 8
PARTS = 4
NEAR = 4
GRANT = 16 * 2**20

F32 = jnp.float32
BF16 = jnp.bfloat16
SMEM = pltpu.SMEM
VMEM = pltpu.VMEM


def smem():
    return pl.BlockSpec(memory_space=SMEM)


def vmem():
    return pl.BlockSpec(memory_space=VMEM)


def anywhere():
    return pl.BlockSpec(memory_space=pl.ANY)


def hbm():
    return pl.BlockSpec(memory_space=pltpu.HBM)


def in_hbm(x):
    return pltpu.with_memory_space_constraint(x, pltpu.HBM)


def copies_of(pairs, sem):
    return [pltpu.make_async_copy(a, b, sem.at[i]) for i, (a, b) in enumerate(pairs)]


def start_all(copies):
    for copy in copies:
        copy.start()


def wait_all(copies):
    for copy in copies:
        copy.wait()


def pieces(x, count):
    parts = []
    for _ in range(count - 1):
        head = x.astype(BF16)
        parts.append(head)
        x = x - head.astype(F32)
    parts.append(x.astype(BF16))
    return parts


def picked(selector, x, count):
    total = None
    for part in pieces(x, count):
        term = jnp.dot(selector, part, preferred_element_type=F32)
        total = term if total is None else total + term
    return total


def dot_lanes(a, b):
    return lax.dot_general(a, b, (((1,), (1,)), ((), ())), preferred_element_type=F32)


def plan_kernel(buses, count_ref, owner_hbm, bus_hbm, near_ref, term_ref, request_ref, owner_ref, bus_ref, sem):
    fetch = copies_of([(owner_hbm, owner_ref), (bus_hbm, bus_ref)], sem)
    start_all(fetch)
    wait_all(fetch)
    ends = owner_ref.shape[1]
    owners = request_ref.shape[0]
    owner = owner_ref[...]
    end_id = lax.broadcasted_iota(jnp.int32, (1, ends), 1)
    live = lax.rem(end_id, ends // 2) < count_ref[0]
    code = jnp.where(live, bus_ref[...] - buses, 0).astype(F32)
    hits = lax.broadcasted_iota(jnp.int32, (owners, ends), 0) == owner
    hits = hits.astype(F32)
    before = lax.broadcasted_iota(jnp.int32, (ends, ends), 0) < lax.broadcasted_iota(
        jnp.int32, (ends, ends), 1
    )
    earlier = jnp.dot(hits.astype(BF16), before.astype(BF16), preferred_element_type=F32)
    rank = jnp.sum(hits * earlier, axis=0, keepdims=True).astype(jnp.int32)
    near_ref[...] = owner * (2 * CAP) + rank
    term_ref[...] = owner * (3 * CAP) + rank
    ranks = lax.broadcasted_iota(jnp.int32, (LANES, ends), 0) == rank
    table = dot_lanes((hits * code).astype(BF16), ranks.astype(BF16))
    request_ref[...] = table.astype(jnp.int32) + buses


def send_rows(asked_ref, volt_ref, out_hbm, row_ref, sem):
    groups = row_ref.shape[0] // GROUP

    def ship(group):
        part = pl.ds(group * GROUP, GROUP)
        return pltpu.make_async_copy(row_ref.at[part], out_hbm.at[part], sem.at[group])

    def step(group, carry):
        for i in range(GROUP):
            o = group * GROUP + i
            for r in range(CAP):
                bus = asked_ref[o, r]
                for c in range(2):
                    row_ref[o, c * CAP + r : c * CAP + r + 1, :] = volt_ref[c, pl.ds(bus, 1), :]
        ship(group).start()
        return carry

    def done(group, carry):
        ship(group).wait()
        return carry

    lax.fori_loop(0, groups, step, 0)
    lax.fori_loop(0, groups, done, 0)


def clear_spare(volt_ref, buses):
    volt_ref[:, buses:, :] = jnp.zeros((2, SPARE, LANES), F32)


def first_send_kernel(asked_any, volt_hbm, out_hbm, asked_ref, volt_ref, row_ref, in_sem, sem):
    buses = volt_hbm.shape[1]
    fetch = copies_of(
        [(asked_any, asked_ref)] + [(volt_hbm.at[c], volt_ref.at[c, 0:buses]) for c in range(2)], in_sem
    )
    start_all(fetch)
    clear_spare(volt_ref, buses)
    wait_all(fetch)
    send_rows(asked_ref, volt_ref, out_hbm, row_ref, sem)


def sin_cos(x):
    turns = jnp.floor(x * 0.636619772367581343 + 0.5)
    r = x - turns * 1.5703125
    r = r - turns * 4.83751296997070312e-04
    r = r - turns * 7.54978995489188216e-08
    n = turns.astype(jnp.int32)
    z = r * r
    s = ((-1.9515295891e-4 * z + 8.3321608736e-3) * z - 1.6666654611e-1) * z * r + r
    c = ((2.443315711809948e-5 * z - 1.388731625493765e-3) * z + 4.166664568298827e-2) * z * z
    c = c - 0.5 * z + 1.0
    odd = (n & 1) == 1
    sine = jnp.where(odd, c, s)
    cosine = jnp.where(odd, s, c)
    sine = jnp.where((n & 2) == 2, -sine, sine)
    cosine = jnp.where(((n + 1) & 2) == 2, -cosine, cosine)
    return sine, cosine


def branch_newton(center, cond, susc):
    k = 2.0 * cond
    vf, af, vt, at = center
    for step in range(NEWTON):
        s, c = sin_cos(af - at)
        w0 = vf - vt * c
        w1 = vt * s
        if step > 0:
            r0, r1, r2, r3 = vf - center[0], af - center[1], vt - center[2], at - center[3]
            r3 = vt * r3
            w0 = w0 - r0 + r2 * c + r3 * s
            w1 = w1 - r1 * vf - r2 * s + r3 * c
        ss, cc, tt = s * s, c * c, vt * vt
        m00 = 1.0 + k * (1.0 + cc + tt * ss)
        m11 = 1.0 + k * (vf * vf + ss + tt * cc)
        m01 = k * (s * c * (tt - 1.0))
        scale = k / (m00 * m11 - m01 * m01)
        z0 = (m11 * w0 - m01 * w1) * scale
        z1 = (m00 * w1 - m01 * w0) * scale
        new = (
            center[0] - z0,
            center[1] - vf * z1,
            center[2] + (c * z0 - s * z1),
            center[3] + vt * (s * z0 + c * z1),
        )
        vf, af, vt, at = new
    s, c = sin_cos(af - at)
    product = vf * vt
    flow_from = cond * vf * vf - product * (cond * c + susc * s)
    flow_to = cond * vt * vt - product * (cond * c - susc * s)
    return (vf, af, vt, at), flow_from, flow_to


def line_kernel(second, count_ref, near_any, term_any, arrived_ref, dual_ref, *refs):
    if second:
        previous_hbm, *refs = refs
    param_ref, out_hbm, other_hbm, *refs = refs
    near_refs, term_refs = refs[:2], refs[2:4]
    out_ref, other_ref, near_start, term_start, out_sem, other_sem, start_sem, *refs = refs[4:]
    index = copies_of([(near_any, near_start), (term_any, term_start)], start_sem)
    start_all(index)
    if second:
        previous_ref, previous_sem = refs
    lines = dual_ref.shape[1]
    blocks = lines // BLOCK

    def pair_rows(pair):
        return pl.ds(pl.multiple_of(pair * 2 * BLOCK, 2 * BLOCK), 2 * BLOCK)

    def fetch(pair):
        rows = pair_rows(pair)
        return pltpu.make_async_copy(
            previous_hbm.at[:, rows], previous_ref.at[:, rows], previous_sem.at[pair]
        )

    def keep(pair):
        rows = pair_rows(pair)
        return pltpu.make_async_copy(
            other_ref.at[:, rows], other_hbm.at[:, rows], other_sem.at[pair]
        )

    def gather(block, near_ref):
        for end in range(2):
            for j in range(BLOCK):
                start = near_start[0, end * lines + block * BLOCK + j]
                for c in range(2):
                    near_ref[2 * end + c, j : j + 1, :] = arrived_ref[pl.ds(start + c * CAP, 1), :]

    def scatter(block, term_ref):
        for end in range(2):
            for j in range(BLOCK):
                start = term_start[0, end * lines + block * BLOCK + j]
                for c in range(3):
                    out_ref[pl.ds(start + c * CAP, 1), :] = term_ref[3 * end + c, j : j + 1, :]

    def solve(block, near_ref, term_ref):
        base = pl.multiple_of(block * BLOCK, BLOCK)
        rows = pl.ds(base, BLOCK)
        near = [near_ref[i] for i in range(4)]
        dual = [dual_ref[i, rows, :] for i in range(4)]
        line_id = lax.broadcasted_iota(jnp.int32, (BLOCK, LANES), 0) + base
        live = line_id < count_ref[0]
        if second:
            dual = [
                jnp.where(live, dual[i] + previous_ref[i, rows, :] - near[i], dual[i])
                for i in range(4)
            ]
            for i in range(4):
                other_ref[i, rows, :] = dual[i]
        center = [near[i] - dual[i] for i in range(4)]
        param = param_ref[rows, :]
        cond = jnp.broadcast_to(param[:, 0:1], (BLOCK, LANES))
        susc = jnp.broadcast_to(param[:, 1:2], (BLOCK, LANES))
        state, flow_from, flow_to = branch_newton(center, cond, susc)
        if not second:
            for i in range(4):
                other_ref[i, rows, :] = state[i]
        terms = [
            state[0] + dual[0], state[1] + dual[1], flow_from,
            state[2] + dual[2], state[3] + dual[3], flow_to,
        ]
        for i in range(6):
            term_ref[i] = jnp.where(live, terms[i], 0.0)

    def step(pair, carry):
        block = 2 * pair
        if second:
            fetch(pair).wait()
        scatter(lax.rem(block + blocks - 1, blocks), term_refs[1])
        gather(block + 1, near_refs[1])
        solve(block, near_refs[0], term_refs[0])
        gather(lax.rem(block + 2, blocks), near_refs[0])
        scatter(block, term_refs[0])
        solve(block + 1, near_refs[1], term_refs[1])
        keep(pair).start()
        return carry

    if second:
        for pair in range(blocks // 2):
            fetch(pair).start()
    out_ref[...] = jnp.zeros_like(out_ref)
    term_refs[1][...] = jnp.zeros_like(term_refs[1])
    wait_all(index)
    gather(0, near_refs[0])
    lax.fori_loop(0, blocks // 2, step, 0)
    scatter(blocks - 1, term_refs[1])
    piece = out_ref.shape[0] // PARTS
    rows = [pl.ds(i * piece, piece) for i in range(PARTS)]
    ship = copies_of([(out_ref.at[r], out_hbm.at[r]) for r in rows], out_sem)
    start_all(ship)
    for pair in range(blocks // 2):
        keep(pair).wait()
    wait_all(ship)


def column(param, index):
    return jnp.broadcast_to(param[:, index : index + 1], (param.shape[0], LANES))


def region_term(param, regional, buses_all):
    ids = lax.broadcasted_iota(jnp.int32, (param.shape[0], REGIONS), 1)
    member = ids == param[:, 6:7].astype(jnp.int32)
    total = picked(member.astype(BF16), regional, 3)
    return total * (REGION_GAIN * REGIONS / buses_all)


def bus_hits(row_ref, buses):
    slots = row_ref.shape[1]
    ids = lax.broadcasted_iota(jnp.int32, (buses, slots), 0)
    return (ids == row_ref[...]).astype(BF16)


def slot_rows(recv_ref, c):
    return recv_ref[:, c * CAP : (c + 1) * CAP, :].reshape(recv_ref.shape[0] * CAP, LANES)


def volt_kernel(send, asked_any, row_ref, recv_ref, volt_ref, param_ref, volt_hbm, *refs):
    if send:
        send_hbm, asked_ref, volt_out, rows_ref, asked_sem, volt_sem, sem = refs
        index = pltpu.make_async_copy(asked_any, asked_ref, asked_sem)
        index.start()
    else:
        volt_out = volt_hbm
    hits = bus_hits(row_ref, volt_ref.shape[1])
    rows = jnp.concatenate([slot_rows(recv_ref, 0), slot_rows(recv_ref, 1)], axis=1)
    pair = picked(hits, rows, 2)
    ones = jnp.ones((hits.shape[1], LANES), BF16)
    degree = jnp.dot(hits, ones, preferred_element_type=F32)
    param = param_ref[...]
    weight = column(param, 0)
    inverse = 1.0 / (degree + weight)
    buses = volt_ref.shape[1]
    volt_out[0, 0:buses, :] = (pair[:, :LANES] + weight * column(param, 1)) * inverse
    volt_out[1, 0:buses, :] = (pair[:, LANES:] + weight * volt_ref[1]) * inverse
    if send:
        keep = pltpu.make_async_copy(volt_out.at[:, 0:buses], volt_hbm, volt_sem)
        keep.start()
        clear_spare(volt_out, buses)
        index.wait()
        send_rows(asked_ref, volt_out, send_hbm, rows_ref, sem)
        keep.wait()


def dispatch_kernel(second, buses_all, scen_all, row_ref, recv_ref, param_ref, region_ref,
                    load_ref, price_ref, nadual_ref, *refs):
    if second:
        (disp1_ref, mism1_ref, regional_ref, totals_ref,
         disp_out, part_out, total_out, price_out) = refs
    else:
        disp_out, mism_out, part_out, total_out = refs
    buses = load_ref.shape[0]
    net = picked(bus_hits(row_ref, buses), slot_rows(recv_ref, 2), 2)
    param = param_ref[...]
    load, price, nadual = load_ref[...], price_ref[...], nadual_ref[...]
    if second:
        commit = jnp.transpose(totals_ref[...])[:, 0:1] / scen_all
        commit = jnp.broadcast_to(commit, (buses, LANES))
        nadual = nadual + disp1_ref[...] - commit
        price = price + mism1_ref[...] + region_term(param, regional_ref[...], buses_all)
    else:
        commit = column(param, 5)
    want = (load + net - price - column(param, 3) + (commit - nadual)) / (
        2.0 * column(param, 2) + 2.0
    )
    dispatch = jnp.clip(want, 0.0, column(param, 4))
    mismatch = dispatch - load - net
    disp_out[...] = dispatch
    if second:
        price_out[...] = price + mismatch
    else:
        mism_out[...] = mismatch
    region = lax.broadcasted_iota(jnp.int32, (REGIONS, buses), 0) == region_ref[...]
    part = picked(region.astype(BF16), mismatch, 3)
    for copy in range(part_out.shape[0] // REGIONS):
        part_out[copy * REGIONS : (copy + 1) * REGIONS, :] = part
    total = None
    ones = jnp.ones((total_out.shape[0], LANES), BF16)
    for piece in pieces(dispatch + nadual, 3):
        term = dot_lanes(ones, piece)
        total = term if total is None else total + term
    total_out[...] = total


def close_kernel(buses_all, param_ref, regional_ref, price_ref, out_ref):
    regional = regional_ref[0:REGIONS, :]
    for part in range(1, regional_ref.shape[0] // REGIONS):
        regional = regional + regional_ref[part * REGIONS : (part + 1) * REGIONS, :]
    out_ref[...] = price_ref[...] + region_term(param_ref[...], regional, buses_all)


def on_device(
    volt_init,
    line_dual,
    conductance,
    susceptance,
    endpoint_owner,
    endpoint_bus,
    line_count,
    bus_region,
    vm_set,
    stiffness,
    load,
    price_init,
    na_dual_init,
    commit_init,
    cost_quad,
    cost_lin,
    pmax,
):
    ngrid = lax.axis_size("grid")
    nscen = lax.axis_size("scen")
    lines = conductance.shape[0]
    ends = 2 * lines
    buses = vm_set.shape[0]
    scen = load.shape[1]
    buses_all = buses * ngrid
    shape = jax.ShapeDtypeStruct

    def exchange(x):
        return lax.all_to_all(x, "grid", split_axis=0, concat_axis=0, tiled=True)

    *starts, request = pl.pallas_call(
        functools.partial(plan_kernel, buses),
        out_shape=[shape((1, ends), jnp.int32)] * 2 + [shape((ngrid, LANES), jnp.int32)],
        in_specs=[smem(), hbm(), hbm()],
        out_specs=[vmem()] * 3,
        scratch_shapes=[VMEM((1, ends), jnp.int32)] * 2 + [pltpu.SemaphoreType.DMA((2,))],
        compiler_params=pltpu.CompilerParams(vmem_limit_bytes=GRANT),
        name="plan",
    )(line_count, in_hbm(endpoint_owner.reshape(1, ends)), in_hbm(endpoint_bus.reshape(1, ends)))
    asked = exchange(request)
    asked_row = asked[:, :CAP].reshape(1, ngrid * CAP)

    line_param = jnp.stack([conductance, susceptance], axis=1)
    bus_param = jnp.stack(
        [stiffness, vm_set, cost_quad, cost_lin, pmax, commit_init, bus_region.astype(F32),
         jnp.zeros_like(pmax)],
        axis=1,
    )
    region_row = bus_region.reshape(1, buses)
    send_shape = (ngrid, 2 * CAP, LANES)
    send_hbm = pltpu.HBM(send_shape, F32)
    bus_shape = shape((buses, LANES), F32)

    sent = pl.pallas_call(
        first_send_kernel,
        out_shape=send_hbm,
        in_specs=[anywhere(), hbm()],
        out_specs=hbm(),
        scratch_shapes=[SMEM(request.shape, jnp.int32), VMEM((2, buses + SPARE, LANES), F32),
                        VMEM(send_shape, F32), pltpu.SemaphoreType.DMA((3,)),
                        pltpu.SemaphoreType.DMA((ngrid // GROUP,))],
        compiler_params=pltpu.CompilerParams(vmem_limit_bytes=GRANT),
        name="first_send",
    )(asked, in_hbm(volt_init))

    def line_call(second, arrived, previous):
        outs = [pltpu.HBM((ngrid * 3 * CAP, LANES), F32), pltpu.HBM((4, lines, LANES), F32)]
        args = [line_count, *starts, arrived.reshape(ngrid * 2 * CAP, LANES), line_dual]
        if second:
            args.append(in_hbm(previous))
        args.append(line_param)
        pair_sem = pltpu.SemaphoreType.DMA((lines // (2 * BLOCK),))
        held = VMEM((4, lines, LANES), F32)
        specs = [smem(), anywhere(), anywhere(), vmem(), vmem()] + [hbm()] * second + [vmem()]
        scratch = [VMEM((4, BLOCK, LANES), F32)] * 2 + [VMEM((6, BLOCK, LANES), F32)] * 2
        scratch += [VMEM((ngrid * 3 * CAP, LANES), F32), held]
        scratch += [SMEM((1, ends), jnp.int32)] * 2
        scratch += [pltpu.SemaphoreType.DMA((PARTS,)), pair_sem, pltpu.SemaphoreType.DMA((2,))]
        scratch += [held, pair_sem] * second
        out, other = pl.pallas_call(
            functools.partial(line_kernel, second),
            out_shape=outs,
            in_specs=specs,
            out_specs=[hbm(), hbm()],
            scratch_shapes=scratch,
            compiler_params=pltpu.CompilerParams(vmem_limit_bytes=GRANT),
            name="lines2" if second else "lines1",
        )(*args)
        return out.reshape(ngrid, 3 * CAP, LANES), other

    def volt_call(send, received, volt):
        volt_shape = (2, buses, LANES)
        outs = [pltpu.HBM(volt_shape, F32), send_hbm] if send else [shape(volt_shape, F32)]
        return pl.pallas_call(
            functools.partial(volt_kernel, send),
            out_shape=outs,
            in_specs=[anywhere()] + [vmem()] * 4,
            out_specs=[hbm()] * 2 if send else [vmem()],
            scratch_shapes=[SMEM(asked.shape, jnp.int32),
                            VMEM((2, buses + SPARE, LANES), F32),
                            VMEM(send_shape, F32), pltpu.SemaphoreType.DMA,
                            pltpu.SemaphoreType.DMA,
                            pltpu.SemaphoreType.DMA((ngrid // GROUP,))] if send else [],
            compiler_params=pltpu.CompilerParams(vmem_limit_bytes=GRANT),
            name="volt1" if send else "volt2",
        )(asked, asked_row, received, volt, bus_param)

    def dispatch_call(second, received, extra):
        outs = [bus_shape] if second else [bus_shape] * 2
        copies = NEAR if second else 1
        outs += [shape((copies * REGIONS, LANES), F32), shape((8, buses), F32)]
        if second:
            outs.append(bus_shape)
        args = [asked_row, received, bus_param, region_row, load, price_init, na_dual_init]
        args += list(extra)
        return pl.pallas_call(
            functools.partial(dispatch_kernel, second, buses_all, scen * nscen),
            out_shape=outs,
            in_specs=[vmem()] * len(args),
            out_specs=[vmem()] * len(outs),
            compiler_params=pltpu.CompilerParams(vmem_limit_bytes=GRANT),
            name="dispatch2" if second else "dispatch1",
        )(*args)

    def near_sum(x, axis, size, step, count):
        parts = [
            lax.ppermute(x, axis, [(i, i ^ (k * step)) for i in range(size)])
            for k in range(1, count)
        ]
        return sum(parts, x)

    def doubling_sum(x, axis, count, step=1):
        while step < count:
            x = near_sum(x, axis, count, step, 2)
            step *= 2
        return x

    out, state = line_call(False, exchange(sent), None)
    received = exchange(out)
    volt, sent = volt_call(True, received, volt_init)
    arrived = exchange(sent)
    disp1, mism1, part, total = dispatch_call(False, received, ())
    for step in range(1, NEAR):
        if step & (step - 1) == 0:
            part = near_sum(part, "grid", ngrid, step, 2)
    part = near_sum(part, "grid", ngrid, NEAR * NEAR, ngrid // (NEAR * NEAR))
    totals = doubling_sum(total, "scen", nscen)
    arrived, part, totals = lax.optimization_barrier((arrived, part, totals))
    regional = near_sum(part, "grid", ngrid, NEAR, NEAR)
    out, dual = line_call(True, arrived, state)
    received = exchange(out)
    dispatch, part, total, price = dispatch_call(True, received, (disp1, mism1, regional, totals))
    near = [[i * NEAR + j for j in range(NEAR)] for i in range(ngrid // NEAR)]
    far = [[i * NEAR + j for i in range(ngrid // NEAR)] for j in range(NEAR)]
    part = lax.all_to_all(part, "grid", 0, 0, axis_index_groups=near, tiled=True)
    total = near_sum(total, "scen", nscen, 1, 2)
    part, total = lax.optimization_barrier((part, total))
    part = jnp.sum(part.reshape(NEAR, REGIONS, LANES), axis=0)
    part = jnp.broadcast_to(part[None], (ngrid // NEAR, REGIONS, LANES))
    parts = lax.all_to_all(part, "grid", 0, 0, axis_index_groups=far, tiled=True)
    commit = doubling_sum(total, "scen", nscen, 2)[0] / (scen * nscen)
    (volt,) = volt_call(False, received, volt)
    price = pl.pallas_call(
        functools.partial(close_kernel, buses_all),
        out_shape=bus_shape,
        in_specs=[vmem()] * 3,
        out_specs=vmem(),
        compiler_params=pltpu.CompilerParams(vmem_limit_bytes=GRANT),
        name="close",
    )(bus_param, parts.reshape(ngrid // NEAR * REGIONS, LANES), price)
    return (volt, dual, dispatch, price, commit)


def solution(mesh):
    in_specs = (
        P(None, "grid", "scen"),
        P(None, "grid", "scen"),
        P("grid"),
        P("grid"),
        P("grid", None),
        P("grid"),
        P("grid"),
        P("grid"),
        P("grid"),
        P("grid"),
        P("grid", "scen"),
        P("grid", "scen"),
        P("grid", "scen"),
        P("grid"),
        P("grid"),
        P("grid"),
        P("grid"),
    )
    out_specs = (
        P(None, "grid", "scen"),
        P(None, "grid", "scen"),
        P("grid", "scen"),
        P("grid", "scen"),
        P("grid"),
    )
    return jax.shard_map(
        on_device, mesh=mesh, in_specs=in_specs, out_specs=out_specs, check_vma=False
    )
```
